32 devices in a mesh: groups: 2 (over y), seq: 8 (over z, x), chan: 2 (over core).
Axes of the slice: x: 2, y: 2, z: 4, core: 2. Of those that a mesh axis runs over, the one named last changes fastest.
Arguments:
- signal: bfloat16 [4096, 1024], P(('groups', 'seq'), 'chan'), parts along dimension 0, may hold values from -6 to 6
- tangent: bfloat16 [4096, 1024], P(('groups', 'seq'), 'chan'), parts along dimension 0, may hold values from -6 to 6
- gains: float32 [2, 1024], P(None, 'chan'), may hold values from 0.5 to 2
- convolution_kernel: bfloat16 [2, 3072, 2, 512], P(None, 'seq', None, 'chan'), may hold values from -0.109375 to 0.109375
- mixing_kernel: bfloat16 [2, 512, 1024], P(None, 'seq', 'chan'), may hold values from -0.25 to 0.25
Outputs:
- out_signal: bfloat16 [4096, 1024], P(('groups', 'seq'), 'chan'), parts along dimension 0
- out_tangent: bfloat16 [4096, 1024], P(('groups', 'seq'), 'chan'), parts along dimension 0
The draws below stay inside these ranges and needn't reach their ends.
There are 2 independent parts, one for each index of `groups`. The reference program is written for one: setup_inputs(seed, part) draws one part's arguments, and reference() takes and returns one part's arrays. A program takes and returns all parts, laid end to end along the dimension named above; an argument that names none is the same for every part. Nothing has to cross between parts.
All inputs are finite; a program needn't handle non-finite values.
Results may differ from the reference program's by a relative error of at most 0.0063.
Values may be sent and summed in bfloat16 or wider, within the bound.
No kernel may reach another device: no remote copies, remote signals or barrier semaphores. Data moves between devices by JAX's collectives and lax.ppermute only.
A program may use at most 64 MiB of HBM per device.

```python
import math
import jax
import jax.numpy as jnp
from jax import lax

C = 1024
E = 512
LAYERS = 2
SEQ = 2048
FIRST_DILATION = 128


def block_levels(own_key, extent, cuts, low, top_value):
    def one(position, shards_of):
        steps = jax.random.uniform(jax.random.fold_in(jax.random.fold_in(own_key, 6), position), (shards_of,), jnp.float32, low / len(cuts), top_value / len(cuts))
        return jnp.repeat(jnp.exp(steps), extent[position] // shards_of).reshape((-1,) + (1,) * (len(extent) - position - 1))

    level = one(*cuts[0])
    for cut in cuts[1:]:
        level = level * one(*cut)
    return level


def gaussian(key, extent, width, reach, split=(), held_as=jnp.bfloat16):
    factor_of = block_levels(key, extent, split, -0.22, 0.18) if split else 1.0
    values = jax.random.normal(key, extent, jnp.float32) * width * factor_of
    return jnp.minimum(jnp.maximum(values, -reach), reach).astype(held_as)


def setup_inputs(seed: int = 0, part: int = 0) -> dict:
    streams_of = jax.random.split(jax.random.key(seed), 6)
    part_keys = jax.random.split(jax.random.fold_in(streams_of[5], part), 6)
    signal = gaussian(part_keys[0], (SEQ, C), 1.0, 6.0, ((0, 8), (1, 2)))
    tangent = gaussian(part_keys[1], (SEQ, C), 1.0, 6.0, ((0, 8), (1, 2)))
    gains = jnp.clip(jnp.exp(math.log(2.0) - 1.3862944 * jax.random.uniform(streams_of[2], (LAYERS, C), jnp.float32) ** block_levels(streams_of[2], (LAYERS, C), ((1, 2),), -0.2, 0.2)), 0.5, 2.0)
    convolution_kernel = gaussian(streams_of[3], (LAYERS, 3 * C, 2, E), (3 * C) ** -0.5, 0.109375, ((1, 8), (3, 2)))
    mixing_kernel = gaussian(streams_of[4], (LAYERS, E, C), E ** -0.5, 0.25, ((1, 8), (2, 2)))
    return dict(signal=signal, tangent=tangent, gains=gains, convolution_kernel=convolution_kernel, mixing_kernel=mixing_kernel)


def lag_rows(values, delay_offset):
    head = jnp.zeros((delay_offset, values.shape[1]), values.dtype)
    return jnp.concatenate([head, values[:-delay_offset]], 0)

def reference(signal, tangent, gains, convolution_kernel, mixing_kernel):
    state = signal
    dstate = tangent
    for layer_number in range(LAYERS):
        dilation_step = FIRST_DILATION * 2 ** layer_number
        xval = state.astype(jnp.float32)
        dxval = dstate.astype(jnp.float32)
        mean_sq = lax.optimization_barrier(jnp.mean(xval * xval, axis=1, keepdims=True))
        mean_cross = lax.optimization_barrier(jnp.mean(xval * dxval, axis=1, keepdims=True))
        scale = lax.rsqrt(mean_sq + 1e-05)
        gain = gains[layer_number][None, :]
        normed = (gain * xval * scale).astype(jnp.bfloat16)
        dnormed = (gain * (dxval * scale - xval * scale * scale * scale * mean_cross)).astype(jnp.bfloat16)
        weight = convolution_kernel[layer_number].reshape(3 * C, 2 * E)

        def convolve(values):
            stacked = jnp.concatenate([values, lag_rows(values, dilation_step), lag_rows(values, 2 * dilation_step)], 1)
            return jnp.dot(stacked, weight, preferred_element_type=jnp.float32)
        full = convolve(normed)
        dfull = convolve(dnormed)
        filt, gate = (full[:, :E], full[:, E:])
        dfilt, dgate = (dfull[:, :E], dfull[:, E:])
        tanh_f = jnp.tanh(filt)
        sig_g = jax.nn.sigmoid(gate)
        gated = (tanh_f * sig_g).astype(jnp.bfloat16)
        dgated = ((1.0 - tanh_f * tanh_f) * sig_g * dfilt + tanh_f * sig_g * (1.0 - sig_g) * dgate).astype(jnp.bfloat16)
        mixed = jnp.dot(gated, mixing_kernel[layer_number], preferred_element_type=jnp.float32)
        dmixed = jnp.dot(dgated, mixing_kernel[layer_number], preferred_element_type=jnp.float32)
        state = (xval + mixed).astype(jnp.bfloat16)
        dstate = (dxval + dmixed).astype(jnp.bfloat16)
    return (state, dstate)
```

```python
import functools

import jax
import jax.numpy as jnp
from jax import lax
from jax.experimental import pallas as pl
from jax.experimental.pallas import tpu as pltpu
from jax.sharding import PartitionSpec as P

TAPS = 3
EPS = 1e-05
F32 = jnp.float32
BF16 = jnp.bfloat16
VMEM = pl.BlockSpec(memory_space=pltpu.VMEM)
SMEM = pl.BlockSpec(memory_space=pltpu.SMEM)
ANY = pl.BlockSpec(memory_space=pl.ANY)
PARAMS = pltpu.CompilerParams(vmem_limit_bytes=56 * 2**20)


def swap_chan(block):
    return lax.ppermute(block, "chan", [(0, 1), (1, 0)])


def swap_groups(block):
    return lax.ppermute(block, "groups", [(0, 1), (1, 0)])


def swap_pair(block, seq):
    return lax.ppermute(block, "seq", [(s, s ^ 1) for s in range(seq)])


def ring(block, seq, by):
    return lax.ppermute(block, "seq", [(s, (s + by) % seq) for s in range(seq)])


def from_behind(block, seq, by):
    return lax.ppermute(block, "seq", [(s - by, s) for s in range(by, seq)])


def weight_copies(place, convs, conv_rows, mix_rows, pairs, wide, mix, sems):
    copies = []

    def add(src, dst):
        copies.append(pltpu.make_async_copy(src, dst, sems.at[len(copies)]))

    if pairs is None:
        add(convs[0], wide)
        add(convs[1], mix)
        return copies
    s, g = place[0], place[1]
    seq = pairs[0]
    for ref, (by, dx, dy) in zip(convs, pairs[1]):
        owner = lax.rem(s + (seq - by), seq)
        if dx:
            owner = owner + 1 - 2 * lax.rem(owner, 2)
        half = (1 - g) if dy else g
        unit = owner * 2 + half
        add(
            ref.at[pl.ds(0, conv_rows)],
            wide.at[pl.ds(pl.multiple_of(unit * conv_rows, conv_rows), conv_rows)],
        )
        add(
            ref.at[pl.ds(conv_rows, mix_rows)],
            mix.at[pl.ds(pl.multiple_of(unit * mix_rows, mix_rows), mix_rows)],
        )
    return copies


def normalise(xm, xp, dxm, dxp, gm, gp, width):
    total = jnp.sum(xm * xm, axis=1, keepdims=True) + jnp.sum(xp * xp, axis=1, keepdims=True)
    cross = jnp.sum(xm * dxm, axis=1, keepdims=True) + jnp.sum(xp * dxp, axis=1, keepdims=True)
    scale = lax.rsqrt(total / width + EPS)
    factor = scale * scale * scale * (cross / width)
    return (
        (gm * xm * scale).astype(BF16),
        (gp * xp * scale).astype(BF16),
        (gm * (dxm * scale - xm * factor)).astype(BF16),
        (gp * (dxp * scale - xp * factor)).astype(BF16),
    )


def gate_into(out, full, dfull, branch):
    tanh_f = jnp.tanh(full[:, :branch])
    sig_g = jax.nn.sigmoid(full[:, branch:])
    out[0][...] = (tanh_f * sig_g).astype(BF16)
    out[1][...] = (
        (1.0 - tanh_f * tanh_f) * sig_g * dfull[:, :branch]
        + tanh_f * sig_g * (1.0 - sig_g) * dfull[:, branch:]
    ).astype(BF16)


def conv0_kernel(cfg, place, gm_ref, gp_ref, *refs):
    rows, half, branch, blocks, starts, slabs, conv_rows, mix_rows, pairs = cfg
    mine = refs[:blocks]
    theirs = refs[blocks : 2 * blocks]
    n_in = 2 * blocks + (2 if pairs is None else len(pairs[1]))
    convs = refs[2 * blocks : n_in]
    z_ref, mix_ref, wide, hm, hp, acc, sems = refs[n_in:]
    copies = weight_copies(place, convs, conv_rows, mix_rows, pairs, wide, mix_ref, sems)
    for copy in copies:
        copy.start()
    gm = gm_ref[0:1, :]
    gp = gp_ref[0:1, :]
    step = 64

    for b in range(blocks):
        base = (blocks - 1 - b) * rows

        def body(i, carry, b=b, base=base):
            at = pl.multiple_of(i * step, step)
            to = pl.multiple_of(base + i * step, step)
            xm = mine[b][0, pl.ds(at, step), :].astype(F32)
            dxm = mine[b][1, pl.ds(at, step), :].astype(F32)
            xp = theirs[b][0, pl.ds(at, step), :].astype(F32)
            dxp = theirs[b][1, pl.ds(at, step), :].astype(F32)
            a, c, d, e = normalise(xm, xp, dxm, dxp, gm, gp, 2 * half)
            hm[0, pl.ds(to, step), :] = a
            hp[0, pl.ds(to, step), :] = c
            hm[1, pl.ds(to, step), :] = d
            hp[1, pl.ds(to, step), :] = e
            return carry

        lax.fori_loop(0, rows // step, body, 0)
    for copy in copies:
        copy.wait()
    c = place[2]
    at_m = pl.multiple_of(c * half, half)
    at_p = pl.multiple_of((1 - c) * half, half)
    for begin, size, lags in slabs:
        for v in range(2):
            for k in range(TAPS):
                row = starts[lags + k]
                part = jnp.dot(
                    hm[v, row : row + size, :],
                    wide[pl.ds(2 * half * k + at_m, half), :],
                    preferred_element_type=F32,
                ) + jnp.dot(
                    hp[v, row : row + size, :],
                    wide[pl.ds(2 * half * k + at_p, half), :],
                    preferred_element_type=F32,
                )
                if k == 0:
                    acc[v, 0:size, :] = part
                else:
                    acc[v, 0:size, :] += part
        for r in range(0, size, rows):
            gate_into(
                (
                    z_ref.at[0, begin + r : begin + r + rows, :],
                    z_ref.at[1, begin + r : begin + r + rows, :],
                ),
                acc[0, r : r + rows, :],
                acc[1, r : r + rows, :],
                branch,
            )


def mix0_kernel(cfg, place, gm_ref, gp_ref, zm_ref, zp_ref, mixm_ref, mixp_ref, *refs):
    rows, half, branch, layer = cfg
    mine = refs[:TAPS]
    theirs = refs[TAPS : 2 * TAPS]
    hm_ref, hp_ref, state_ref = refs[2 * TAPS :]
    c = place[2]
    at_m = pl.ds(pl.multiple_of(c * branch, branch), branch)
    at_p = pl.ds(pl.multiple_of((1 - c) * branch, branch), branch)
    gm = gm_ref[layer : layer + 1, :]
    gp = gp_ref[layer : layer + 1, :]
    step = min(128, rows)
    for j in range(TAPS):
        base = (TAPS - 1 - j) * rows

        def body(i, carry, j=j, base=base):
            at = pl.multiple_of(i * step, step)
            to = pl.multiple_of(base + i * step, step)
            new = []
            for v in range(2):
                zm = zm_ref[v, pl.ds(to, step), :]
                zp = zp_ref[v, pl.ds(to, step), :]
                for x_ref, mix in ((mine[j], mixm_ref), (theirs[j], mixp_ref)):
                    y = jnp.dot(zm, mix[at_m, :], preferred_element_type=F32)
                    y = y + jnp.dot(zp, mix[at_p, :], preferred_element_type=F32)
                    new.append((x_ref[v, pl.ds(at, step), :].astype(F32) + y).astype(BF16))
            if j == 0:
                state_ref[0, pl.ds(at, step), :] = new[0]
                state_ref[1, pl.ds(at, step), :] = new[2]
            xm, xp, dxm, dxp = (t.astype(F32) for t in new)
            a, b, d, e = normalise(xm, xp, dxm, dxp, gm, gp, 2 * half)
            hm_ref[0, pl.ds(to, step), :] = a
            hp_ref[0, pl.ds(to, step), :] = b
            hm_ref[1, pl.ds(to, step), :] = d
            hp_ref[1, pl.ds(to, step), :] = e
            return carry

        lax.fori_loop(0, rows // step, body, 0)


def conv1_kernel(cfg, place, hm, hp, *refs):
    rows, half, branch, conv_rows, mix_rows, pairs = cfg
    n_in = 2 if pairs is None else len(pairs[1])
    convs = refs[:n_in]
    z_ref, mix_ref, wide, acc, sems = refs[n_in:]
    copies = weight_copies(place, convs, conv_rows, mix_rows, pairs, wide, mix_ref, sems)
    for copy in copies:
        copy.start()
    for copy in copies:
        copy.wait()
    c = place[2]
    at_m = pl.multiple_of(c * half, half)
    at_p = pl.multiple_of((1 - c) * half, half)
    for v in range(2):
        for k in range(TAPS):
            row = (TAPS - 1 - k) * rows
            part = jnp.dot(
                hm[v, row : row + rows, :],
                wide[pl.ds(2 * half * k + at_m, half), :],
                preferred_element_type=F32,
            ) + jnp.dot(
                hp[v, row : row + rows, :],
                wide[pl.ds(2 * half * k + at_p, half), :],
                preferred_element_type=F32,
            )
            if k == 0:
                acc[v, :, :] = part
            else:
                acc[v, :, :] += part
    gate_into((z_ref.at[0], z_ref.at[1]), acc[0], acc[1], branch)


def mix1_kernel(cfg, place, zm_ref, zp_ref, mix_ref, state_ref, out_ref, dout_ref):
    (branch,) = cfg
    c = place[2]
    at_m = pl.ds(pl.multiple_of(c * branch, branch), branch)
    at_p = pl.ds(pl.multiple_of((1 - c) * branch, branch), branch)
    for v, out in ((0, out_ref), (1, dout_ref)):
        y = jnp.dot(zm_ref[v], mix_ref[at_m, :], preferred_element_type=F32)
        y = y + jnp.dot(zp_ref[v], mix_ref[at_p, :], preferred_element_type=F32)
        out[...] = (state_ref[v].astype(F32) + y).astype(BF16)


def gather_weights(chunks, seq, share):
    order = []
    layers = []
    hops = seq // 2
    for chunk, across in zip(chunks, share):
        pieces = []
        order = []
        for k in range(hops):
            own = chunk if k == 0 else ring(chunk, seq, 2 * k)
            by_x = swap_pair(own, seq)
            by_y = swap_groups(own)
            both = swap_groups(by_x) if k < across else swap_pair(by_y, seq)
            for piece, dx, dy in ((own, 0, 0), (by_x, 1, 0), (by_y, 0, 1), (both, 1, 1)):
                pieces.append(piece)
                order.append((2 * k, dx, dy))
        layers.append(pieces)
    return layers, (seq, tuple(order))


def on_device(signal, tangent, gains, convolution_kernel, mixing_kernel):
    rows, half = signal.shape
    seq = lax.axis_size("seq")
    layers = gains.shape[0]
    branch = convolution_kernel.shape[3]
    shard = convolution_kernel.shape[1]
    mix_shard = mixing_kernel.shape[1]
    lag = rows * seq // 16
    place = jnp.stack([lax.axis_index("seq"), lax.axis_index("groups"), lax.axis_index("chan")])
    place = place.astype(jnp.int32)
    wide_rows, mix_whole = shard * seq, mix_shard * seq

    conv_local = convolution_kernel.reshape(layers, shard, 2 * branch)
    small = seq <= 8
    if small:
        conv_rows, mix_rows = shard // 2, mix_shard // 2
        g = lax.axis_index("groups")
        chunks = [
            jnp.concatenate(
                [
                    lax.dynamic_slice_in_dim(conv_local[l], g * conv_rows, conv_rows, 0),
                    lax.dynamic_slice_in_dim(mixing_kernel[l], g * mix_rows, mix_rows, 0),
                ],
                0,
            )
            for l in range(layers)
        ]
        weights, pairs = gather_weights(chunks, seq, (3, 2))
    else:
        conv_rows, mix_rows, pairs = shard, mix_shard, None
        weights = [
            [
                lax.all_gather(conv_local[l], "seq", axis=0, tiled=True),
                lax.all_gather(mixing_kernel[l], "seq", axis=0, tiled=True),
            ]
            for l in range(layers)
        ]

    own = jnp.stack([signal, tangent], 0)
    joined = 2 * lag == rows
    if joined:
        two = from_behind(own, seq, 2)
        odd = lax.rem(lax.axis_index("seq"), 2) == 1
        one = swap_pair(jnp.where(odd, two, own), seq)
        three = from_behind(one, seq, 2)
        mine = [own, one, two, three]
        step, used = lag, (0, 1, 2)
    else:
        mine = [own] + [from_behind(own, seq, k * (lag // rows)) for k in range(1, 7)]
        step, used = rows, (0, 2, 4)
    theirs = [swap_chan(block) for block in mine]
    gains_p = swap_chan(gains)
    blocks = len(mine)
    tall = blocks * rows
    starts = tuple(tall - rows - m * step for m in range(7))
    if joined:
        slabs = ((0, TAPS * rows, 4),)
    else:
        slabs = tuple(((TAPS - 1 - j) * rows, rows, 2 * j) for j in range(TAPS))
    slab = slabs[0][1]

    n_copies = 2 if pairs is None else 2 * len(pairs[1])
    cfg = (rows, half, branch, blocks, starts, slabs, conv_rows, mix_rows, pairs)
    z_mine, mix_mine = pl.pallas_call(
        functools.partial(conv0_kernel, cfg),
        out_shape=(
            jax.ShapeDtypeStruct((2, TAPS * rows, branch), BF16),
            jax.ShapeDtypeStruct((mix_whole, half), BF16),
        ),
        in_specs=[SMEM, VMEM, VMEM] + [VMEM] * (2 * blocks) + [ANY] * len(weights[0]),
        out_specs=(VMEM, VMEM),
        scratch_shapes=[
            pltpu.VMEM((wide_rows, 2 * branch), BF16),
            pltpu.VMEM((2, tall, half), BF16),
            pltpu.VMEM((2, tall, half), BF16),
            pltpu.VMEM((2, slab, 2 * branch), F32),
            pltpu.SemaphoreType.DMA((n_copies,)),
        ],
        compiler_params=PARAMS,
        name="conv0",
    )(place, gains, gains_p, *mine, *theirs, *weights[0])
    mix_theirs = swap_chan(mix_mine)
    z_theirs = swap_chan(z_mine)
    hm, hp, state = pl.pallas_call(
        functools.partial(mix0_kernel, (rows, half, branch, 1)),
        out_shape=(
            jax.ShapeDtypeStruct((2, TAPS * rows, half), BF16),
            jax.ShapeDtypeStruct((2, TAPS * rows, half), BF16),
            jax.ShapeDtypeStruct((2, rows, half), BF16),
        ),
        in_specs=[SMEM] + [VMEM] * (6 + 2 * TAPS),
        out_specs=(VMEM, VMEM, VMEM),
        compiler_params=PARAMS,
        name="mix0",
    )(
        place,
        gains,
        gains_p,
        z_mine,
        z_theirs,
        mix_mine,
        mix_theirs,
        *[mine[b] for b in used],
        *[theirs[b] for b in used],
    )
    z_mine, mix_mine = pl.pallas_call(
        functools.partial(conv1_kernel, (rows, half, branch, conv_rows, mix_rows, pairs)),
        out_shape=(
            jax.ShapeDtypeStruct((2, rows, branch), BF16),
            jax.ShapeDtypeStruct((mix_whole, half), BF16),
        ),
        in_specs=[SMEM, VMEM, VMEM] + [ANY] * len(weights[1]),
        out_specs=(VMEM, VMEM),
        scratch_shapes=[
            pltpu.VMEM((wide_rows, 2 * branch), BF16),
            pltpu.VMEM((2, rows, 2 * branch), F32),
            pltpu.SemaphoreType.DMA((n_copies,)),
        ],
        compiler_params=PARAMS,
        name="conv1",
    )(place, hm, hp, *weights[1])
    z_theirs = swap_chan(z_mine)
    return pl.pallas_call(
        functools.partial(mix1_kernel, (branch,)),
        out_shape=(
            jax.ShapeDtypeStruct((rows, half), BF16),
            jax.ShapeDtypeStruct((rows, half), BF16),
        ),
        in_specs=[SMEM] + [VMEM] * 4,
        out_specs=(VMEM, VMEM),
        compiler_params=PARAMS,
        name="mix1",
    )(place, z_mine, z_theirs, mix_mine, state)


def solution(mesh):
    return jax.shard_map(
        on_device,
        mesh=mesh,
        in_specs=(
            P(("groups", "seq"), "chan"),
            P(("groups", "seq"), "chan"),
            P(None, "chan"),
            P(None, "seq", None, "chan"),
            P(None, "seq", "chan"),
        ),
        out_specs=(P(("groups", "seq"), "chan"), P(("groups", "seq"), "chan")),
        check_vma=False,
    )
```

```python
import functools

import jax
import jax.numpy as jnp
from jax import lax
from jax.experimental import pallas as pl
from jax.experimental.pallas import tpu as pltpu
from jax.sharding import PartitionSpec as P

TAPS = 3
EPS = 1e-05
F32 = jnp.float32
BF16 = jnp.bfloat16
VMEM = pl.BlockSpec(memory_space=pltpu.VMEM)
SMEM = pl.BlockSpec(memory_space=pltpu.SMEM)
ANY = pl.BlockSpec(memory_space=pltpu.HBM)


def scoped(mebibytes):
    return pltpu.CompilerParams(vmem_limit_bytes=mebibytes * 2**20)


def near(block):
    return pltpu.with_memory_space_constraint(block, pltpu.VMEM)


def far(block):
    return pltpu.with_memory_space_constraint(block, pltpu.HBM)


def near_out(*shape):
    return pltpu.VMEM(shape, BF16)


def cost(flops, bytes_moved):
    return pl.CostEstimate(flops=flops, bytes_accessed=bytes_moved, transcendentals=0)


def swap_chan(block):
    return lax.ppermute(block, "chan", [(0, 1), (1, 0)])


def swap_groups(block):
    return lax.ppermute(block, "groups", [(0, 1), (1, 0)])


def swap_pair(block, seq):
    return lax.ppermute(block, "seq", [(s, s ^ 1) for s in range(seq)])


def ring(block, seq, by):
    return lax.ppermute(block, "seq", [(s, (s + by) % seq) for s in range(seq)])


def from_behind(block, seq, by):
    return lax.ppermute(block, "seq", [(s - by, s) for s in range(by, seq)])


def weight_moves(place, refs, conv_rows, mix_rows, pairs, wide, mix):
    if pairs is None:
        return [(refs[0], wide), (refs[1], mix)]
    s, g = place[0], place[1]
    seq, order = pairs
    moves = []
    for index, begin, skip, count, by, dx, dy in order:
        owner = lax.rem(s + (seq - by), seq)
        if dx:
            owner = owner + 1 - 2 * lax.rem(owner, 2)
        half = (1 - g) if dy else g
        unit = owner * 2 + half
        n_conv = min(conv_rows - skip, count)
        to = pl.multiple_of(unit * conv_rows + skip, 16)
        moves.append((refs[index].at[pl.ds(begin, n_conv)], wide.at[pl.ds(to, n_conv)]))
        if count > n_conv:
            to = pl.multiple_of(unit * mix_rows, 16)
            moves.append(
                (refs[index].at[pl.ds(begin + n_conv, mix_rows)], mix.at[pl.ds(to, mix_rows)])
            )
    return moves


def normalise(xm, xp, dxm, dxp, gm, gp, width):
    total = jnp.sum(xm * xm, axis=1, keepdims=True) + jnp.sum(xp * xp, axis=1, keepdims=True)
    cross = jnp.sum(xm * dxm, axis=1, keepdims=True) + jnp.sum(xp * dxp, axis=1, keepdims=True)
    scale = lax.rsqrt(total / width + EPS)
    factor = scale * scale * scale * (cross / width)
    return (
        (gm * xm * scale).astype(BF16),
        (gp * xp * scale).astype(BF16),
        (gm * (dxm * scale - xm * factor)).astype(BF16),
        (gp * (dxp * scale - xp * factor)).astype(BF16),
    )


def gate_into(out, full, dfull, branch):
    tanh_f = jnp.tanh(full[:, :branch])
    sig_g = jax.nn.sigmoid(full[:, branch:])
    out[0][...] = (tanh_f * sig_g).astype(BF16)
    out[1][...] = (
        (1.0 - tanh_f * tanh_f) * sig_g * dfull[:, :branch]
        + tanh_f * sig_g * (1.0 - sig_g) * dfull[:, branch:]
    ).astype(BF16)


def conv0_kernel(cfg, place, gm_ref, gp_ref, *refs):
    rows, half, branch, blocks, starts, slabs, conv_rows, mix_rows, pairs, n_conv = cfg
    convs = refs[2 * blocks : 2 * blocks + n_conv]
    z_ref, mix_ref, wide, raw, hm, hp, acc, sems, wsems = refs[2 * blocks + n_conv :]
    copies = [
        [
            pltpu.make_async_copy(refs[b + i * blocks], raw.at[i, b], sems.at[i, b])
            for i in range(2)
        ]
        for b in range(blocks)
    ]
    for pair in copies:
        for copy in pair:
            copy.start()
    moves = weight_moves(place, convs, conv_rows, mix_rows, pairs, wide, mix_ref)
    moves = [pltpu.make_async_copy(*move, wsems.at[i]) for i, move in enumerate(moves)]
    for copy in moves:
        copy.start()
    gm = gm_ref[0:1, :]
    gp = gp_ref[0:1, :]
    step = 64
    for b in range(blocks):
        base = (blocks - 1 - b) * rows
        for copy in copies[b]:
            copy.wait()

        def body(i, carry, b=b, base=base):
            at = pl.ds(pl.multiple_of(i * step, step), step)
            to = pl.ds(pl.multiple_of(base + i * step, step), step)
            xm = raw[0, b, 0, at, :].astype(F32)
            dxm = raw[0, b, 1, at, :].astype(F32)
            xp = raw[1, b, 0, at, :].astype(F32)
            dxp = raw[1, b, 1, at, :].astype(F32)
            hm[0, to, :], hp[0, to, :], hm[1, to, :], hp[1, to, :] = normalise(
                xm, xp, dxm, dxp, gm, gp, 2 * half
            )
            return carry

        lax.fori_loop(0, rows // step, body, 0)
    for copy in moves:
        copy.wait()
    c = place[2]
    at_m = pl.multiple_of(c * half, half)
    at_p = pl.multiple_of((1 - c) * half, half)
    for begin, size, lags in slabs:
        for k in range(TAPS):
            row = starts[lags + k]
            for v in range(2):
                part = jnp.dot(
                    hm[v, row : row + size, :],
                    wide[pl.ds(2 * half * k + at_m, half), :],
                    preferred_element_type=F32,
                ) + jnp.dot(
                    hp[v, row : row + size, :],
                    wide[pl.ds(2 * half * k + at_p, half), :],
                    preferred_element_type=F32,
                )
                if k == 0:
                    acc[v, 0:size, :] = part
                else:
                    acc[v, 0:size, :] += part
        for r in range(0, size, rows):
            gate_into(
                (
                    z_ref.at[0, begin + r : begin + r + rows, :],
                    z_ref.at[1, begin + r : begin + r + rows, :],
                ),
                acc[0, r : r + rows, :],
                acc[1, r : r + rows, :],
                branch,
            )


def mix0_kernel(cfg, place, gm_ref, gp_ref, zm_ref, zp_ref, mixm_ref, mixp_ref, *refs):
    rows, half, branch, layer = cfg
    mine = refs[:TAPS]
    theirs = refs[TAPS : 2 * TAPS]
    hm_ref, hp_ref, state_ref = refs[2 * TAPS :]
    c = place[2]
    at_m = pl.ds(pl.multiple_of(c * branch, branch), branch)
    at_p = pl.ds(pl.multiple_of((1 - c) * branch, branch), branch)
    gm = gm_ref[layer : layer + 1, :]
    gp = gp_ref[layer : layer + 1, :]
    step = min(128, rows)
    for j in range(TAPS):
        base = (TAPS - 1 - j) * rows

        def body(i, carry, j=j, base=base):
            at = pl.multiple_of(i * step, step)
            to = pl.multiple_of(base + i * step, step)
            new = []
            for v in range(2):
                zm = zm_ref[v, pl.ds(to, step), :]
                zp = zp_ref[v, pl.ds(to, step), :]
                for x_ref, mix in ((mine[j], mixm_ref), (theirs[j], mixp_ref)):
                    y = jnp.dot(zm, mix[at_m, :], preferred_element_type=F32)
                    y = y + jnp.dot(zp, mix[at_p, :], preferred_element_type=F32)
                    new.append((x_ref[v, pl.ds(at, step), :].astype(F32) + y).astype(BF16))
            if j == 0:
                state_ref[0, pl.ds(at, step), :] = new[0]
                state_ref[1, pl.ds(at, step), :] = new[2]
            xm, xp, dxm, dxp = (t.astype(F32) for t in new)
            a, b, d, e = normalise(xm, xp, dxm, dxp, gm, gp, 2 * half)
            hm_ref[j, 0, pl.ds(at, step), :] = a
            hp_ref[j, 0, pl.ds(at, step), :] = b
            hm_ref[j, 1, pl.ds(at, step), :] = d
            hp_ref[j, 1, pl.ds(at, step), :] = e
            return carry

        lax.fori_loop(0, rows // step, body, 0)


def conv1_kernel(cfg, place, hm, hp, *refs):
    rows, half, branch, conv_rows, mix_rows, pairs, n_conv = cfg
    convs = refs[:n_conv]
    z_ref, mix_ref, wide, acc = refs[n_conv:]
    for src, dst in weight_moves(place, convs, conv_rows, mix_rows, pairs, wide, mix_ref):
        dst[...] = src[...]
    c = place[2]
    at_m = pl.multiple_of(c * half, half)
    at_p = pl.multiple_of((1 - c) * half, half)
    for k in range(TAPS):
        part = jnp.dot(
            hm[k].reshape(2 * rows, half),
            wide[pl.ds(2 * half * k + at_m, half), :],
            preferred_element_type=F32,
        ) + jnp.dot(
            hp[k].reshape(2 * rows, half),
            wide[pl.ds(2 * half * k + at_p, half), :],
            preferred_element_type=F32,
        )
        if k == 0:
            acc[...] = part
        else:
            acc[...] += part
    gate_into((z_ref.at[0], z_ref.at[1]), acc[0:rows, :], acc[rows : 2 * rows, :], branch)


def mix1_kernel(cfg, place, zm_ref, zp_ref, mix_ref, state_ref, out_ref, dout_ref):
    (branch,) = cfg
    c = place[2]
    at_m = pl.ds(pl.multiple_of(c * branch, branch), branch)
    at_p = pl.ds(pl.multiple_of((1 - c) * branch, branch), branch)
    for v, out in ((0, out_ref), (1, dout_ref)):
        y = jnp.dot(zm_ref[v], mix_ref[at_m, :], preferred_element_type=F32)
        y = y + jnp.dot(zp_ref[v], mix_ref[at_p, :], preferred_element_type=F32)
        out[...] = (state_ref[v].astype(F32) + y).astype(BF16)


def exchange(own, chunks, seq):
    c0, c1 = chunks
    rows = own.shape[1]
    half = own.shape[2]
    unit = c0.shape[0]
    pieces = ([], [])
    order = ([], [])

    def keep(layer, array, *slots):
        for begin, skip, count, k, dx, dy in slots:
            order[layer].append((len(pieces[layer]), begin, skip, count, 2 * k, dx, dy))
        pieces[layer].append(array)

    def whole(layer, array, *slots):
        keep(layer, array, *[(i * unit, 0, unit, *slot) for i, slot in enumerate(slots)])

    def part(array, i):
        return array[i * unit : (i + 1) * unit]

    def cat(*arrays):
        return jnp.concatenate(arrays, 0)

    def flat(block):
        return block.reshape(2 * rows, half)

    def together(*blocks):
        return lax.optimization_barrier(blocks)

    def x(block):
        return swap_pair(block, seq)

    def y(block):
        return swap_groups(block)

    def z(block, by=1):
        return ring(block, seq, 2 * by)

    whole(0, c0, (0, 0, 0))
    whole(1, c1, (0, 0, 0))
    z1a, z1b = z(c0), z(c0, 3)
    c01 = cat(c0, c1)
    z1a, z1b, x1, y1, own, c1 = together(z1a, z1b, x(c01), y(c01), own, c1)
    whole(0, z1a, (1, 0, 0))
    whole(0, z1b, (3, 0, 0))
    x0, y0 = part(x1, 0), part(y1, 1)
    whole(0, x1, (0, 1, 0))
    keep(1, x1, (unit, 0, unit, 0, 1, 0))
    whole(0, y1, (0, 0, 1))
    keep(1, y1, (unit, 0, unit, 0, 0, 1))
    z2 = z(cat(z1a, flat(own)))
    x2 = x(cat(z1a, z1b, y0))
    y2 = y(cat(z1a, z1b, x0))
    z2, x2, y2, own, c1 = together(z2, x2, y2, own, c1)
    q2 = part(z2, 0)
    two = from_first(z2[unit:].reshape(own.shape), seq, 1)
    keep(0, z2, (0, 0, unit, 2, 0, 0))
    whole(0, x2, (1, 1, 0), (3, 1, 0))
    keep(1, x2, (2 * unit, 0, unit, 0, 1, 1))
    whole(0, y2, (1, 0, 1), (3, 0, 1), (0, 1, 1))
    z3a, z3b = z(c1), z(c1, 3)
    odd = lax.rem(lax.axis_index("seq"), 2) == 1
    x3 = x(cat(q2, flat(jnp.where(odd, two, own))))
    y3 = y(cat(q2, x2[: 2 * unit]))
    z3a, z3b, x3, y3 = together(z3a, z3b, x3, y3)
    one = from_first(x3[unit:].reshape(own.shape), seq, 0)
    whole(1, z3a, (1, 0, 0))
    whole(1, z3b, (3, 0, 0))
    keep(0, x3, (0, 0, unit, 2, 1, 0))
    whole(0, y3, (2, 0, 1), (1, 1, 1), (3, 1, 1))
    z4 = z(cat(z3a, flat(one)))
    x4 = x(cat(z3a, z3b))
    y4 = y(cat(z3a, z3b, part(x3, 0)))
    z4, x4, y4 = together(z4, x4, y4)
    p2 = part(z4, 0)
    three = from_first(z4[unit:].reshape(own.shape), seq, 1)
    keep(1, z4, (0, 0, unit, 2, 0, 0))
    whole(1, x4, (1, 1, 0), (3, 1, 0))
    whole(1, y4, (1, 0, 1), (3, 0, 1))
    keep(0, y4, (2 * unit, 0, unit, 2, 1, 1))
    x5 = x(cat(p2, part(y4, 0)))
    y5 = y(cat(p2, part(x4, 1)))
    whole(1, x5, (2, 1, 0), (1, 1, 1))
    whole(1, y5, (2, 0, 1), (3, 1, 1))
    cut = unit // 2
    x6 = x(y5[:cut])
    y6 = y(x5[cut:unit])
    keep(1, x6, (0, 0, cut, 2, 1, 1))
    keep(1, y6, (0, cut, unit - cut, 2, 1, 1))
    return (one, two, three), (x5, y5), pieces, tuple((seq, tuple(o)) for o in order)


def from_first(block, seq, planes):
    s = lax.axis_index("seq")
    first = s < 2 if planes else s < 1
    return jnp.where(first, jnp.zeros_like(block), block)


def on_device(signal, tangent, gains, convolution_kernel, mixing_kernel):
    rows, half = signal.shape
    seq = lax.axis_size("seq")
    layers = gains.shape[0]
    branch = convolution_kernel.shape[3]
    shard = convolution_kernel.shape[1]
    mix_shard = mixing_kernel.shape[1]
    lag = rows * seq // 16
    place = jnp.stack([lax.axis_index("seq"), lax.axis_index("groups"), lax.axis_index("chan")])
    place = place.astype(jnp.int32)
    wide_rows, mix_whole = shard * seq, mix_shard * seq

    conv_local = convolution_kernel.reshape(layers, shard, 2 * branch)
    own = jnp.stack([signal, tangent], 0)
    if 2 * lag == rows:
        conv_rows, mix_rows = shard // 2, mix_shard // 2
        g = lax.axis_index("groups")
        both = jnp.concatenate(
            [
                lax.dynamic_slice_in_dim(conv_local, g * conv_rows, conv_rows, 1),
                lax.dynamic_slice_in_dim(mixing_kernel, g * mix_rows, mix_rows, 1),
            ],
            1,
        )
        chunks = [both[l] for l in range(layers)]
        pairs = None
        step, used = lag, (0, 1, 2)
        blocks = 4
    else:
        conv_rows, mix_rows, pairs = shard, mix_shard, (None, None)
        weights = [
            [
                lax.all_gather(conv_local[l], "seq", axis=0, tiled=True),
                lax.all_gather(mixing_kernel[l], "seq", axis=0, tiled=True),
            ]
            for l in range(layers)
        ]
        step, used = rows, (0, 2, 4)
        blocks = 7
    gains_p = swap_chan(gains)
    tall = blocks * rows
    starts = tuple(tall - rows - m * step for m in range(7))
    if 2 * lag == rows:
        slabs = ((0, TAPS * rows, 4),)
    else:
        slabs = tuple(((TAPS - 1 - j) * rows, rows, 2 * j) for j in range(TAPS))
    slab = slabs[0][1]

    if pairs is None:
        halo, beside, weights, pairs = exchange(own, chunks, seq)
        mine = [own, *halo]
    else:
        beside = ()
        mine = [own] + [from_behind(own, seq, k * (lag // rows)) for k in range(1, 7)]
    theirs = [swap_chan(block) for block in mine]

    n_conv = [len(w) for w in weights]
    cfg = (rows, half, branch, blocks, starts, slabs, conv_rows, mix_rows, pairs[0], n_conv[0])
    z_mine, mix_mine = pl.pallas_call(
        functools.partial(conv0_kernel, cfg),
        out_shape=(near_out(2, TAPS * rows, branch), near_out(mix_whole, half)),
        in_specs=[SMEM, VMEM, VMEM] + [ANY] * (2 * blocks + n_conv[0]),
        out_specs=(VMEM, VMEM),
        scratch_shapes=[
            pltpu.VMEM((wide_rows, 2 * branch), BF16),
            pltpu.VMEM((2, blocks, 2, rows, half), BF16),
            pltpu.VMEM((2, tall, half), BF16),
            pltpu.VMEM((2, tall, half), BF16),
            pltpu.VMEM((2, slab, 2 * branch), F32),
            pltpu.SemaphoreType.DMA((2, blocks)),
            pltpu.SemaphoreType.DMA((2 if pairs[0] is None else 2 * len(pairs[0][1]),)),
        ],
        compiler_params=scoped(28),
        cost_estimate=cost(0, 32 * 2**20),
        name="conv0",
    )(
        place,
        near(gains),
        near(gains_p),
        *[far(block) for block in (*mine, *theirs, *weights[0])],
    )
    z_mine, mix_mine = lax.optimization_barrier((z_mine, mix_mine, *beside))[:2]
    mix_theirs = swap_chan(mix_mine)
    z_theirs = swap_chan(z_mine)
    hm, hp, state = pl.pallas_call(
        functools.partial(mix0_kernel, (rows, half, branch, 1)),
        out_shape=(
            near_out(TAPS, 2, rows, half),
            near_out(TAPS, 2, rows, half),
            near_out(2, rows, half),
        ),
        in_specs=[SMEM] + [VMEM] * (6 + 2 * TAPS),
        out_specs=(VMEM, VMEM, VMEM),
        compiler_params=scoped(6),
        cost_estimate=cost(0, 20 * 2**20),
        name="mix0",
    )(
        place,
        near(gains),
        near(gains_p),
        z_mine,
        near(z_theirs),
        mix_mine,
        near(mix_theirs),
        *[near(mine[b]) for b in used],
        *[near(theirs[b]) for b in used],
    )
    cfg = (rows, half, branch, conv_rows, mix_rows, pairs[1], n_conv[1])
    z_mine, mix_mine = pl.pallas_call(
        functools.partial(conv1_kernel, cfg),
        out_shape=(near_out(2, rows, branch), near_out(mix_whole, half)),
        in_specs=[SMEM] + [VMEM] * (2 + n_conv[1]),
        out_specs=(VMEM, VMEM),
        scratch_shapes=[
            pltpu.VMEM((wide_rows, 2 * branch), BF16),
            pltpu.VMEM((2 * rows, 2 * branch), F32),
        ],
        compiler_params=scoped(8),
        name="conv1",
    )(place, hm, hp, *[near(w) for w in weights[1]])
    z_theirs = swap_chan(z_mine)
    return pl.pallas_call(
        functools.partial(mix1_kernel, (branch,)),
        out_shape=(
            jax.ShapeDtypeStruct((rows, half), BF16),
            jax.ShapeDtypeStruct((rows, half), BF16),
        ),
        in_specs=[SMEM] + [VMEM] * 4,
        out_specs=(VMEM, VMEM),
        compiler_params=scoped(4),
        name="mix1",
    )(place, z_mine, near(z_theirs), mix_mine, state)


def solution(mesh):
    return jax.shard_map(
        on_device,
        mesh=mesh,
        in_specs=(
            P(("groups", "seq"), "chan"),
            P(("groups", "seq"), "chan"),
            P(None, "chan"),
            P(None, "seq", None, "chan"),
            P(None, "seq", "chan"),
        ),
        out_specs=(P(("groups", "seq"), "chan"), P(("groups", "seq"), "chan")),
        check_vma=False,
    )
```

```python
import functools

import jax
import jax.numpy as jnp
from jax import lax
from jax.experimental import pallas as pl
from jax.experimental.pallas import tpu as pltpu
from jax.sharding import PartitionSpec as P

TAPS = 3
EPS = 1e-05
F32 = jnp.float32
BF16 = jnp.bfloat16
VMEM = pl.BlockSpec(memory_space=pltpu.VMEM)
SMEM = pl.BlockSpec(memory_space=pltpu.SMEM)
ANY = pl.BlockSpec(memory_space=pltpu.HBM)


def scoped(mebibytes):
    return pltpu.CompilerParams(vmem_limit_bytes=mebibytes * 2**20)


def near(block):
    return pltpu.with_memory_space_constraint(block, pltpu.VMEM)


def far(block):
    return pltpu.with_memory_space_constraint(block, pltpu.HBM)


def near_out(*shape):
    return pltpu.VMEM(shape, BF16)


def cost(flops, bytes_moved):
    return pl.CostEstimate(flops=flops, bytes_accessed=bytes_moved, transcendentals=0)


def swap_chan(block):
    return lax.ppermute(block, "chan", [(0, 1), (1, 0)])


def swap_groups(block):
    return lax.ppermute(block, "groups", [(0, 1), (1, 0)])


def swap_pair(block, seq):
    return lax.ppermute(block, "seq", [(s, s ^ 1) for s in range(seq)])


def ring(block, seq, by):
    return lax.ppermute(block, "seq", [(s, (s + by) % seq) for s in range(seq)])


def from_behind(block, seq, by):
    return lax.ppermute(block, "seq", [(s - by, s) for s in range(by, seq)])


def weight_moves(place, refs, conv_rows, mix_rows, pairs, wide, mix):
    if pairs is None:
        return [(refs[0], wide), (refs[1], mix)]
    s, g = place[0], place[1]
    seq, order = pairs
    moves = []
    for index, begin, skip, count, by, dx, dy in order:
        owner = lax.rem(s + (seq - by), seq)
        if dx:
            owner = owner + 1 - 2 * lax.rem(owner, 2)
        half = (1 - g) if dy else g
        unit = owner * 2 + half
        n_conv = min(conv_rows - skip, count)
        to = pl.multiple_of(unit * conv_rows + skip, 16)
        moves.append((refs[index].at[pl.ds(begin, n_conv)], wide.at[pl.ds(to, n_conv)]))
        if count > n_conv:
            to = pl.multiple_of(unit * mix_rows, 16)
            moves.append(
                (refs[index].at[pl.ds(begin + n_conv, mix_rows)], mix.at[pl.ds(to, mix_rows)])
            )
    return moves


def normalise(xm, xp, dxm, dxp, gm, gp, width):
    total = jnp.sum(xm * xm, axis=1, keepdims=True) + jnp.sum(xp * xp, axis=1, keepdims=True)
    cross = jnp.sum(xm * dxm, axis=1, keepdims=True) + jnp.sum(xp * dxp, axis=1, keepdims=True)
    scale = lax.rsqrt(total / width + EPS)
    factor = scale * scale * scale * (cross / width)
    return (
        (gm * xm * scale).astype(BF16),
        (gp * xp * scale).astype(BF16),
        (gm * (dxm * scale - xm * factor)).astype(BF16),
        (gp * (dxp * scale - xp * factor)).astype(BF16),
    )


def gate_into(out, full, dfull, branch):
    tanh_f = jnp.tanh(full[:, :branch])
    sig_g = jax.nn.sigmoid(full[:, branch:])
    out[0][...] = (tanh_f * sig_g).astype(BF16)
    out[1][...] = (
        (1.0 - tanh_f * tanh_f) * sig_g * dfull[:, :branch]
        + tanh_f * sig_g * (1.0 - sig_g) * dfull[:, branch:]
    ).astype(BF16)


def conv0_kernel(cfg, place, gm_ref, gp_ref, *refs):
    rows, half, branch, blocks, starts, slabs, conv_rows, mix_rows, pairs, n_conv = cfg
    convs = refs[2 * blocks : 2 * blocks + n_conv]
    z_ref, mix_ref, wide, hm, hp, acc = refs[2 * blocks + n_conv :]
    moves = weight_moves(place, convs, conv_rows, mix_rows, pairs, wide, mix_ref)
    for src, dst in moves:
        dst[...] = src[...]
    gm = gm_ref[0:1, :]
    gp = gp_ref[0:1, :]
    step = 64
    for b in range(blocks):
        base = (blocks - 1 - b) * rows

        def body(i, carry, b=b, base=base):
            at = pl.ds(pl.multiple_of(i * step, step), step)
            to = pl.ds(pl.multiple_of(base + i * step, step), step)
            xm = refs[b][0, at, :].astype(F32)
            dxm = refs[b][1, at, :].astype(F32)
            xp = refs[b + blocks][0, at, :].astype(F32)
            dxp = refs[b + blocks][1, at, :].astype(F32)
            hm[0, to, :], hp[0, to, :], hm[1, to, :], hp[1, to, :] = normalise(
                xm, xp, dxm, dxp, gm, gp, 2 * half
            )
            return carry

        lax.fori_loop(0, rows // step, body, 0)
    c = place[2]
    at_m = pl.multiple_of(c * half, half)
    at_p = pl.multiple_of((1 - c) * half, half)
    for begin, size, lags in slabs:
        for k in range(TAPS):
            row = starts[lags + k]
            for v in range(2):
                part = jnp.dot(
                    hm[v, row : row + size, :],
                    wide[pl.ds(2 * half * k + at_m, half), :],
                    preferred_element_type=F32,
                ) + jnp.dot(
                    hp[v, row : row + size, :],
                    wide[pl.ds(2 * half * k + at_p, half), :],
                    preferred_element_type=F32,
                )
                if k == 0:
                    acc[v, 0:size, :] = part
                else:
                    acc[v, 0:size, :] += part
        for r in range(0, size, rows):
            gate_into(
                (
                    z_ref.at[0, begin + r : begin + r + rows, :],
                    z_ref.at[1, begin + r : begin + r + rows, :],
                ),
                acc[0, r : r + rows, :],
                acc[1, r : r + rows, :],
                branch,
            )


def mix0_kernel(cfg, place, gm_ref, gp_ref, zm_ref, zp_ref, mixm_ref, mixp_ref, *refs):
    rows, half, branch, layer = cfg
    mine = refs[:TAPS]
    theirs = refs[TAPS : 2 * TAPS]
    hm_ref, hp_ref, state_ref = refs[2 * TAPS :]
    c = place[2]
    at_m = pl.ds(pl.multiple_of(c * branch, branch), branch)
    at_p = pl.ds(pl.multiple_of((1 - c) * branch, branch), branch)
    gm = gm_ref[layer : layer + 1, :]
    gp = gp_ref[layer : layer + 1, :]
    step = min(256, rows)
    for j in range(TAPS):
        base = (TAPS - 1 - j) * rows

        def body(i, carry, j=j, base=base):
            at = pl.multiple_of(i * step, step)
            to = pl.multiple_of(base + i * step, step)
            new = []
            for v in range(2):
                zm = zm_ref[v, pl.ds(to, step), :]
                zp = zp_ref[v, pl.ds(to, step), :]
                for x_ref, mix in ((mine[j], mixm_ref), (theirs[j], mixp_ref)):
                    y = jnp.dot(zm, mix[at_m, :], preferred_element_type=F32)
                    y = y + jnp.dot(zp, mix[at_p, :], preferred_element_type=F32)
                    new.append((x_ref[v, pl.ds(at, step), :].astype(F32) + y).astype(BF16))
            if j == 0:
                state_ref[0, pl.ds(at, step), :] = new[0]
                state_ref[1, pl.ds(at, step), :] = new[2]
            xm, xp, dxm, dxp = (t.astype(F32) for t in new)
            a, b, d, e = normalise(xm, xp, dxm, dxp, gm, gp, 2 * half)
            hm_ref[j, 0, pl.ds(at, step), :] = a
            hp_ref[j, 0, pl.ds(at, step), :] = b
            hm_ref[j, 1, pl.ds(at, step), :] = d
            hp_ref[j, 1, pl.ds(at, step), :] = e
            return carry

        lax.fori_loop(0, rows // step, body, 0)


def conv1_kernel(cfg, place, hm, hp, *refs):
    rows, half, branch, conv_rows, mix_rows, pairs, n_conv = cfg
    convs = refs[:n_conv]
    z_ref, mix_ref, wide, acc = refs[n_conv:]
    for src, dst in weight_moves(place, convs, conv_rows, mix_rows, pairs, wide, mix_ref):
        dst[...] = src[...]
    c = place[2]
    at_m = pl.multiple_of(c * half, half)
    at_p = pl.multiple_of((1 - c) * half, half)
    for k in range(TAPS):
        part = jnp.dot(
            hm[k].reshape(2 * rows, half),
            wide[pl.ds(2 * half * k + at_m, half), :],
            preferred_element_type=F32,
        ) + jnp.dot(
            hp[k].reshape(2 * rows, half),
            wide[pl.ds(2 * half * k + at_p, half), :],
            preferred_element_type=F32,
        )
        if k == 0:
            acc[...] = part
        else:
            acc[...] += part
    gate_into((z_ref.at[0], z_ref.at[1]), acc[0:rows, :], acc[rows : 2 * rows, :], branch)


def mix1_kernel(cfg, place, zm_ref, zp_ref, mix_ref, state_ref, out_ref, dout_ref):
    (branch,) = cfg
    c = place[2]
    at_m = pl.ds(pl.multiple_of(c * branch, branch), branch)
    at_p = pl.ds(pl.multiple_of((1 - c) * branch, branch), branch)
    for v, out in ((0, out_ref), (1, dout_ref)):
        y = jnp.dot(zm_ref[v], mix_ref[at_m, :], preferred_element_type=F32)
        y = y + jnp.dot(zp_ref[v], mix_ref[at_p, :], preferred_element_type=F32)
        out[...] = (state_ref[v].astype(F32) + y).astype(BF16)


def pack(seq, place, *buffers):
    arrays = []

    def index(array):
        for i, known in enumerate(arrays):
            if known is array:
                return i
        arrays.append(array)
        return len(arrays) - 1

    plan = []
    for buffer in buffers:
        parts = []
        for array, begin, count, *mark in buffer:
            planes, even = (mark + [None, None])[:2] if mark else (None, None)
            parts.append(
                (index(array), begin, count, planes, None if even is None else index(even))
            )
        plan.append(parts)
    width = arrays[0].shape[-1]

    def kernel(place_ref, *refs):
        s = place_ref[0]
        for out, parts in zip(refs[len(arrays) :], plan):
            to = 0
            for i, begin, count, planes, even in parts:
                value = refs[i][begin : begin + count, :]
                if planes is not None:
                    value = jnp.where(s < max(2 * planes, 1), jnp.zeros_like(value), value)
                if even is not None:
                    value = jnp.where(lax.rem(s, 2) == 1, value, refs[even][...])
                out[to : to + count, :] = value
                to += count

    return pl.pallas_call(
        kernel,
        out_shape=tuple(near_out(sum(part[2] for part in buf), width) for buf in buffers),
        in_specs=[SMEM] + [VMEM] * len(arrays),
        out_specs=(VMEM,) * len(buffers),
        compiler_params=scoped(4),
        name="pack",
    )(place, *[near(array) for array in arrays])


def exchange(place, own, chunks, gains, seq):
    both = chunks
    unit = both.shape[0] // 2
    tall = own.shape[0]
    pieces = ([], [])
    order = ([], [])

    def keep(layer, array, *slots):
        for begin, skip, count, k, dx, dy in slots:
            order[layer].append((len(pieces[layer]), begin, skip, count, 2 * k, dx, dy))
        pieces[layer].append(array)

    def whole(layer, array, *slots):
        keep(layer, array, *[(i * unit, 0, unit, *slot) for i, slot in enumerate(slots)])

    def together(*blocks):
        return lax.optimization_barrier(blocks)

    def x(block):
        return swap_pair(block, seq)

    def y(block):
        return swap_groups(block)

    def z(block, by=1):
        return ring(block, seq, 2 * by)

    c0, c1 = both[:unit], both[unit:]
    whole(0, both, (0, 0, 0))
    keep(1, both, (unit, 0, unit, 0, 0, 0))
    z1a, z1b, x1, y1, own, c1 = together(z(c0), z(c0, 3), x(both), y(both), own, c1)
    whole(0, z1a, (1, 0, 0))
    whole(0, z1b, (3, 0, 0))
    whole(0, x1, (0, 1, 0))
    keep(1, x1, (unit, 0, unit, 0, 1, 0))
    whole(0, y1, (0, 0, 1))
    keep(1, y1, (unit, 0, unit, 0, 0, 1))
    to_z, to_x, to_y = pack(
        seq,
        place,
        [(z1a, 0, unit), (own, 0, tall)],
        [(z1a, 0, unit), (z1b, 0, unit), (y1, unit, unit)],
        [(z1a, 0, unit), (z1b, 0, unit), (x1, 0, unit)],
    )
    z2, x2, y2, own, c1, gains_p = together(z(to_z), x(to_x), y(to_y), own, c1, swap_chan(gains))
    keep(0, z2, (0, 0, unit, 2, 0, 0))
    whole(0, x2, (1, 1, 0), (3, 1, 0))
    keep(1, x2, (2 * unit, 0, unit, 0, 1, 1))
    whole(0, y2, (1, 0, 1), (3, 0, 1), (0, 1, 1))
    to_z, to_x, to_y, two = pack(
        seq,
        place,
        [(both, unit, unit), (x2, 2 * unit, unit)],
        [(z2, 0, unit), (z2, unit, tall, 1, own)],
        [(z2, 0, unit), (x2, 0, 2 * unit)],
        [(z2, unit, tall, 1)],
    )
    z3a, z3b, x3, y3 = together(z(to_z), z(c1, 3), x(to_x), y(to_y))
    whole(1, z3a, (1, 0, 0), (1, 1, 1))
    whole(1, z3b, (3, 0, 0))
    keep(0, x3, (0, 0, unit, 2, 1, 0))
    whole(0, y3, (2, 0, 1), (1, 1, 1), (3, 1, 1))
    to_z, to_x, to_y, one = pack(
        seq,
        place,
        [(z3a, 0, unit), (x3, unit, tall, 0)],
        [(z3a, 0, unit), (z3b, 0, unit)],
        [(z3a, 0, unit), (z3b, 0, unit), (x3, 0, unit)],
        [(x3, unit, tall, 0)],
    )
    z4, x4, y4 = together(z(to_z), x(to_x), y(to_y))
    keep(1, z4, (0, 0, unit, 2, 0, 0))
    whole(1, x4, (1, 1, 0), (3, 1, 0))
    whole(1, y4, (1, 0, 1), (3, 0, 1))
    keep(0, y4, (2 * unit, 0, unit, 2, 1, 1))
    cut = unit // 2
    to_z, to_x, to_y, three = pack(
        seq,
        place,
        [(z3a, unit, unit)],
        [(z4, 0, unit), (y4, unit, cut)],
        [(z4, 0, unit), (x4, unit + cut, unit - cut)],
        [(z4, unit, tall, 1)],
    )
    x5, y5, z5 = x(to_x), y(to_y), z(to_z)
    whole(1, z5, (2, 1, 1))
    keep(1, x5, (0, 0, unit, 2, 1, 0), (unit, 0, cut, 3, 1, 1))
    keep(1, y5, (0, 0, unit, 2, 0, 1), (unit, cut, unit - cut, 3, 1, 1))
    return gains_p, (one, two, three), (x5, y5, z5), pieces, tuple((seq, tuple(o)) for o in order)


def on_device(signal, tangent, gains, convolution_kernel, mixing_kernel):
    rows, half = signal.shape
    seq = lax.axis_size("seq")
    layers = gains.shape[0]
    branch = convolution_kernel.shape[3]
    shard = convolution_kernel.shape[1]
    mix_shard = mixing_kernel.shape[1]
    lag = rows * seq // 16
    place = jnp.stack([lax.axis_index("seq"), lax.axis_index("groups"), lax.axis_index("chan")])
    place = place.astype(jnp.int32)
    wide_rows, mix_whole = shard * seq, mix_shard * seq

    conv_local = convolution_kernel.reshape(layers, shard, 2 * branch)
    own = jnp.stack([signal, tangent], 0)
    if 2 * lag == rows:
        conv_rows, mix_rows = shard // 2, mix_shard // 2
        g = lax.axis_index("groups")
        chunks = jnp.concatenate(
            [
                lax.dynamic_slice_in_dim(conv_local, g * conv_rows, conv_rows, 1),
                lax.dynamic_slice_in_dim(mixing_kernel, g * mix_rows, mix_rows, 1),
            ],
            1,
        ).reshape(layers * (conv_rows + mix_rows), 2 * branch)
        pairs = None
        step, used = lag, (0, 1, 2)
        blocks = 4
    else:
        conv_rows, mix_rows, pairs = shard, mix_shard, (None, None)
        weights = [
            [
                lax.all_gather(conv_local[l], "seq", axis=0, tiled=True),
                lax.all_gather(mixing_kernel[l], "seq", axis=0, tiled=True),
            ]
            for l in range(layers)
        ]
        step, used = rows, (0, 2, 4)
        blocks = 7
    tall = blocks * rows
    starts = tuple(tall - rows - m * step for m in range(7))
    if 2 * lag == rows:
        slabs = ((0, TAPS * rows, 4),)
    else:
        slabs = tuple(((TAPS - 1 - j) * rows, rows, 2 * j) for j in range(TAPS))
    slab = slabs[0][1]

    if pairs is None:
        gains_p, halo, beside, weights, pairs = exchange(
            place, own.reshape(2 * rows, half), chunks, gains, seq
        )
        mine = [own, *[block.reshape(own.shape) for block in halo]]
    else:
        beside = ()
        gains_p = swap_chan(gains)
        mine = [own] + [from_behind(own, seq, k * (lag // rows)) for k in range(1, 7)]
    theirs = [swap_chan(block) for block in mine]

    n_conv = [len(w) for w in weights]
    cfg = (rows, half, branch, blocks, starts, slabs, conv_rows, mix_rows, pairs[0], n_conv[0])
    z_mine, mix_mine = pl.pallas_call(
        functools.partial(conv0_kernel, cfg),
        out_shape=(near_out(2, TAPS * rows, branch), near_out(mix_whole, half)),
        in_specs=[SMEM] + [VMEM] * (2 + 2 * blocks + n_conv[0]),
        out_specs=(VMEM, VMEM),
        scratch_shapes=[
            pltpu.VMEM((wide_rows, 2 * branch), BF16),
            pltpu.VMEM((2, tall, half), BF16),
            pltpu.VMEM((2, tall, half), BF16),
            pltpu.VMEM((2, slab, 2 * branch), F32),
        ],
        compiler_params=scoped(20),
        cost_estimate=cost(0, 32 * 2**20),
        name="conv0",
    )(
        place,
        near(gains),
        near(gains_p),
        *[near(block) for block in (*mine, *theirs)],
        *[near(w) for w in weights[0]],
    )
    z_mine, mix_mine = lax.optimization_barrier((z_mine, mix_mine, *beside))[:2]
    mix_theirs = swap_chan(mix_mine)
    z_theirs = swap_chan(z_mine)
    hm, hp, state = pl.pallas_call(
        functools.partial(mix0_kernel, (rows, half, branch, 1)),
        out_shape=(
            near_out(TAPS, 2, rows, half),
            near_out(TAPS, 2, rows, half),
            near_out(2, rows, half),
        ),
        in_specs=[SMEM] + [VMEM] * (6 + 2 * TAPS),
        out_specs=(VMEM, VMEM, VMEM),
        compiler_params=scoped(6),
        cost_estimate=cost(0, 20 * 2**20),
        name="mix0",
    )(
        place,
        near(gains),
        near(gains_p),
        z_mine,
        near(z_theirs),
        mix_mine,
        near(mix_theirs),
        *[near(mine[b]) for b in used],
        *[near(theirs[b]) for b in used],
    )
    cfg = (rows, half, branch, conv_rows, mix_rows, pairs[1], n_conv[1])
    z_mine, mix_mine = pl.pallas_call(
        functools.partial(conv1_kernel, cfg),
        out_shape=(near_out(2, rows, branch), near_out(mix_whole, half)),
        in_specs=[SMEM] + [VMEM] * (2 + n_conv[1]),
        out_specs=(VMEM, VMEM),
        scratch_shapes=[
            pltpu.VMEM((wide_rows, 2 * branch), BF16),
            pltpu.VMEM((2 * rows, 2 * branch), F32),
        ],
        compiler_params=scoped(8),
        name="conv1",
    )(place, hm, hp, *[near(w) for w in weights[1]])
    z_theirs = swap_chan(z_mine)
    return pl.pallas_call(
        functools.partial(mix1_kernel, (branch,)),
        out_shape=(
            jax.ShapeDtypeStruct((rows, half), BF16),
            jax.ShapeDtypeStruct((rows, half), BF16),
        ),
        in_specs=[SMEM] + [VMEM] * 4,
        out_specs=(VMEM, VMEM),
        compiler_params=scoped(4),
        name="mix1",
    )(place, z_mine, near(z_theirs), mix_mine, state)


def solution(mesh):
    return jax.shard_map(
        on_device,
        mesh=mesh,
        in_specs=(
            P(("groups", "seq"), "chan"),
            P(("groups", "seq"), "chan"),
            P(None, "chan"),
            P(None, "seq", None, "chan"),
            P(None, "seq", "chan"),
        ),
        out_specs=(P(("groups", "seq"), "chan"), P(("groups", "seq"), "chan")),
        check_vma=False,
    )
```

```python
import functools

import jax
import jax.numpy as jnp
from jax import lax
from jax.experimental import pallas as pl
from jax.experimental.pallas import tpu as pltpu
from jax.sharding import PartitionSpec as P

TAPS = 3
EPS = 1e-05
F32 = jnp.float32
BF16 = jnp.bfloat16
VMEM = pl.BlockSpec(memory_space=pltpu.VMEM)
SMEM = pl.BlockSpec(memory_space=pltpu.SMEM)
ANY = pl.BlockSpec(memory_space=pltpu.HBM)


def scoped(mebibytes):
    return pltpu.CompilerParams(vmem_limit_bytes=mebibytes * 2**20)


def near(block):
    return pltpu.with_memory_space_constraint(block, pltpu.VMEM)


def far(block):
    return pltpu.with_memory_space_constraint(block, pltpu.HBM)


def near_out(*shape):
    return pltpu.VMEM(shape, BF16)


def cost(flops, bytes_moved):
    return pl.CostEstimate(flops=flops, bytes_accessed=bytes_moved, transcendentals=0)


def swap_chan(block):
    return lax.ppermute(block, "chan", [(0, 1), (1, 0)])


def swap_groups(block):
    return lax.ppermute(block, "groups", [(0, 1), (1, 0)])


def swap_pair(block, seq):
    return lax.ppermute(block, "seq", [(s, s ^ 1) for s in range(seq)])


def ring(block, seq, by):
    return lax.ppermute(block, "seq", [(s, (s + by) % seq) for s in range(seq)])


def from_behind(block, seq, by):
    return lax.ppermute(block, "seq", [(s - by, s) for s in range(by, seq)])


def weight_moves(place, refs, conv_rows, mix_rows, pairs, wide, mix):
    if pairs is None:
        return [(refs[0], wide), (refs[1], mix)]
    s, g = place[0], place[1]
    seq, order = pairs
    moves = []
    for index, begin, skip, count, by, dx, dy in order:
        owner = lax.rem(s + (seq - by), seq)
        if dx:
            owner = owner + 1 - 2 * lax.rem(owner, 2)
        half = (1 - g) if dy else g
        unit = owner * 2 + half
        n_conv = min(conv_rows - skip, count)
        if wide is not None:
            to = pl.multiple_of(unit * conv_rows + skip, 16)
            moves.append((refs[index].at[pl.ds(begin, n_conv)], wide.at[pl.ds(to, n_conv)]))
        if count > n_conv and mix is not None:
            to = pl.multiple_of(unit * mix_rows, 16)
            moves.append(
                (refs[index].at[pl.ds(begin + n_conv, mix_rows)], mix.at[pl.ds(to, mix_rows)])
            )
    return moves


def normalise(xm, xp, dxm, dxp, gm, gp, width):
    total = jnp.sum(xm * xm, axis=1, keepdims=True) + jnp.sum(xp * xp, axis=1, keepdims=True)
    cross = jnp.sum(xm * dxm, axis=1, keepdims=True) + jnp.sum(xp * dxp, axis=1, keepdims=True)
    scale = lax.rsqrt(total / width + EPS)
    factor = scale * scale * scale * (cross / width)
    return (
        (gm * xm * scale).astype(BF16),
        (gp * xp * scale).astype(BF16),
        (gm * (dxm * scale - xm * factor)).astype(BF16),
        (gp * (dxp * scale - xp * factor)).astype(BF16),
    )


def gate_into(out, full, dfull, branch):
    tanh_f = jnp.tanh(full[:, :branch])
    sig_g = jax.nn.sigmoid(full[:, branch:])
    out[0][...] = (tanh_f * sig_g).astype(BF16)
    out[1][...] = (
        (1.0 - tanh_f * tanh_f) * sig_g * dfull[:, :branch]
        + tanh_f * sig_g * (1.0 - sig_g) * dfull[:, branch:]
    ).astype(BF16)


def norm_rows(gm, gp, mine, theirs, hm, hp, base):
    rows, half = mine.shape[1:]
    step = 64

    def body(i, carry):
        at = pl.ds(pl.multiple_of(i * step, step), step)
        to = pl.ds(pl.multiple_of(base + i * step, step), step)
        xm = mine[0, at, :].astype(F32)
        dxm = mine[1, at, :].astype(F32)
        xp = theirs[0, at, :].astype(F32)
        dxp = theirs[1, at, :].astype(F32)
        hm[0, to, :], hp[0, to, :], hm[1, to, :], hp[1, to, :] = normalise(
            xm, xp, dxm, dxp, gm, gp, 2 * half
        )
        return carry

    lax.fori_loop(0, rows // step, body, 0)


def ready_kernel(cfg, place, gm_ref, gp_ref, *refs):
    rows, tall, n_blocks, conv_rows, mix_rows, pairs = cfg
    wide, mix, hm, hp = refs[-4:]
    convs = refs[2 * n_blocks : -4]
    for src, dst in weight_moves(place, convs, conv_rows, mix_rows, pairs, wide, mix):
        dst[...] = src[...]
    for b in range(n_blocks):
        norm_rows(
            gm_ref[0:1, :],
            gp_ref[0:1, :],
            refs[b],
            refs[n_blocks + b],
            hm,
            hp,
            tall - (b + 1) * rows,
        )


def place_kernel(cfg, place, *refs):
    conv_rows, mix_rows, pairs = cfg
    wide, mix = refs[-2:]
    for src, dst in weight_moves(place, refs[:-2], conv_rows, mix_rows, pairs, wide, mix):
        dst[...] = src[...]


def conv_slabs(cfg, place, hm, hp, wide, z_ref, acc):
    rows, half, branch, slabs = cfg
    c = place[2]
    at_m = pl.multiple_of(c * half, half)
    at_p = pl.multiple_of((1 - c) * half, half)
    for begin, size, taps in slabs:
        for k, row in enumerate(taps):
            for v in range(2):
                part = jnp.dot(
                    hm[v, row : row + size, :],
                    wide[pl.ds(2 * half * k + at_m, half), :],
                    preferred_element_type=F32,
                ) + jnp.dot(
                    hp[v, row : row + size, :],
                    wide[pl.ds(2 * half * k + at_p, half), :],
                    preferred_element_type=F32,
                )
                if k == 0:
                    acc[v, 0:size, :] = part
                else:
                    acc[v, 0:size, :] += part
        for r in range(0, size, rows):
            gate_into(
                (
                    z_ref.at[0, begin + r : begin + r + rows, :],
                    z_ref.at[1, begin + r : begin + r + rows, :],
                ),
                acc[0, r : r + rows, :],
                acc[1, r : r + rows, :],
                branch,
            )


def conv0_near_kernel(cfg, weight_cfg, place, hm, hp, *refs):
    z_ref, wide, mix, acc = refs[-4:]
    if weight_cfg[2] is not None:
        for src, dst in weight_moves(place, refs[:-6], *weight_cfg, wide, mix):
            dst[...] = src[...]
    conv_slabs(cfg, place, hm, hp, wide, z_ref, acc)


def conv0_far_kernel(cfg, place, gm_ref, gp_ref, mine, theirs, wide, _, __, z_ref, hm, hp, acc):
    norm_rows(gm_ref[0:1, :], gp_ref[0:1, :], mine, theirs, hm, hp, 0)
    conv_slabs(cfg, place, hm, hp, wide, z_ref, acc)


def mix0_kernel(cfg, place, gm_ref, gp_ref, zma, zpa, zmb, zpb, mixm_ref, mixp_ref, *refs):
    rows, half, branch, layer = cfg
    mine = refs[:TAPS]
    theirs = refs[TAPS : 2 * TAPS]
    hm_ref, hp_ref, state_ref = refs[2 * TAPS :]
    c = place[2]
    at_m = pl.ds(pl.multiple_of(c * branch, branch), branch)
    at_p = pl.ds(pl.multiple_of((1 - c) * branch, branch), branch)
    gm = gm_ref[layer : layer + 1, :]
    gp = gp_ref[layer : layer + 1, :]
    step = min(256, rows)
    for j in range(TAPS):
        zm_ref, zp_ref, base = (zma, zpa, (1 - j) * rows) if j < 2 else (zmb, zpb, 0)

        def body(i, carry, j=j, base=base, zm_ref=zm_ref, zp_ref=zp_ref):
            at = pl.multiple_of(i * step, step)
            to = pl.multiple_of(base + i * step, step)
            new = []
            for v in range(2):
                zm = zm_ref[v, pl.ds(to, step), :]
                zp = zp_ref[v, pl.ds(to, step), :]
                for x_ref, mix in ((mine[j], mixm_ref), (theirs[j], mixp_ref)):
                    y = jnp.dot(zm, mix[at_m, :], preferred_element_type=F32)
                    y = y + jnp.dot(zp, mix[at_p, :], preferred_element_type=F32)
                    new.append((x_ref[v, pl.ds(at, step), :].astype(F32) + y).astype(BF16))
            if j == 0:
                state_ref[0, pl.ds(at, step), :] = new[0]
                state_ref[1, pl.ds(at, step), :] = new[2]
            xm, xp, dxm, dxp = (t.astype(F32) for t in new)
            a, b, d, e = normalise(xm, xp, dxm, dxp, gm, gp, 2 * half)
            hm_ref[j, 0, pl.ds(at, step), :] = a
            hp_ref[j, 0, pl.ds(at, step), :] = b
            hm_ref[j, 1, pl.ds(at, step), :] = d
            hp_ref[j, 1, pl.ds(at, step), :] = e
            return carry

        lax.fori_loop(0, rows // step, body, 0)


def conv1_kernel(cfg, place, hm, hp, wide, z_ref, acc):
    rows, half, branch = cfg
    c = place[2]
    at_m = pl.multiple_of(c * half, half)
    at_p = pl.multiple_of((1 - c) * half, half)
    for k in range(TAPS):
        part = jnp.dot(
            hm[k].reshape(2 * rows, half),
            wide[pl.ds(2 * half * k + at_m, half), :],
            preferred_element_type=F32,
        ) + jnp.dot(
            hp[k].reshape(2 * rows, half),
            wide[pl.ds(2 * half * k + at_p, half), :],
            preferred_element_type=F32,
        )
        if k == 0:
            acc[...] = part
        else:
            acc[...] += part
    gate_into((z_ref.at[0], z_ref.at[1]), acc[0:rows, :], acc[rows : 2 * rows, :], branch)


def mix1_kernel(cfg, place, zm_ref, zp_ref, mix_ref, state_ref, out_ref, dout_ref):
    (branch,) = cfg
    c = place[2]
    at_m = pl.ds(pl.multiple_of(c * branch, branch), branch)
    at_p = pl.ds(pl.multiple_of((1 - c) * branch, branch), branch)
    for v, out in ((0, out_ref), (1, dout_ref)):
        y = jnp.dot(zm_ref[v], mix_ref[at_m, :], preferred_element_type=F32)
        y = y + jnp.dot(zp_ref[v], mix_ref[at_p, :], preferred_element_type=F32)
        out[...] = (state_ref[v].astype(F32) + y).astype(BF16)


def pack(seq, place, *buffers):
    arrays = []

    def index(array):
        for i, known in enumerate(arrays):
            if known is array:
                return i
        arrays.append(array)
        return len(arrays) - 1

    plan = []
    for buffer in buffers:
        parts = []
        for array, begin, count, *mark in buffer:
            planes, even = (mark + [None, None])[:2] if mark else (None, None)
            parts.append(
                (index(array), begin, count, planes, None if even is None else index(even))
            )
        plan.append(parts)
    width = arrays[0].shape[-1]

    def kernel(place_ref, *refs):
        s = place_ref[0]
        for out, parts in zip(refs[len(arrays) :], plan):
            to = 0
            for i, begin, count, planes, even in parts:
                value = refs[i][begin : begin + count, :]
                if planes is not None:
                    value = jnp.where(s < max(2 * planes, 1), jnp.zeros_like(value), value)
                if even is not None:
                    value = jnp.where(lax.rem(s, 2) == 1, value, refs[even][...])
                out[to : to + count, :] = value
                to += count

    return pl.pallas_call(
        kernel,
        out_shape=tuple(near_out(sum(part[2] for part in buf), width) for buf in buffers),
        in_specs=[SMEM] + [VMEM] * len(arrays),
        out_specs=(VMEM,) * len(buffers),
        compiler_params=scoped(4),
        name="pack",
    )(place, *[near(array) for array in arrays])


def exchange(place, own, chunks, gains, seq, ready, newest):
    both = chunks
    unit = both.shape[0] // 2
    tall = own.shape[0]
    pieces = ([], [])
    order = ([], [])

    def keep(layer, array, *slots):
        for begin, skip, count, k, dx, dy in slots:
            order[layer].append((len(pieces[layer]), begin, skip, count, 2 * k, dx, dy))
        pieces[layer].append(array)

    def whole(layer, array, *slots):
        keep(layer, array, *[(i * unit, 0, unit, *slot) for i, slot in enumerate(slots)])

    def together(*blocks):
        return lax.optimization_barrier(blocks)

    def x(block):
        return swap_pair(block, seq)

    def y(block):
        return swap_groups(block)

    def z(block, by=1):
        return ring(block, seq, 2 * by)

    c0, c1 = both[:unit], both[unit:]
    whole(0, both, (0, 0, 0))
    keep(1, both, (unit, 0, unit, 0, 0, 0))
    z1a, z1b, x1, y1, own, c1 = together(z(c0), z(c0, 3), x(both), y(both), own, c1)
    whole(0, z1a, (1, 0, 0))
    whole(0, z1b, (3, 0, 0))
    whole(0, x1, (0, 1, 0))
    keep(1, x1, (unit, 0, unit, 0, 1, 0))
    whole(0, y1, (0, 0, 1))
    keep(1, y1, (unit, 0, unit, 0, 0, 1))
    to_z, to_x, to_y = pack(
        seq,
        place,
        [(z1a, 0, unit), (own, 0, tall)],
        [(z1a, 0, unit), (z1b, 0, unit), (y1, unit, unit)],
        [(z1a, 0, unit), (z1b, 0, unit), (x1, 0, unit)],
    )
    z2, x2, y2, own, c1, gains_p = together(z(to_z), x(to_x), y(to_y), own, c1, swap_chan(gains))
    keep(0, z2, (0, 0, unit, 2, 0, 0))
    whole(0, x2, (1, 1, 0), (3, 1, 0))
    keep(1, x2, (2 * unit, 0, unit, 0, 1, 1))
    whole(0, y2, (1, 0, 1), (3, 0, 1), (0, 1, 1))
    to_z, to_x, to_y, two = pack(
        seq,
        place,
        [(both, unit, unit), (x2, 2 * unit, unit)],
        [(z2, 0, unit), (z2, unit, tall, 1, own)],
        [(z2, 0, unit), (x2, 0, 2 * unit)],
        [(z2, unit, tall, 1)],
    )
    z3a, z3b, x3, y3 = together(z(to_z), z(c1, 3), x(to_x), y(to_y))
    whole(1, z3a, (1, 0, 0), (1, 1, 1))
    whole(1, z3b, (3, 0, 0))
    keep(0, x3, (0, 0, unit, 2, 1, 0))
    whole(0, y3, (2, 0, 1), (1, 1, 1), (3, 1, 1))
    cut = unit // 2
    to_z, to_x, w_x, w_y, one = pack(
        seq,
        place,
        [(z3a, 0, unit), (x3, unit, tall, 0)],
        [(z3a, 0, unit), (z3b, 0, unit)],
        [(y3, 0, cut)],
        [(x3, cut, unit - cut)],
        [(x3, unit, tall, 0)],
    )
    first = ready(gains_p, (own, one, two), pieces[0], (seq, tuple(order[0])))
    pieces[0].clear()
    order[0].clear()
    x4a, y4a = x(w_x), y(w_y)
    keep(0, x4a, (0, 0, cut, 2, 1, 1))
    keep(0, y4a, (0, cut, unit - cut, 2, 1, 1))
    made = newest(first, pieces[0], (seq, tuple(order[0])))
    to_x = together(to_x, x4a, y4a)[0]
    z4, x4, y4, made = together(z(to_z), x(to_x), y(to_x), made)
    keep(1, z4, (0, 0, unit, 2, 0, 0))
    whole(1, x4, (1, 1, 0), (3, 1, 0))
    whole(1, y4, (1, 0, 1), (3, 0, 1))
    to_z, to_x, to_y, three = pack(
        seq,
        place,
        [(z3a, cut, 2 * unit - cut)],
        [(z4, 0, unit), (y4, unit, cut)],
        [(z4, 0, unit), (x4, unit + cut, unit - cut)],
        [(z4, unit, tall, 1)],
    )
    x5, y5, z5 = x(to_x), y(to_y), z(to_z)
    keep(1, z5, (unit - cut, 0, unit, 2, 1, 1))
    keep(1, x5, (0, 0, unit, 2, 1, 0), (unit, 0, cut, 3, 1, 1))
    keep(1, y5, (0, 0, unit, 2, 0, 1), (unit, cut, unit - cut, 3, 1, 1))
    return gains_p, (one, two, three), made, (x5, y5, z5), pieces[1], (seq, tuple(order[1]))


def on_device(signal, tangent, gains, convolution_kernel, mixing_kernel):
    rows, half = signal.shape
    seq = lax.axis_size("seq")
    layers = gains.shape[0]
    branch = convolution_kernel.shape[3]
    shard = convolution_kernel.shape[1]
    mix_shard = mixing_kernel.shape[1]
    lag = rows * seq // 16
    place = jnp.stack([lax.axis_index("seq"), lax.axis_index("groups"), lax.axis_index("chan")])
    place = place.astype(jnp.int32)
    wide_rows, mix_whole = shard * seq, mix_shard * seq

    own = jnp.stack([signal, tangent], 0)
    if 2 * lag == rows:
        conv_rows, mix_rows = shard // 2, mix_shard // 2
        g = lax.axis_index("groups")
        chunks = jnp.concatenate(
            [
                lax.dynamic_slice_in_dim(
                    convolution_kernel, g * conv_rows, conv_rows, 1
                ).reshape(layers, conv_rows, 2 * branch),
                lax.dynamic_slice_in_dim(mixing_kernel, g * mix_rows, mix_rows, 1),
            ],
            1,
        ).reshape(layers * (conv_rows + mix_rows), 2 * branch)
        step, used = lag, (0, 1, 2)
        blocks = 4
    else:
        conv_rows, mix_rows = shard, mix_shard
        conv_local = convolution_kernel.reshape(layers, shard, 2 * branch)
        weights = [
            [
                lax.all_gather(conv_local[l], "seq", axis=0, tiled=True),
                lax.all_gather(mixing_kernel[l], "seq", axis=0, tiled=True),
            ]
            for l in range(layers)
        ]
        step, used = rows, (0, 2, 4)
        blocks = 7
    tall = blocks * rows
    starts = tuple(tall - rows - m * step for m in range(7))
    if 2 * lag == rows:
        slabs = ((0, 2 * rows, tuple(starts[2 + k] for k in range(TAPS))),)
    else:
        slabs = tuple(
            ((1 - j) * rows, rows, tuple(starts[2 * j + k] for k in range(TAPS))) for j in range(2)
        )
    far_slabs = ((0, rows, tuple(starts[4 + k] for k in range(TAPS))),)

    mine, theirs = [], []

    def ready(gains_p, halo, pieces, pairs):
        for block in halo:
            mine.append(block.reshape(own.shape))
            theirs.append(swap_chan(mine[-1]))
        cfg = (rows, tall, len(halo), conv_rows, mix_rows, pairs)
        return pl.pallas_call(
            functools.partial(ready_kernel, cfg),
            out_shape=(
                near_out(wide_rows, 2 * branch),
                near_out(mix_whole, half),
                near_out(2, tall, half),
                near_out(2, tall, half),
            ),
            in_specs=[SMEM] + [VMEM] * (2 + 2 * len(halo) + len(pieces)),
            out_specs=(VMEM,) * 4,
            compiler_params=scoped(4),
            cost_estimate=cost(0, 2**16),
            name="ready",
        )(
            place,
            near(gains),
            near(gains_p),
            *[near(block) for block in (*mine, *theirs)],
            *[near(piece) for piece in pieces],
        )

    def newest(made, pieces, pairs):
        wide, mix, hm, hp = made
        n_in = 3 + len(pieces)
        z, wide, mix = pl.pallas_call(
            functools.partial(
                conv0_near_kernel, (rows, half, branch, slabs), (conv_rows, mix_rows, pairs)
            ),
            out_shape=(
                near_out(2, 2 * rows, branch),
                near_out(wide_rows, 2 * branch),
                near_out(mix_whole, half),
            ),
            in_specs=[SMEM] + [VMEM] * (n_in + 1),
            out_specs=(VMEM,) * 3,
            input_output_aliases={n_in: 1, n_in + 1: 2},
            scratch_shapes=[pltpu.VMEM((2, slabs[0][1], 2 * branch), F32)],
            compiler_params=scoped(12),
            cost_estimate=cost(0, 2**16),
            name="conv0_near",
        )(place, hm, hp, *[near(piece) for piece in pieces], wide, mix)
        return z, mix, wide, hm, hp

    if 2 * lag == rows:
        flat = own.reshape(2 * rows, half)
        gains_p, halo, made, beside, weights1, pairs1 = exchange(
            place, flat, chunks, gains, seq, ready, newest
        )
        last = halo[-1].reshape(own.shape)
    else:
        gains_p = swap_chan(gains)
        halo = [from_behind(own, seq, k * (lag // rows)) for k in range(1, 7)]
        made = newest(ready(gains_p, (own, *halo[:-1]), weights[0], None), [], None)
        last, beside, weights1, pairs1 = halo[-1], (), weights[1], None
    za_mine, mix_mine, wide, hm, hp = made
    last_theirs, za_theirs, mix_theirs = lax.optimization_barrier(
        (swap_chan(last), swap_chan(za_mine), swap_chan(mix_mine))
    )

    z_mine = pl.pallas_call(
        functools.partial(conv0_far_kernel, (rows, half, branch, far_slabs)),
        out_shape=(
            near_out(2, rows, branch),
            near_out(2, tall, half),
            near_out(2, tall, half),
        ),
        in_specs=[SMEM] + [VMEM] * 7,
        out_specs=(VMEM,) * 3,
        input_output_aliases={6: 1, 7: 2},
        scratch_shapes=[pltpu.VMEM((2, rows, 2 * branch), F32)],
        compiler_params=scoped(8),
        cost_estimate=cost(0, 2**16),
        name="conv0_far",
    )(place, near(gains), near(gains_p), near(last), near(last_theirs), wide, hm, hp)[0]
    z_theirs = swap_chan(z_mine)
    hm, hp, state = pl.pallas_call(
        functools.partial(mix0_kernel, (rows, half, branch, 1)),
        out_shape=(
            near_out(TAPS, 2, rows, half),
            near_out(TAPS, 2, rows, half),
            near_out(2, rows, half),
        ),
        in_specs=[SMEM] + [VMEM] * (8 + 2 * TAPS),
        out_specs=(VMEM, VMEM, VMEM),
        compiler_params=scoped(6),
        cost_estimate=cost(0, 2**16),
        name="mix0",
    )(
        place,
        near(gains),
        near(gains_p),
        near(za_mine),
        near(za_theirs),
        z_mine,
        near(z_theirs),
        near(mix_mine),
        near(mix_theirs),
        *[near(mine[b]) for b in used],
        *[near(theirs[b]) for b in used],
    )
    hm, hp, *weights1 = lax.optimization_barrier((hm, hp, *weights1))
    placed = pl.pallas_call(
        functools.partial(place_kernel, (conv_rows, mix_rows, pairs1)),
        out_shape=(near_out(wide_rows, 2 * branch), near_out(mix_whole, half)),
        in_specs=[SMEM] + [VMEM] * len(weights1),
        out_specs=(VMEM, VMEM),
        compiler_params=scoped(2),
        name="place",
    )(place, *[near(w) for w in weights1])
    wide, mix_last = placed
    z_mine = pl.pallas_call(
        functools.partial(conv1_kernel, (rows, half, branch)),
        out_shape=near_out(2, rows, branch),
        in_specs=[SMEM] + [VMEM] * 3,
        out_specs=VMEM,
        scratch_shapes=[pltpu.VMEM((2 * rows, 2 * branch), F32)],
        compiler_params=scoped(8),
        name="conv1",
    )(place, hm, hp, wide)
    z_theirs = swap_chan(z_mine)
    return pl.pallas_call(
        functools.partial(mix1_kernel, (branch,)),
        out_shape=(
            jax.ShapeDtypeStruct((rows, half), BF16),
            jax.ShapeDtypeStruct((rows, half), BF16),
        ),
        in_specs=[SMEM] + [VMEM] * 4,
        out_specs=(VMEM, VMEM),
        compiler_params=scoped(4),
        name="mix1",
    )(place, z_mine, near(z_theirs), mix_last, state)


def solution(mesh):
    return jax.shard_map(
        on_device,
        mesh=mesh,
        in_specs=(
            P(("groups", "seq"), "chan"),
            P(("groups", "seq"), "chan"),
            P(None, "chan"),
            P(None, "seq", None, "chan"),
            P(None, "seq", "chan"),
        ),
        out_specs=(P(("groups", "seq"), "chan"), P(("groups", "seq"), "chan")),
        check_vma=False,
    )
```

```python
import functools

import jax
import jax.numpy as jnp
from jax import lax
from jax.experimental import pallas as pl
from jax.experimental.pallas import tpu as pltpu
from jax.sharding import PartitionSpec as P

TAPS = 3
EPS = 1e-05
F32 = jnp.float32
BF16 = jnp.bfloat16
VMEM = pl.BlockSpec(memory_space=pltpu.VMEM)
SMEM = pl.BlockSpec(memory_space=pltpu.SMEM)
ANY = pl.BlockSpec(memory_space=pltpu.HBM)


def scoped(mebibytes):
    return pltpu.CompilerParams(vmem_limit_bytes=mebibytes * 2**20)


def near(block):
    return pltpu.with_memory_space_constraint(block, pltpu.VMEM)


def far(block):
    return pltpu.with_memory_space_constraint(block, pltpu.HBM)


def near_out(*shape):
    return pltpu.VMEM(shape, BF16)


def cost(flops, bytes_moved):
    return pl.CostEstimate(flops=flops, bytes_accessed=bytes_moved, transcendentals=0)


def swap_chan(block):
    return lax.ppermute(block, "chan", [(0, 1), (1, 0)])


def swap_groups(block):
    return lax.ppermute(block, "groups", [(0, 1), (1, 0)])


def swap_pair(block, seq):
    return lax.ppermute(block, "seq", [(s, s ^ 1) for s in range(seq)])


def ring(block, seq, by):
    return lax.ppermute(block, "seq", [(s, (s + by) % seq) for s in range(seq)])


def from_behind(block, seq, by):
    return lax.ppermute(block, "seq", [(s - by, s) for s in range(by, seq)])


def weight_moves(place, refs, conv_rows, mix_rows, pairs, wide, mix):
    if pairs is None:
        return [(refs[0], wide), (refs[1], mix)]
    s, g = place[0], place[1]
    seq, order = pairs
    moves = []
    for index, begin, skip, count, by, dx, dy in order:
        owner = lax.rem(s + (seq - by), seq)
        if dx:
            owner = owner + 1 - 2 * lax.rem(owner, 2)
        half = (1 - g) if dy else g
        unit = owner * 2 + half
        n_conv = min(conv_rows - skip, count)
        if wide is not None:
            to = pl.multiple_of(unit * conv_rows + skip, 16)
            moves.append((refs[index].at[pl.ds(begin, n_conv)], wide.at[pl.ds(to, n_conv)]))
        if count > n_conv and mix is not None:
            to = pl.multiple_of(unit * mix_rows, 16)
            moves.append(
                (refs[index].at[pl.ds(begin + n_conv, mix_rows)], mix.at[pl.ds(to, mix_rows)])
            )
    return moves


def normalise(xm, xp, dxm, dxp, gm, gp, width):
    total = jnp.sum(xm * xm, axis=1, keepdims=True) + jnp.sum(xp * xp, axis=1, keepdims=True)
    cross = jnp.sum(xm * dxm, axis=1, keepdims=True) + jnp.sum(xp * dxp, axis=1, keepdims=True)
    scale = lax.rsqrt(total / width + EPS)
    factor = scale * scale * scale * (cross / width)
    return (
        (gm * xm * scale).astype(BF16),
        (gp * xp * scale).astype(BF16),
        (gm * (dxm * scale - xm * factor)).astype(BF16),
        (gp * (dxp * scale - xp * factor)).astype(BF16),
    )


def gate_into(out, full, dfull, branch):
    tanh_f = jnp.tanh(full[:, :branch])
    sig_g = jax.nn.sigmoid(full[:, branch:])
    out[0][...] = (tanh_f * sig_g).astype(BF16)
    out[1][...] = (
        (1.0 - tanh_f * tanh_f) * sig_g * dfull[:, :branch]
        + tanh_f * sig_g * (1.0 - sig_g) * dfull[:, branch:]
    ).astype(BF16)


def norm_rows(gm, gp, mine, theirs, hm, hp, base):
    rows, half = mine.shape[1:]
    step = 64

    def body(i, carry):
        at = pl.ds(pl.multiple_of(i * step, step), step)
        to = pl.ds(pl.multiple_of(base + i * step, step), step)
        xm = mine[0, at, :].astype(F32)
        dxm = mine[1, at, :].astype(F32)
        xp = theirs[0, at, :].astype(F32)
        dxp = theirs[1, at, :].astype(F32)
        hm[0, to, :], hp[0, to, :], hm[1, to, :], hp[1, to, :] = normalise(
            xm, xp, dxm, dxp, gm, gp, 2 * half
        )
        return carry

    lax.fori_loop(0, rows // step, body, 0)


def ready_kernel(cfg, place, gm_ref, gp_ref, *refs):
    rows, tall, n_blocks, conv_rows, mix_rows, pairs = cfg
    wide, mix, hm, hp = refs[-4:]
    convs = refs[2 * n_blocks : -4]
    for src, dst in weight_moves(place, convs, conv_rows, mix_rows, pairs, wide, mix):
        dst[...] = src[...]
    for b in range(n_blocks):
        norm_rows(
            gm_ref[0:1, :],
            gp_ref[0:1, :],
            refs[b],
            refs[n_blocks + b],
            hm,
            hp,
            tall - (b + 1) * rows,
        )


def place_kernel(cfg, place, *refs):
    conv_rows, mix_rows, pairs = cfg
    wide, mix = refs[-2:]
    for src, dst in weight_moves(place, refs[:-2], conv_rows, mix_rows, pairs, wide, mix):
        dst[...] = src[...]


def conv_slabs(cfg, place, hm, hp, wide, z_refs, acc):
    rows, half, branch, slabs = cfg
    c = place[2]
    at_m = pl.multiple_of(c * half, half)
    at_p = pl.multiple_of((1 - c) * half, half)
    for begin, size, taps in slabs:
        for k, row in enumerate(taps):
            for v in range(2):
                part = jnp.dot(
                    hm[v, row : row + size, :],
                    wide[pl.ds(2 * half * k + at_m, half), :],
                    preferred_element_type=F32,
                ) + jnp.dot(
                    hp[v, row : row + size, :],
                    wide[pl.ds(2 * half * k + at_p, half), :],
                    preferred_element_type=F32,
                )
                if k == 0:
                    acc[v, 0:size, :] = part
                else:
                    acc[v, 0:size, :] += part
        for r in range(0, size, rows):
            gate_into(
                [z_ref.at[begin + r : begin + r + rows, :] for z_ref in z_refs],
                acc[0, r : r + rows, :],
                acc[1, r : r + rows, :],
                branch,
            )


def conv0_near_kernel(cfg, weight_cfg, place, hm, hp, *refs):
    z_ref, wide, mix, acc = refs[-4:]
    if weight_cfg[2] is not None:
        for src, dst in weight_moves(place, refs[:-6], *weight_cfg, wide, mix):
            dst[...] = src[...]
    conv_slabs(cfg, place, hm, hp, wide, (z_ref.at[0], z_ref.at[1]), acc)


def conv0_far_kernel(cfg, place, gm_ref, gp_ref, mine, theirs, wide, _, __, *refs):
    z_ref, dz_ref, hm, hp, acc = refs
    norm_rows(gm_ref[0:1, :], gp_ref[0:1, :], mine, theirs, hm, hp, 0)
    conv_slabs(cfg, place, hm, hp, wide, (z_ref, dz_ref), acc)


def mix0_kernel(cfg, place, gm_ref, gp_ref, mixm_ref, mixp_ref, *refs):
    rows, half, branch, layer, count, n_z = cfg
    if n_z == 1:
        zm_refs, zp_refs = ([ref.at[0], ref.at[1]] for ref in refs[:2])
    else:
        zm_refs, zp_refs = refs[:2], refs[2:4]
    refs = refs[2 * n_z :]
    mine, theirs = refs[:count], refs[count : 2 * count]
    hm_ref, hp_ref, *state_refs = refs[2 * count :]
    c = place[2]
    at_m = pl.ds(pl.multiple_of(c * branch, branch), branch)
    at_p = pl.ds(pl.multiple_of((1 - c) * branch, branch), branch)
    gm = gm_ref[layer : layer + 1, :]
    gp = gp_ref[layer : layer + 1, :]
    for j in range(count):
        at = slice((count - 1 - j) * rows, (count - j) * rows)
        new = []
        for v in range(2):
            zm = zm_refs[v][at, :]
            zp = zp_refs[v][at, :]
            for x_ref, mix in ((mine[j], mixm_ref), (theirs[j], mixp_ref)):
                y = jnp.dot(zm, mix[at_m, :], preferred_element_type=F32)
                y = y + jnp.dot(zp, mix[at_p, :], preferred_element_type=F32)
                new.append((x_ref[v].astype(F32) + y).astype(BF16))
        if j == 0 and state_refs:
            state_refs[0][0] = new[0]
            state_refs[0][1] = new[2]
        xm, xp, dxm, dxp = (t.astype(F32) for t in new)
        hm_ref[j, 0], hp_ref[j, 0], hm_ref[j, 1], hp_ref[j, 1] = normalise(
            xm, xp, dxm, dxp, gm, gp, 2 * half
        )


def conv1_kernel(cfg, place, hm_near, hp_near, hm_far, hp_far, wide, z_ref, acc):
    rows, half, branch = cfg
    c = place[2]
    at_m = pl.multiple_of(c * half, half)
    at_p = pl.multiple_of((1 - c) * half, half)
    for k in range(TAPS):
        part = jnp.dot(
            (hm_near[k] if k < 2 else hm_far[0]).reshape(2 * rows, half),
            wide[pl.ds(2 * half * k + at_m, half), :],
            preferred_element_type=F32,
        ) + jnp.dot(
            (hp_near[k] if k < 2 else hp_far[0]).reshape(2 * rows, half),
            wide[pl.ds(2 * half * k + at_p, half), :],
            preferred_element_type=F32,
        )
        if k == 0:
            acc[...] = part
        else:
            acc[...] += part
    gate_into((z_ref.at[0], z_ref.at[1]), acc[0:rows, :], acc[rows : 2 * rows, :], branch)


def mix1_kernel(cfg, place, zm_ref, zp_ref, mix_ref, state_ref, out_ref, dout_ref):
    (branch,) = cfg
    c = place[2]
    at_m = pl.ds(pl.multiple_of(c * branch, branch), branch)
    at_p = pl.ds(pl.multiple_of((1 - c) * branch, branch), branch)
    for v, out in ((0, out_ref), (1, dout_ref)):
        y = jnp.dot(zm_ref[v], mix_ref[at_m, :], preferred_element_type=F32)
        y = y + jnp.dot(zp_ref[v], mix_ref[at_p, :], preferred_element_type=F32)
        out[...] = (state_ref[v].astype(F32) + y).astype(BF16)


def pack(seq, place, *buffers):
    arrays = []

    def index(array):
        for i, known in enumerate(arrays):
            if known is array:
                return i
        arrays.append(array)
        return len(arrays) - 1

    plan = []
    for buffer in buffers:
        parts = []
        for array, begin, count, *mark in buffer:
            planes, even = (mark + [None, None])[:2] if mark else (None, None)
            parts.append(
                (index(array), begin, count, planes, None if even is None else index(even))
            )
        plan.append(parts)
    width = arrays[0].shape[-1]

    def kernel(place_ref, *refs):
        s = place_ref[0]
        for out, parts in zip(refs[len(arrays) :], plan):
            to = 0
            for i, begin, count, planes, even in parts:
                value = refs[i][begin : begin + count, :]
                if planes is not None:
                    value = jnp.where(s < max(2 * planes, 1), jnp.zeros_like(value), value)
                if even is not None:
                    value = jnp.where(lax.rem(s, 2) == 1, value, refs[even][...])
                out[to : to + count, :] = value
                to += count

    return pl.pallas_call(
        kernel,
        out_shape=tuple(near_out(sum(part[2] for part in buf), width) for buf in buffers),
        in_specs=[SMEM] + [VMEM] * len(arrays),
        out_specs=(VMEM,) * len(buffers),
        compiler_params=scoped(4),
        name="pack",
    )(place, *[near(array) for array in arrays])


def exchange(place, own, chunks, gains, seq, ready, newest):
    both = chunks
    unit = both.shape[0] // 2
    tall = own.shape[0]
    pieces = ([], [])
    order = ([], [])

    def keep(layer, array, *slots):
        for begin, skip, count, k, dx, dy in slots:
            order[layer].append((len(pieces[layer]), begin, skip, count, 2 * k, dx, dy))
        pieces[layer].append(array)

    def whole(layer, array, *slots):
        keep(layer, array, *[(i * unit, 0, unit, *slot) for i, slot in enumerate(slots)])

    def together(*blocks):
        return lax.optimization_barrier(blocks)

    def x(block):
        return swap_pair(block, seq)

    def y(block):
        return swap_groups(block)

    def z(block, by=1):
        return ring(block, seq, 2 * by)

    c0, c1 = both[:unit], both[unit:]
    whole(0, both, (0, 0, 0))
    keep(1, both, (unit, 0, unit, 0, 0, 0))
    z1a, z1b, x1, y1, own, c1 = together(z(c0), z(c0, 3), x(both), y(both), own, c1)
    whole(0, z1a, (1, 0, 0))
    whole(0, z1b, (3, 0, 0))
    whole(0, x1, (0, 1, 0))
    keep(1, x1, (unit, 0, unit, 0, 1, 0))
    whole(0, y1, (0, 0, 1))
    keep(1, y1, (unit, 0, unit, 0, 0, 1))
    to_z, to_x, to_y = pack(
        seq,
        place,
        [(z1a, 0, unit), (own, 0, tall)],
        [(z1a, 0, unit), (z1b, 0, unit), (y1, unit, unit)],
        [(z1a, 0, unit), (z1b, 0, unit), (x1, 0, unit)],
    )
    z2, x2, y2, own, c1, gains_p = together(z(to_z), x(to_x), y(to_y), own, c1, swap_chan(gains))
    keep(0, z2, (0, 0, unit, 2, 0, 0))
    whole(0, x2, (1, 1, 0), (3, 1, 0))
    keep(1, x2, (2 * unit, 0, unit, 0, 1, 1))
    whole(0, y2, (1, 0, 1), (3, 0, 1), (0, 1, 1))
    to_z, to_x, to_y, two = pack(
        seq,
        place,
        [(both, unit, unit), (x2, 2 * unit, unit)],
        [(z2, 0, unit), (z2, unit, tall, 1, own)],
        [(z2, 0, unit), (x2, 0, 2 * unit)],
        [(z2, unit, tall, 1)],
    )
    z3a, z3b, x3, y3 = together(z(to_z), z(c1, 3), x(to_x), y(to_y))
    whole(1, z3a, (1, 0, 0), (1, 1, 1))
    whole(1, z3b, (3, 0, 0))
    keep(0, x3, (0, 0, unit, 2, 1, 0))
    whole(0, y3, (2, 0, 1), (1, 1, 1), (3, 1, 1))
    cut = unit // 2
    to_z, to_x, w_x, w_y, one = pack(
        seq,
        place,
        [(z3a, 0, unit), (x3, unit, tall, 0)],
        [(z3a, 0, unit), (z3b, 0, unit)],
        [(y3, 0, cut)],
        [(x3, cut, unit - cut)],
        [(x3, unit, tall, 0)],
    )
    first = ready(gains_p, (own, one, two), pieces[0], (seq, tuple(order[0])))
    pieces[0].clear()
    order[0].clear()
    x4a, y4a = x(w_x), y(w_y)
    keep(0, x4a, (0, 0, cut, 2, 1, 1))
    keep(0, y4a, (0, cut, unit - cut, 2, 1, 1))
    made = newest(first, pieces[0], (seq, tuple(order[0])))
    to_x = together(to_x, x4a, y4a)[0]
    z4, x4, y4, made = together(z(to_z), x(to_x), y(to_x), made)
    keep(1, z4, (0, 0, unit, 2, 0, 0))
    whole(1, x4, (1, 1, 0), (3, 1, 0))
    whole(1, y4, (1, 0, 1), (3, 0, 1))
    to_z, to_x, to_y, three = pack(
        seq,
        place,
        [(z3a, unit, unit)],
        [(z4, 0, unit), (y4, unit, cut)],
        [(z4, 0, unit), (x4, unit + cut, unit - cut)],
        [(z4, unit, tall, 1)],
    )
    x5, y5, z5 = x(to_x), y(to_y), z(to_z)
    whole(1, z5, (2, 1, 1))
    keep(1, x5, (0, 0, unit, 2, 1, 0), (unit, 0, cut, 3, 1, 1))
    keep(1, y5, (0, 0, unit, 2, 0, 1), (unit, cut, unit - cut, 3, 1, 1))
    return gains_p, (one, two, three), made, (x5, y5, z5), pieces[1], (seq, tuple(order[1]))


def on_device(signal, tangent, gains, convolution_kernel, mixing_kernel):
    rows, half = signal.shape
    seq = lax.axis_size("seq")
    layers = gains.shape[0]
    branch = convolution_kernel.shape[3]
    shard = convolution_kernel.shape[1]
    mix_shard = mixing_kernel.shape[1]
    lag = rows * seq // 16
    place = jnp.stack([lax.axis_index("seq"), lax.axis_index("groups"), lax.axis_index("chan")])
    place = place.astype(jnp.int32)
    wide_rows, mix_whole = shard * seq, mix_shard * seq

    own = jnp.stack([signal, tangent], 0)
    if 2 * lag == rows:
        conv_rows, mix_rows = shard // 2, mix_shard // 2
        g = lax.axis_index("groups")
        chunks = jnp.concatenate(
            [
                lax.dynamic_slice_in_dim(
                    convolution_kernel, g * conv_rows, conv_rows, 1
                ).reshape(layers, conv_rows, 2 * branch),
                lax.dynamic_slice_in_dim(mixing_kernel, g * mix_rows, mix_rows, 1),
            ],
            1,
        ).reshape(layers * (conv_rows + mix_rows), 2 * branch)
        step, used = lag, (0, 1, 2)
        blocks = 4
    else:
        conv_rows, mix_rows = shard, mix_shard
        conv_local = convolution_kernel.reshape(layers, shard, 2 * branch)
        weights = [
            [
                lax.all_gather(conv_local[l], "seq", axis=0, tiled=True),
                lax.all_gather(mixing_kernel[l], "seq", axis=0, tiled=True),
            ]
            for l in range(layers)
        ]
        step, used = rows, (0, 2, 4)
        blocks = 7
    tall = blocks * rows
    starts = tuple(tall - rows - m * step for m in range(7))
    if 2 * lag == rows:
        slabs = ((0, 2 * rows, tuple(starts[2 + k] for k in range(TAPS))),)
    else:
        slabs = tuple(
            ((1 - j) * rows, rows, tuple(starts[2 * j + k] for k in range(TAPS))) for j in range(2)
        )
    far_slabs = ((0, rows, tuple(starts[4 + k] for k in range(TAPS))),)

    mine, theirs = [], []

    def ready(gains_p, halo, pieces, pairs):
        for block in halo:
            mine.append(block.reshape(own.shape))
            theirs.append(swap_chan(mine[-1]))
        cfg = (rows, tall, len(halo), conv_rows, mix_rows, pairs)
        return pl.pallas_call(
            functools.partial(ready_kernel, cfg),
            out_shape=(
                near_out(wide_rows, 2 * branch),
                near_out(mix_whole, half),
                near_out(2, tall, half),
                near_out(2, tall, half),
            ),
            in_specs=[SMEM] + [VMEM] * (2 + 2 * len(halo) + len(pieces)),
            out_specs=(VMEM,) * 4,
            compiler_params=scoped(4),
            cost_estimate=cost(0, 2**16),
            name="ready",
        )(
            place,
            near(gains),
            near(gains_p),
            *[near(block) for block in (*mine, *theirs)],
            *[near(piece) for piece in pieces],
        )

    def newest(made, pieces, pairs):
        wide, mix, hm, hp = made
        n_in = 3 + len(pieces)
        z, wide, mix = pl.pallas_call(
            functools.partial(
                conv0_near_kernel, (rows, half, branch, slabs), (conv_rows, mix_rows, pairs)
            ),
            out_shape=(
                near_out(2, 2 * rows, branch),
                near_out(wide_rows, 2 * branch),
                near_out(mix_whole, half),
            ),
            in_specs=[SMEM] + [VMEM] * (n_in + 1),
            out_specs=(VMEM,) * 3,
            input_output_aliases={n_in: 1, n_in + 1: 2},
            scratch_shapes=[pltpu.VMEM((2, slabs[0][1], 2 * branch), F32)],
            compiler_params=scoped(12),
            cost_estimate=cost(0, 2**16),
            name="conv0_near",
        )(place, hm, hp, *[near(piece) for piece in pieces], wide, mix)
        return z, mix, wide, hm, hp

    if 2 * lag == rows:
        flat = own.reshape(2 * rows, half)
        gains_p, halo, made, beside, weights1, pairs1 = exchange(
            place, flat, chunks, gains, seq, ready, newest
        )
        last = halo[-1].reshape(own.shape)
    else:
        gains_p = swap_chan(gains)
        halo = [from_behind(own, seq, k * (lag // rows)) for k in range(1, 7)]
        made = newest(ready(gains_p, (own, *halo[:-1]), weights[0], None), [], None)
        last, beside, weights1, pairs1 = halo[-1], (), weights[1], None
    za_mine, mix_mine, wide, hm, hp = made
    last_theirs, za_theirs, mix_theirs = lax.optimization_barrier(
        (swap_chan(last), swap_chan(za_mine), swap_chan(mix_mine))
    )

    z = pl.pallas_call(
        functools.partial(conv0_far_kernel, (rows, half, branch, far_slabs)),
        out_shape=(
            near_out(rows, branch),
            near_out(rows, branch),
            near_out(2, tall, half),
            near_out(2, tall, half),
        ),
        in_specs=[SMEM] + [VMEM] * 7,
        out_specs=(VMEM,) * 4,
        input_output_aliases={6: 2, 7: 3},
        scratch_shapes=[pltpu.VMEM((2, rows, 2 * branch), F32)],
        compiler_params=scoped(8),
        cost_estimate=cost(0, 2**16),
        name="conv0_far",
    )(place, near(gains), near(gains_p), near(last), near(last_theirs), wide, hm, hp)[:2]

    def mix0(z, z_theirs, blocks_used, name):
        n = len(blocks_used)
        states = [near_out(2, rows, half)] if blocks_used[0] == 0 else []
        return pl.pallas_call(
            functools.partial(mix0_kernel, (rows, half, branch, 1, n, len(z))),
            out_shape=(near_out(n, 2, rows, half), near_out(n, 2, rows, half), *states),
            in_specs=[SMEM] + [VMEM] * (4 + 2 * len(z) + 2 * n),
            out_specs=(VMEM,) * (2 + len(states)),
            compiler_params=scoped(12),
            cost_estimate=cost(0, 2**16),
            name=name,
        )(
            place,
            near(gains),
            near(gains_p),
            near(mix_mine),
            near(mix_theirs),
            *[near(t) for t in (*z, *z_theirs)],
            *[near(mine[b]) for b in blocks_used],
            *[near(theirs[b]) for b in blocks_used],
        )

    za_mine, *z = lax.optimization_barrier((za_mine, *z))
    hm1, hp1, state = mix0([za_mine], [za_theirs], used[:2], "mix0_near")
    hm, hp = mix0(z, [swap_chan(t) for t in z], used[2:], "mix0_far")
    hm, hp, hm1, hp1, *weights1 = lax.optimization_barrier((hm, hp, hm1, hp1, *weights1))
    placed = pl.pallas_call(
        functools.partial(place_kernel, (conv_rows, mix_rows, pairs1)),
        out_shape=(near_out(wide_rows, 2 * branch), near_out(mix_whole, half)),
        in_specs=[SMEM] + [VMEM] * len(weights1),
        out_specs=(VMEM, VMEM),
        compiler_params=scoped(2),
        name="place",
    )(place, *[near(w) for w in weights1])
    wide, mix_last = placed
    z_mine = pl.pallas_call(
        functools.partial(conv1_kernel, (rows, half, branch)),
        out_shape=near_out(2, rows, branch),
        in_specs=[SMEM] + [VMEM] * 5,
        out_specs=VMEM,
        scratch_shapes=[pltpu.VMEM((2 * rows, 2 * branch), F32)],
        compiler_params=scoped(8),
        name="conv1",
    )(place, hm1, hp1, hm, hp, wide)
    z_theirs = swap_chan(z_mine)
    return pl.pallas_call(
        functools.partial(mix1_kernel, (branch,)),
        out_shape=(
            jax.ShapeDtypeStruct((rows, half), BF16),
            jax.ShapeDtypeStruct((rows, half), BF16),
        ),
        in_specs=[SMEM] + [VMEM] * 4,
        out_specs=(VMEM, VMEM),
        compiler_params=scoped(4),
        name="mix1",
    )(place, z_mine, near(z_theirs), mix_last, state)


def solution(mesh):
    return jax.shard_map(
        on_device,
        mesh=mesh,
        in_specs=(
            P(("groups", "seq"), "chan"),
            P(("groups", "seq"), "chan"),
            P(None, "chan"),
            P(None, "seq", None, "chan"),
            P(None, "seq", "chan"),
        ),
        out_specs=(P(("groups", "seq"), "chan"), P(("groups", "seq"), "chan")),
        check_vma=False,
    )
```

```python
import functools

import jax
import jax.numpy as jnp
from jax import lax
from jax.experimental import pallas as pl
from jax.experimental.pallas import tpu as pltpu
from jax.sharding import PartitionSpec as P

TAPS = 3
EPS = 1e-05
F32 = jnp.float32
BF16 = jnp.bfloat16
VMEM = pl.BlockSpec(memory_space=pltpu.VMEM)
SMEM = pl.BlockSpec(memory_space=pltpu.SMEM)
ANY = pl.BlockSpec(memory_space=pltpu.HBM)


def scoped(mebibytes):
    return pltpu.CompilerParams(vmem_limit_bytes=mebibytes * 2**20)


def near(block):
    return pltpu.with_memory_space_constraint(block, pltpu.VMEM)


def far(block):
    return pltpu.with_memory_space_constraint(block, pltpu.HBM)


def near_out(*shape):
    return pltpu.VMEM(shape, BF16)


def cost(flops, bytes_moved):
    return pl.CostEstimate(flops=flops, bytes_accessed=bytes_moved, transcendentals=0)


def swap_chan(block):
    return lax.ppermute(block, "chan", [(0, 1), (1, 0)])


def swap_groups(block):
    return lax.ppermute(block, "groups", [(0, 1), (1, 0)])


def swap_pair(block, seq):
    return lax.ppermute(block, "seq", [(s, s ^ 1) for s in range(seq)])


def ring(block, seq, by):
    return lax.ppermute(block, "seq", [(s, (s + by) % seq) for s in range(seq)])


def from_behind(block, seq, by):
    return lax.ppermute(block, "seq", [(s - by, s) for s in range(by, seq)])


def weight_moves(place, refs, conv_rows, mix_rows, pairs, wide, mix):
    if pairs is None:
        return [(refs[0], wide), (refs[1], mix)]
    s, g = place[0], place[1]
    seq, order = pairs
    moves = []
    for index, begin, skip, count, by, dx, dy in order:
        owner = lax.rem(s + (seq - by), seq)
        if dx:
            owner = owner + 1 - 2 * lax.rem(owner, 2)
        half = (1 - g) if dy else g
        unit = owner * 2 + half
        n_conv = min(conv_rows - skip, count)
        if wide is not None:
            to = pl.multiple_of(unit * conv_rows + skip, 16)
            moves.append((refs[index].at[pl.ds(begin, n_conv)], wide.at[pl.ds(to, n_conv)]))
        if count > n_conv and mix is not None:
            to = pl.multiple_of(unit * mix_rows, 16)
            moves.append(
                (refs[index].at[pl.ds(begin + n_conv, mix_rows)], mix.at[pl.ds(to, mix_rows)])
            )
    return moves


def normalise(xm, xp, dxm, dxp, gm, gp, width):
    total = jnp.sum(xm * xm, axis=1, keepdims=True) + jnp.sum(xp * xp, axis=1, keepdims=True)
    cross = jnp.sum(xm * dxm, axis=1, keepdims=True) + jnp.sum(xp * dxp, axis=1, keepdims=True)
    scale = lax.rsqrt(total / width + EPS)
    factor = scale * scale * scale * (cross / width)
    return (
        (gm * xm * scale).astype(BF16),
        (gp * xp * scale).astype(BF16),
        (gm * (dxm * scale - xm * factor)).astype(BF16),
        (gp * (dxp * scale - xp * factor)).astype(BF16),
    )


def gate_into(out, full, dfull, branch):
    tanh_f = jnp.tanh(full[:, :branch])
    sig_g = jax.nn.sigmoid(full[:, branch:])
    out[0][...] = (tanh_f * sig_g).astype(BF16)
    out[1][...] = (
        (1.0 - tanh_f * tanh_f) * sig_g * dfull[:, :branch]
        + tanh_f * sig_g * (1.0 - sig_g) * dfull[:, branch:]
    ).astype(BF16)


def norm_rows(gm, gp, mine, theirs, hm, hp, base):
    rows, half = mine.shape[1:]
    step = 64

    def body(i, carry):
        at = pl.ds(pl.multiple_of(i * step, step), step)
        to = pl.ds(pl.multiple_of(base + i * step, step), step)
        xm = mine[0, at, :].astype(F32)
        dxm = mine[1, at, :].astype(F32)
        xp = theirs[0, at, :].astype(F32)
        dxp = theirs[1, at, :].astype(F32)
        hm[0, to, :], hp[0, to, :], hm[1, to, :], hp[1, to, :] = normalise(
            xm, xp, dxm, dxp, gm, gp, 2 * half
        )
        return carry

    lax.fori_loop(0, rows // step, body, 0)


def ready_kernel(cfg, place, gm_ref, gp_ref, *refs):
    rows, tall, n_blocks, conv_rows, mix_rows, pairs = cfg
    wide, mix, hm, hp = refs[-4:]
    convs = refs[2 * n_blocks : -4]
    for src, dst in weight_moves(place, convs, conv_rows, mix_rows, pairs, wide, mix):
        dst[...] = src[...]
    for b in range(n_blocks):
        norm_rows(
            gm_ref[0:1, :],
            gp_ref[0:1, :],
            refs[b],
            refs[n_blocks + b],
            hm,
            hp,
            tall - (b + 1) * rows,
        )


def conv_slabs(cfg, place, hm, hp, wide, z_refs, acc):
    rows, half, branch, slabs = cfg
    c = place[2]
    at_m = pl.multiple_of(c * half, half)
    at_p = pl.multiple_of((1 - c) * half, half)
    for begin, size, taps in slabs:
        for v in range(2):
            full = None
            for k, row in enumerate(taps):
                for h, at in ((hm, at_m), (hp, at_p)):
                    part = jnp.dot(
                        h[v, row : row + size, :],
                        wide[pl.ds(2 * half * k + at, half), :],
                        preferred_element_type=F32,
                    )
                    full = part if full is None else full + part
            acc[v, 0:size, :] = full
        for r in range(0, size, rows):
            gate_into(
                [z_ref.at[begin + r : begin + r + rows, :] for z_ref in z_refs],
                acc[0, r : r + rows, :],
                acc[1, r : r + rows, :],
                branch,
            )


def conv0_near_kernel(cfg, weight_cfg, place, hm, hp, *refs):
    z_ref, wide, mix, acc = refs[-4:]
    if weight_cfg[2] is not None:
        for src, dst in weight_moves(place, refs[:-6], *weight_cfg, wide, mix):
            dst[...] = src[...]
    conv_slabs(cfg, place, hm, hp, wide, (z_ref.at[0], z_ref.at[1]), acc)


def conv0_far_kernel(cfg, place, gm_ref, gp_ref, mine, theirs, wide, _, __, *refs):
    z_ref, dz_ref, hm, hp, acc = refs
    norm_rows(gm_ref[0:1, :], gp_ref[0:1, :], mine, theirs, hm, hp, 0)
    conv_slabs(cfg, place, hm, hp, wide, (z_ref, dz_ref), acc)


def mix0_kernel(cfg, place, gm_ref, gp_ref, mixm_ref, mixp_ref, *refs):
    rows, half, branch, layer, count, n_z = cfg
    if n_z == 1:
        zm_refs, zp_refs = ([ref.at[0], ref.at[1]] for ref in refs[:2])
    else:
        zm_refs, zp_refs = refs[:2], refs[2:4]
    refs = refs[2 * n_z :]
    mine, theirs = refs[:count], refs[count : 2 * count]
    hm_ref, hp_ref, *state_refs = refs[2 * count :]
    c = place[2]
    at_m = pl.ds(pl.multiple_of(c * branch, branch), branch)
    at_p = pl.ds(pl.multiple_of((1 - c) * branch, branch), branch)
    gm = gm_ref[layer : layer + 1, :]
    gp = gp_ref[layer : layer + 1, :]
    for j in range(count):
        at = slice((count - 1 - j) * rows, (count - j) * rows)
        new = []
        for v in range(2):
            zm = zm_refs[v][at, :]
            zp = zp_refs[v][at, :]
            for x_ref, mix in ((mine[j], mixm_ref), (theirs[j], mixp_ref)):
                y = jnp.dot(zm, mix[at_m, :], preferred_element_type=F32)
                y = y + jnp.dot(zp, mix[at_p, :], preferred_element_type=F32)
                new.append((x_ref[v].astype(F32) + y).astype(BF16))
        if j == 0 and state_refs:
            state_refs[0][0] = new[0]
            state_refs[0][1] = new[2]
        xm, xp, dxm, dxp = (t.astype(F32) for t in new)
        hm_ref[j, 0], hp_ref[j, 0], hm_ref[j, 1], hp_ref[j, 1] = normalise(
            xm, xp, dxm, dxp, gm, gp, 2 * half
        )


def conv1_kernel(cfg, weight_cfg, place, hm_near, hp_near, hm_far, hp_far, *refs):
    rows, half, branch = cfg
    z_ref, mix, wide, acc = refs[-4:]
    for src, dst in weight_moves(place, refs[:-4], *weight_cfg, wide, mix):
        dst[...] = src[...]
    c = place[2]
    at_m = pl.multiple_of(c * half, half)
    at_p = pl.multiple_of((1 - c) * half, half)
    full = None
    for k in range(TAPS):
        for near_ref, far_ref, at in ((hm_near, hm_far, at_m), (hp_near, hp_far, at_p)):
            part = jnp.dot(
                (near_ref[k] if k < 2 else far_ref[0]).reshape(2 * rows, half),
                wide[pl.ds(2 * half * k + at, half), :],
                preferred_element_type=F32,
            )
            full = part if full is None else full + part
    acc[...] = full
    gate_into((z_ref.at[0], z_ref.at[1]), acc[0:rows, :], acc[rows : 2 * rows, :], branch)


def mix1_kernel(cfg, place, zm_ref, zp_ref, mix_ref, state_ref, out_ref, dout_ref):
    (branch,) = cfg
    c = place[2]
    at_m = pl.ds(pl.multiple_of(c * branch, branch), branch)
    at_p = pl.ds(pl.multiple_of((1 - c) * branch, branch), branch)
    for v, out in ((0, out_ref), (1, dout_ref)):
        y = jnp.dot(zm_ref[v], mix_ref[at_m, :], preferred_element_type=F32)
        y = y + jnp.dot(zp_ref[v], mix_ref[at_p, :], preferred_element_type=F32)
        out[...] = (state_ref[v].astype(F32) + y).astype(BF16)


def pack(seq, place, *buffers):
    arrays = []

    def index(array):
        for i, known in enumerate(arrays):
            if known is array:
                return i
        arrays.append(array)
        return len(arrays) - 1

    plan = []
    for buffer in buffers:
        parts = []
        for array, begin, count, *mark in buffer:
            planes, even = (mark + [None, None])[:2] if mark else (None, None)
            parts.append(
                (index(array), begin, count, planes, None if even is None else index(even))
            )
        plan.append(parts)
    width = arrays[0].shape[-1]

    def kernel(place_ref, *refs):
        s = place_ref[0]
        for out, parts in zip(refs[len(arrays) :], plan):
            to = 0
            for i, begin, count, planes, even in parts:
                value = refs[i][begin : begin + count, :]
                if planes is not None:
                    value = jnp.where(s < max(2 * planes, 1), jnp.zeros_like(value), value)
                if even is not None:
                    value = jnp.where(lax.rem(s, 2) == 1, value, refs[even][...])
                out[to : to + count, :] = value
                to += count

    return pl.pallas_call(
        kernel,
        out_shape=tuple(near_out(sum(part[2] for part in buf), width) for buf in buffers),
        in_specs=[SMEM] + [VMEM] * len(arrays),
        out_specs=(VMEM,) * len(buffers),
        compiler_params=scoped(4),
        name="pack",
    )(place, *[near(array) for array in arrays])


def exchange(place, own, chunks, gains, seq, ready, newest):
    both = chunks
    unit = both.shape[0] // 2
    tall = own.shape[0]
    pieces = ([], [])
    order = ([], [])

    def keep(layer, array, *slots):
        for begin, skip, count, k, dx, dy in slots:
            order[layer].append((len(pieces[layer]), begin, skip, count, 2 * k, dx, dy))
        pieces[layer].append(array)

    def whole(layer, array, *slots):
        keep(layer, array, *[(i * unit, 0, unit, *slot) for i, slot in enumerate(slots)])

    def together(*blocks):
        return lax.optimization_barrier(blocks)

    def x(block):
        return swap_pair(block, seq)

    def y(block):
        return swap_groups(block)

    def z(block, by=1):
        return ring(block, seq, 2 * by)

    c0, c1 = both[:unit], both[unit:]
    whole(0, both, (0, 0, 0))
    keep(1, both, (unit, 0, unit, 0, 0, 0))
    z1a, z1b, x1, y1, own, c1 = together(z(c0), z(c0, 3), x(both), y(both), own, c1)
    whole(0, z1a, (1, 0, 0))
    whole(0, z1b, (3, 0, 0))
    whole(0, x1, (0, 1, 0))
    keep(1, x1, (unit, 0, unit, 0, 1, 0))
    whole(0, y1, (0, 0, 1))
    keep(1, y1, (unit, 0, unit, 0, 0, 1))
    to_z, to_x, to_y = pack(
        seq,
        place,
        [(z1a, 0, unit), (own, 0, tall)],
        [(z1a, 0, unit), (z1b, 0, unit), (y1, unit, unit)],
        [(z1a, 0, unit), (z1b, 0, unit), (x1, 0, unit)],
    )
    z2, x2, y2, own, c1, gains_p = together(z(to_z), x(to_x), y(to_y), own, c1, swap_chan(gains))
    keep(0, z2, (0, 0, unit, 2, 0, 0))
    whole(0, x2, (1, 1, 0), (3, 1, 0))
    keep(1, x2, (2 * unit, 0, unit, 0, 1, 1))
    whole(0, y2, (1, 0, 1), (3, 0, 1), (0, 1, 1))
    to_z, to_x, to_y, two = pack(
        seq,
        place,
        [(both, unit, unit), (x2, 2 * unit, unit)],
        [(z2, 0, unit), (z2, unit, tall, 1, own)],
        [(z2, 0, unit), (x2, 0, 2 * unit)],
        [(z2, unit, tall, 1)],
    )
    z3a, z3b, x3, y3 = together(z(to_z), z(c1, 3), x(to_x), y(to_y))
    whole(1, z3a, (1, 0, 0), (1, 1, 1))
    whole(1, z3b, (3, 0, 0))
    keep(0, x3, (0, 0, unit, 2, 1, 0))
    whole(0, y3, (2, 0, 1), (1, 1, 1), (3, 1, 1))
    cut = unit // 2
    to_z, to_x, w_x, w_y, one = pack(
        seq,
        place,
        [(z3a, 0, unit), (x3, unit, tall, 0)],
        [(z3a, 0, unit), (z3b, 0, unit)],
        [(y3, 0, cut)],
        [(x3, cut, unit - cut)],
        [(x3, unit, tall, 0)],
    )
    first = ready(gains_p, (own, one, two), pieces[0], (seq, tuple(order[0])))
    pieces[0].clear()
    order[0].clear()
    x4a, y4a = x(w_x), y(w_y)
    keep(0, x4a, (0, 0, cut, 2, 1, 1))
    keep(0, y4a, (0, cut, unit - cut, 2, 1, 1))
    made = newest(first, pieces[0], (seq, tuple(order[0])))
    to_x = together(to_x, x4a, y4a)[0]
    z4, x4, y4, made = together(z(to_z), x(to_x), y(to_x), made)
    keep(1, z4, (0, 0, unit, 2, 0, 0))
    whole(1, x4, (1, 1, 0), (3, 1, 0))
    whole(1, y4, (1, 0, 1), (3, 0, 1))
    to_z, to_x, to_y, three = pack(
        seq,
        place,
        [(z3a, unit, unit)],
        [(z4, 0, unit), (y4, unit, cut)],
        [(z4, 0, unit), (x4, unit + cut, unit - cut)],
        [(z4, unit, tall, 1)],
    )
    x5, y5, z5 = x(to_x), y(to_y), z(to_z)
    whole(1, z5, (2, 1, 1))
    keep(1, x5, (0, 0, unit, 2, 1, 0), (unit, 0, cut, 3, 1, 1))
    keep(1, y5, (0, 0, unit, 2, 0, 1), (unit, cut, unit - cut, 3, 1, 1))
    return gains_p, (one, two, three), made, (x5, y5, z5), pieces[1], (seq, tuple(order[1]))


def on_device(signal, tangent, gains, convolution_kernel, mixing_kernel):
    rows, half = signal.shape
    seq = lax.axis_size("seq")
    layers = gains.shape[0]
    branch = convolution_kernel.shape[3]
    shard = convolution_kernel.shape[1]
    mix_shard = mixing_kernel.shape[1]
    lag = rows * seq // 16
    place = jnp.stack([lax.axis_index("seq"), lax.axis_index("groups"), lax.axis_index("chan")])
    place = place.astype(jnp.int32)
    wide_rows, mix_whole = shard * seq, mix_shard * seq

    own = jnp.stack([signal, tangent], 0)
    if 2 * lag == rows:
        conv_rows, mix_rows = shard // 2, mix_shard // 2
        g = lax.axis_index("groups")
        chunks = jnp.concatenate(
            [
                lax.dynamic_slice_in_dim(
                    convolution_kernel, g * conv_rows, conv_rows, 1
                ).reshape(layers, conv_rows, 2 * branch),
                lax.dynamic_slice_in_dim(mixing_kernel, g * mix_rows, mix_rows, 1),
            ],
            1,
        ).reshape(layers * (conv_rows + mix_rows), 2 * branch)
        step, used = lag, (0, 1, 2)
        blocks = 4
    else:
        conv_rows, mix_rows = shard, mix_shard
        conv_local = convolution_kernel.reshape(layers, shard, 2 * branch)
        weights = [
            [
                lax.all_gather(conv_local[l], "seq", axis=0, tiled=True),
                lax.all_gather(mixing_kernel[l], "seq", axis=0, tiled=True),
            ]
            for l in range(layers)
        ]
        step, used = rows, (0, 2, 4)
        blocks = 7
    tall = blocks * rows
    starts = tuple(tall - rows - m * step for m in range(7))
    if 2 * lag == rows:
        slabs = ((0, 2 * rows, tuple(starts[2 + k] for k in range(TAPS))),)
    else:
        slabs = tuple(
            ((1 - j) * rows, rows, tuple(starts[2 * j + k] for k in range(TAPS))) for j in range(2)
        )
    far_slabs = ((0, rows, tuple(starts[4 + k] for k in range(TAPS))),)

    mine, theirs = [], []

    def ready(gains_p, halo, pieces, pairs):
        for block in halo:
            mine.append(block.reshape(own.shape))
            theirs.append(swap_chan(mine[-1]))
        cfg = (rows, tall, len(halo), conv_rows, mix_rows, pairs)
        return pl.pallas_call(
            functools.partial(ready_kernel, cfg),
            out_shape=(
                near_out(wide_rows, 2 * branch),
                near_out(mix_whole, half),
                near_out(2, tall, half),
                near_out(2, tall, half),
            ),
            in_specs=[SMEM] + [VMEM] * (2 + 2 * len(halo) + len(pieces)),
            out_specs=(VMEM,) * 4,
            compiler_params=scoped(4),
            cost_estimate=cost(0, 2**16),
            name="ready",
        )(
            place,
            near(gains),
            near(gains_p),
            *[near(block) for block in (*mine, *theirs)],
            *[near(piece) for piece in pieces],
        )

    def newest(made, pieces, pairs):
        wide, mix, hm, hp = made
        n_in = 3 + len(pieces)
        z, wide, mix = pl.pallas_call(
            functools.partial(
                conv0_near_kernel, (rows, half, branch, slabs), (conv_rows, mix_rows, pairs)
            ),
            out_shape=(
                near_out(2, 2 * rows, branch),
                near_out(wide_rows, 2 * branch),
                near_out(mix_whole, half),
            ),
            in_specs=[SMEM] + [VMEM] * (n_in + 1),
            out_specs=(VMEM,) * 3,
            input_output_aliases={n_in: 1, n_in + 1: 2},
            scratch_shapes=[pltpu.VMEM((2, slabs[0][1], 2 * branch), F32)],
            compiler_params=scoped(12),
            cost_estimate=cost(0, 2**16),
            name="conv0_near",
        )(place, hm, hp, *[near(piece) for piece in pieces], wide, mix)
        return z, mix, wide, hm, hp

    if 2 * lag == rows:
        flat = own.reshape(2 * rows, half)
        gains_p, halo, made, beside, weights1, pairs1 = exchange(
            place, flat, chunks, gains, seq, ready, newest
        )
        last = halo[-1].reshape(own.shape)
    else:
        gains_p = swap_chan(gains)
        halo = [from_behind(own, seq, k * (lag // rows)) for k in range(1, 7)]
        made = newest(ready(gains_p, (own, *halo[:-1]), weights[0], None), [], None)
        last, beside, weights1, pairs1 = halo[-1], (), weights[1], None
    za_mine, mix_mine, wide, hm, hp = made
    last_theirs, za_theirs, mix_theirs = lax.optimization_barrier(
        (swap_chan(last), swap_chan(za_mine), swap_chan(mix_mine))
    )

    z = pl.pallas_call(
        functools.partial(conv0_far_kernel, (rows, half, branch, far_slabs)),
        out_shape=(
            near_out(rows, branch),
            near_out(rows, branch),
            near_out(2, tall, half),
            near_out(2, tall, half),
        ),
        in_specs=[SMEM] + [VMEM] * 7,
        out_specs=(VMEM,) * 4,
        input_output_aliases={6: 2, 7: 3},
        scratch_shapes=[pltpu.VMEM((2, rows, 2 * branch), F32)],
        compiler_params=scoped(8),
        cost_estimate=cost(0, 2**16),
        name="conv0_far",
    )(place, near(gains), near(gains_p), near(last), near(last_theirs), wide, hm, hp)[:2]

    def mix0(z, z_theirs, blocks_used, name):
        n = len(blocks_used)
        states = [near_out(2, rows, half)] if blocks_used[0] == 0 else []
        return pl.pallas_call(
            functools.partial(mix0_kernel, (rows, half, branch, 1, n, len(z))),
            out_shape=(near_out(n, 2, rows, half), near_out(n, 2, rows, half), *states),
            in_specs=[SMEM] + [VMEM] * (4 + 2 * len(z) + 2 * n),
            out_specs=(VMEM,) * (2 + len(states)),
            compiler_params=scoped(12),
            cost_estimate=cost(0, 2**16),
            name=name,
        )(
            place,
            near(gains),
            near(gains_p),
            near(mix_mine),
            near(mix_theirs),
            *[near(t) for t in (*z, *z_theirs)],
            *[near(mine[b]) for b in blocks_used],
            *[near(theirs[b]) for b in blocks_used],
        )

    za_mine, *z = lax.optimization_barrier((za_mine, *z))
    hm1, hp1, state = mix0([za_mine], [za_theirs], used[:2], "mix0_near")
    hm, hp = mix0(z, [swap_chan(t) for t in z], used[2:], "mix0_far")
    hm, hp, hm1, hp1, *weights1 = lax.optimization_barrier((hm, hp, hm1, hp1, *weights1))
    z_mine, mix_last = pl.pallas_call(
        functools.partial(
            conv1_kernel, (rows, half, branch), (conv_rows, mix_rows, pairs1)
        ),
        out_shape=(near_out(2, rows, branch), near_out(mix_whole, half)),
        in_specs=[SMEM] + [VMEM] * (4 + len(weights1)),
        out_specs=(VMEM, VMEM),
        scratch_shapes=[
            pltpu.VMEM((wide_rows, 2 * branch), BF16),
            pltpu.VMEM((2 * rows, 2 * branch), F32),
        ],
        compiler_params=scoped(12),
        name="conv1",
    )(place, hm1, hp1, hm, hp, *[near(w) for w in weights1])
    z_theirs = swap_chan(z_mine)
    return pl.pallas_call(
        functools.partial(mix1_kernel, (branch,)),
        out_shape=(
            jax.ShapeDtypeStruct((rows, half), BF16),
            jax.ShapeDtypeStruct((rows, half), BF16),
        ),
        in_specs=[SMEM] + [VMEM] * 4,
        out_specs=(VMEM, VMEM),
        compiler_params=scoped(4),
        name="mix1",
    )(place, z_mine, near(z_theirs), mix_last, state)


def solution(mesh):
    return jax.shard_map(
        on_device,
        mesh=mesh,
        in_specs=(
            P(("groups", "seq"), "chan"),
            P(("groups", "seq"), "chan"),
            P(None, "chan"),
            P(None, "seq", None, "chan"),
            P(None, "seq", "chan"),
        ),
        out_specs=(P(("groups", "seq"), "chan"), P(("groups", "seq"), "chan")),
        check_vma=False,
    )
```

```python
import functools

import jax
import jax.numpy as jnp
from jax import lax
from jax.experimental import pallas as pl
from jax.experimental.pallas import tpu as pltpu
from jax.sharding import PartitionSpec as P

TAPS = 3
EPS = 1e-05
F32 = jnp.float32
BF16 = jnp.bfloat16
VMEM = pl.BlockSpec(memory_space=pltpu.VMEM)
SMEM = pl.BlockSpec(memory_space=pltpu.SMEM)
ANY = pl.BlockSpec(memory_space=pltpu.HBM)


def scoped(mebibytes):
    return pltpu.CompilerParams(vmem_limit_bytes=mebibytes * 2**20)


def near(block):
    return pltpu.with_memory_space_constraint(block, pltpu.VMEM)


def far(block):
    return pltpu.with_memory_space_constraint(block, pltpu.HBM)


def near_out(*shape):
    return pltpu.VMEM(shape, BF16)


def cost(flops, bytes_moved):
    return pl.CostEstimate(flops=flops, bytes_accessed=bytes_moved, transcendentals=0)


def swap_chan(block):
    return lax.ppermute(block, "chan", [(0, 1), (1, 0)])


def swap_groups(block):
    return lax.ppermute(block, "groups", [(0, 1), (1, 0)])


def swap_pair(block, seq):
    return lax.ppermute(block, "seq", [(s, s ^ 1) for s in range(seq)])


def ring(block, seq, by):
    return lax.ppermute(block, "seq", [(s, (s + by) % seq) for s in range(seq)])


def from_behind(block, seq, by):
    return lax.ppermute(block, "seq", [(s - by, s) for s in range(by, seq)])


def weight_moves(place, refs, conv_rows, mix_rows, pairs, wide, mix):
    if pairs is None:
        return [(refs[0], wide), (refs[1], mix)]
    s, g = place[0], place[1]
    seq, order = pairs
    moves = []
    for index, begin, skip, count, by, dx, dy in order:
        owner = lax.rem(s + (seq - by), seq)
        if dx:
            owner = owner + 1 - 2 * lax.rem(owner, 2)
        half = (1 - g) if dy else g
        unit = owner * 2 + half
        n_conv = min(conv_rows - skip, count)
        if wide is not None:
            to = pl.multiple_of(unit * conv_rows + skip, 16)
            moves.append((refs[index].at[pl.ds(begin, n_conv)], wide.at[pl.ds(to, n_conv)]))
        if count > n_conv and mix is not None:
            to = pl.multiple_of(unit * mix_rows, 16)
            moves.append(
                (refs[index].at[pl.ds(begin + n_conv, mix_rows)], mix.at[pl.ds(to, mix_rows)])
            )
    return moves


def normalise(xm, xp, dxm, dxp, gm, gp, width):
    total = jnp.sum(xm * xm, axis=1, keepdims=True) + jnp.sum(xp * xp, axis=1, keepdims=True)
    cross = jnp.sum(xm * dxm, axis=1, keepdims=True) + jnp.sum(xp * dxp, axis=1, keepdims=True)
    scale = lax.rsqrt(total / width + EPS)
    factor = scale * scale * scale * (cross / width)
    return (
        (gm * xm * scale).astype(BF16),
        (gp * xp * scale).astype(BF16),
        (gm * (dxm * scale - xm * factor)).astype(BF16),
        (gp * (dxp * scale - xp * factor)).astype(BF16),
    )


def gate_into(out, full, dfull, branch):
    tanh_f = jnp.tanh(full[:, :branch])
    sig_g = jax.nn.sigmoid(full[:, branch:])
    out[0][...] = (tanh_f * sig_g).astype(BF16)
    out[1][...] = (
        (1.0 - tanh_f * tanh_f) * sig_g * dfull[:, :branch]
        + tanh_f * sig_g * (1.0 - sig_g) * dfull[:, branch:]
    ).astype(BF16)


def norm_rows(gm, gp, mine, theirs, hm, hp, base):
    rows, half = mine.shape[1:]
    step = 64

    def body(i, carry):
        at = pl.ds(pl.multiple_of(i * step, step), step)
        to = pl.ds(pl.multiple_of(base + i * step, step), step)
        xm = mine[0, at, :].astype(F32)
        dxm = mine[1, at, :].astype(F32)
        xp = theirs[0, at, :].astype(F32)
        dxp = theirs[1, at, :].astype(F32)
        hm[0, to, :], hp[0, to, :], hm[1, to, :], hp[1, to, :] = normalise(
            xm, xp, dxm, dxp, gm, gp, 2 * half
        )
        return carry

    lax.fori_loop(0, rows // step, body, 0)


def ready_kernel(cfg, place, gm_ref, gp_ref, *refs):
    rows, tall, n_blocks, conv_rows, mix_rows, pairs = cfg
    wide, mix, hm, hp = refs[-4:]
    convs = refs[2 * n_blocks : -4]
    for src, dst in weight_moves(place, convs, conv_rows, mix_rows, pairs, wide, mix):
        dst[...] = src[...]
    for b in range(n_blocks):
        norm_rows(
            gm_ref[0:1, :],
            gp_ref[0:1, :],
            refs[b],
            refs[n_blocks + b],
            hm,
            hp,
            tall - (b + 1) * rows,
        )


def conv_slabs(cfg, place, hm, hp, wide, z_refs, acc):
    rows, half, branch, slabs = cfg
    c = place[2]
    at_m = pl.multiple_of(c * half, half)
    at_p = pl.multiple_of((1 - c) * half, half)
    for begin, size, taps in slabs:
        for v in range(2):
            full = None
            for k, row in enumerate(taps):
                for h, at in ((hm, at_m), (hp, at_p)):
                    part = jnp.dot(
                        h[v, row : row + size, :],
                        wide[pl.ds(2 * half * k + at, half), :],
                        preferred_element_type=F32,
                    )
                    full = part if full is None else full + part
            acc[v, 0:size, :] = full
        for r in range(0, size, rows):
            gate_into(
                [z_ref.at[begin + r : begin + r + rows, :] for z_ref in z_refs],
                acc[0, r : r + rows, :],
                acc[1, r : r + rows, :],
                branch,
            )


def conv0_near_kernel(cfg, weight_cfg, place, hm, hp, *refs):
    z_ref, wide, mix, acc = refs[-4:]
    if weight_cfg[2] is not None:
        for src, dst in weight_moves(place, refs[:-6], *weight_cfg, wide, mix):
            dst[...] = src[...]
    conv_slabs(cfg, place, hm, hp, wide, (z_ref.at[0], z_ref.at[1]), acc)


def conv0_far_kernel(cfg, place, gm_ref, gp_ref, mine, theirs, wide, _, __, *refs):
    z_ref, dz_ref, hm, hp, acc = refs
    norm_rows(gm_ref[0:1, :], gp_ref[0:1, :], mine, theirs, hm, hp, 0)
    conv_slabs(cfg, place, hm, hp, wide, (z_ref, dz_ref), acc)


def mix0_kernel(cfg, place, gm_ref, gp_ref, mixm_ref, mixp_ref, *refs):
    rows, half, branch, layer, count, n_z = cfg
    if n_z == 1:
        zm_refs, zp_refs = ([ref.at[0], ref.at[1]] for ref in refs[:2])
    else:
        zm_refs, zp_refs = refs[:2], refs[2:4]
    refs = refs[2 * n_z :]
    mine, theirs = refs[:count], refs[count : 2 * count]
    hm_ref, hp_ref, *state_refs = refs[2 * count :]
    c = place[2]
    at_m = pl.ds(pl.multiple_of(c * branch, branch), branch)
    at_p = pl.ds(pl.multiple_of((1 - c) * branch, branch), branch)
    gm = gm_ref[layer : layer + 1, :]
    gp = gp_ref[layer : layer + 1, :]
    for j in range(count):
        at = slice((count - 1 - j) * rows, (count - j) * rows)
        new = []
        for v in range(2):
            zm = zm_refs[v][at, :]
            zp = zp_refs[v][at, :]
            for x_ref, mix in ((mine[j], mixm_ref), (theirs[j], mixp_ref)):
                y = jnp.dot(zm, mix[at_m, :], preferred_element_type=F32)
                y = y + jnp.dot(zp, mix[at_p, :], preferred_element_type=F32)
                new.append((x_ref[v].astype(F32) + y).astype(BF16))
        if j == 0 and state_refs:
            state_refs[0][0] = new[0]
            state_refs[0][1] = new[2]
        xm, xp, dxm, dxp = (t.astype(F32) for t in new)
        hm_ref[j, 0], hp_ref[j, 0], hm_ref[j, 1], hp_ref[j, 1] = normalise(
            xm, xp, dxm, dxp, gm, gp, 2 * half
        )


def conv1_kernel(cfg, weight_cfg, place, hm_near, hp_near, hm_far, hp_far, *refs):
    rows, half, branch = cfg
    z_ref, mix, wide, acc = refs[-4:]
    for src, dst in weight_moves(place, refs[:-4], *weight_cfg, wide, mix):
        dst[...] = src[...]
    c = place[2]
    at_m = pl.multiple_of(c * half, half)
    at_p = pl.multiple_of((1 - c) * half, half)
    full = None
    for k in range(TAPS):
        for near_ref, far_ref, at in ((hm_near, hm_far, at_m), (hp_near, hp_far, at_p)):
            part = jnp.dot(
                (near_ref[k] if k < 2 else far_ref[0]).reshape(2 * rows, half),
                wide[pl.ds(2 * half * k + at, half), :],
                preferred_element_type=F32,
            )
            full = part if full is None else full + part
    acc[...] = full
    gate_into((z_ref.at[0], z_ref.at[1]), acc[0:rows, :], acc[rows : 2 * rows, :], branch)


def mix1_kernel(cfg, place, zm_ref, zp_ref, mix_ref, state_ref, out_ref, dout_ref):
    (branch,) = cfg
    c = place[2]
    at_m = pl.ds(pl.multiple_of(c * branch, branch), branch)
    at_p = pl.ds(pl.multiple_of((1 - c) * branch, branch), branch)
    for v, out in ((0, out_ref), (1, dout_ref)):
        y = jnp.dot(zm_ref[v], mix_ref[at_m, :], preferred_element_type=F32)
        y = y + jnp.dot(zp_ref[v], mix_ref[at_p, :], preferred_element_type=F32)
        out[...] = (state_ref[v].astype(F32) + y).astype(BF16)


def pack(seq, place, *buffers):
    arrays = []

    def index(array):
        for i, known in enumerate(arrays):
            if known is array:
                return i
        arrays.append(array)
        return len(arrays) - 1

    plan = []
    for buffer in buffers:
        parts = []
        for array, begin, count, *mark in buffer:
            planes, even = (mark + [None, None])[:2] if mark else (None, None)
            parts.append(
                (index(array), begin, count, planes, None if even is None else index(even))
            )
        plan.append(parts)
    width = arrays[0].shape[-1]

    def kernel(place_ref, *refs):
        s = place_ref[0]
        for out, parts in zip(refs[len(arrays) :], plan):
            to = 0
            for i, begin, count, planes, even in parts:
                value = refs[i][begin : begin + count, :]
                if planes is not None:
                    value = jnp.where(s < max(2 * planes, 1), jnp.zeros_like(value), value)
                if even is not None:
                    value = jnp.where(lax.rem(s, 2) == 1, value, refs[even][...])
                out[to : to + count, :] = value
                to += count

    return pl.pallas_call(
        kernel,
        out_shape=tuple(near_out(sum(part[2] for part in buf), width) for buf in buffers),
        in_specs=[SMEM] + [VMEM] * len(arrays),
        out_specs=(VMEM,) * len(buffers),
        compiler_params=scoped(4),
        name="pack",
    )(place, *[near(array) for array in arrays])


def exchange(place, own, chunks, gains, seq, ready, newest):
    both = chunks
    unit = both.shape[0] // 2
    tall = own.shape[0]
    pieces = ([], [])
    order = ([], [])

    def keep(layer, array, *slots):
        for begin, skip, count, k, dx, dy in slots:
            order[layer].append((len(pieces[layer]), begin, skip, count, 2 * k, dx, dy))
        pieces[layer].append(array)

    def whole(layer, array, *slots):
        keep(layer, array, *[(i * unit, 0, unit, *slot) for i, slot in enumerate(slots)])

    def together(*blocks):
        return lax.optimization_barrier(blocks)

    def x(block):
        return swap_pair(block, seq)

    def y(block):
        return swap_groups(block)

    def z(block, by=1):
        return ring(block, seq, 2 * by)

    c0, c1 = both[:unit], both[unit:]
    whole(0, both, (0, 0, 0))
    keep(1, both, (unit, 0, unit, 0, 0, 0))
    z1a, z1b, x1, y1, own, c1 = together(z(c0), z(c0, 3), x(both), y(both), own, c1)
    whole(0, z1a, (1, 0, 0))
    whole(0, z1b, (3, 0, 0))
    whole(0, x1, (0, 1, 0))
    keep(1, x1, (unit, 0, unit, 0, 1, 0))
    whole(0, y1, (0, 0, 1))
    keep(1, y1, (unit, 0, unit, 0, 0, 1))
    to_z, to_x, to_y = pack(
        seq,
        place,
        [(z1a, 0, unit), (own, 0, tall)],
        [(z1a, 0, unit), (z1b, 0, unit), (y1, unit, unit)],
        [(z1a, 0, unit), (z1b, 0, unit), (x1, 0, unit)],
    )
    z2, x2, y2, own, c1, gains_p, own_p = together(
        z(to_z), x(to_x), y(to_y), own, c1, swap_chan(gains), swap_chan(own)
    )
    keep(0, z2, (0, 0, unit, 2, 0, 0))
    whole(0, x2, (1, 1, 0), (3, 1, 0))
    keep(1, x2, (2 * unit, 0, unit, 0, 1, 1))
    whole(0, y2, (1, 0, 1), (3, 0, 1), (0, 1, 1))
    to_z, to_x, to_y, two = pack(
        seq,
        place,
        [(both, unit, unit), (x2, 2 * unit, unit)],
        [(z2, 0, unit), (z2, unit, tall, 1, own)],
        [(z2, 0, unit), (x2, 0, 2 * unit)],
        [(z2, unit, tall, 1)],
    )
    z3a, z3b, x3, y3 = together(z(to_z), z(c1, 3), x(to_x), y(to_y))
    whole(1, z3a, (1, 0, 0), (1, 1, 1))
    whole(1, z3b, (3, 0, 0))
    keep(0, x3, (0, 0, unit, 2, 1, 0))
    whole(0, y3, (2, 0, 1), (1, 1, 1), (3, 1, 1))
    cut = unit // 2
    to_z, to_x, w_x, w_y, one = pack(
        seq,
        place,
        [(z3a, 0, unit), (x3, unit, tall, 0)],
        [(z3a, 0, unit), (z3b, 0, unit)],
        [(y3, 0, cut)],
        [(x3, cut, unit - cut)],
        [(x3, unit, tall, 0)],
    )
    x4a, y4a = x(w_x), y(w_y)
    halo = (own, one, two), (own_p, swap_chan(one), swap_chan(two))
    first = ready(gains_p, halo, pieces[0], (seq, tuple(order[0])))
    pieces[0].clear()
    order[0].clear()
    keep(0, x4a, (0, 0, cut, 2, 1, 1))
    keep(0, y4a, (0, cut, unit - cut, 2, 1, 1))
    made = newest(first, pieces[0], (seq, tuple(order[0])))
    to_x = together(to_x, x4a, y4a)[0]
    z4, x4, y4, made = together(z(to_z), x(to_x), y(to_x), made)
    keep(1, z4, (0, 0, unit, 2, 0, 0))
    whole(1, x4, (1, 1, 0), (3, 1, 0))
    whole(1, y4, (1, 0, 1), (3, 0, 1))
    to_z, to_x, to_y, three = pack(
        seq,
        place,
        [(z3a, unit, unit)],
        [(z4, 0, unit), (y4, unit, cut)],
        [(z4, 0, unit), (x4, unit + cut, unit - cut)],
        [(z4, unit, tall, 1)],
    )
    x5, y5, z5 = x(to_x), y(to_y), z(to_z)
    whole(1, z5, (2, 1, 1))
    keep(1, x5, (0, 0, unit, 2, 1, 0), (unit, 0, cut, 3, 1, 1))
    keep(1, y5, (0, 0, unit, 2, 0, 1), (unit, cut, unit - cut, 3, 1, 1))
    return gains_p, (one, two, three), made, (x5, y5, z5), pieces[1], (seq, tuple(order[1]))


def on_device(signal, tangent, gains, convolution_kernel, mixing_kernel):
    rows, half = signal.shape
    seq = lax.axis_size("seq")
    layers = gains.shape[0]
    branch = convolution_kernel.shape[3]
    shard = convolution_kernel.shape[1]
    mix_shard = mixing_kernel.shape[1]
    lag = rows * seq // 16
    place = jnp.stack([lax.axis_index("seq"), lax.axis_index("groups"), lax.axis_index("chan")])
    place = place.astype(jnp.int32)
    wide_rows, mix_whole = shard * seq, mix_shard * seq

    own = jnp.stack([signal, tangent], 0)
    if 2 * lag == rows:
        conv_rows, mix_rows = shard // 2, mix_shard // 2
        g = lax.axis_index("groups")
        chunks = jnp.concatenate(
            [
                lax.dynamic_slice_in_dim(
                    convolution_kernel, g * conv_rows, conv_rows, 1
                ).reshape(layers, conv_rows, 2 * branch),
                lax.dynamic_slice_in_dim(mixing_kernel, g * mix_rows, mix_rows, 1),
            ],
            1,
        ).reshape(layers * (conv_rows + mix_rows), 2 * branch)
        step, used = lag, (0, 1, 2)
        blocks = 4
    else:
        conv_rows, mix_rows = shard, mix_shard
        conv_local = convolution_kernel.reshape(layers, shard, 2 * branch)
        weights = [
            [
                lax.all_gather(conv_local[l], "seq", axis=0, tiled=True),
                lax.all_gather(mixing_kernel[l], "seq", axis=0, tiled=True),
            ]
            for l in range(layers)
        ]
        step, used = rows, (0, 2, 4)
        blocks = 7
    tall = blocks * rows
    starts = tuple(tall - rows - m * step for m in range(7))
    if 2 * lag == rows:
        slabs = ((0, 2 * rows, tuple(starts[2 + k] for k in range(TAPS))),)
    else:
        slabs = tuple(
            ((1 - j) * rows, rows, tuple(starts[2 * j + k] for k in range(TAPS))) for j in range(2)
        )
    far_slabs = ((0, rows, tuple(starts[4 + k] for k in range(TAPS))),)

    mine, theirs = [], []

    def ready(gains_p, halo, pieces, pairs):
        mine.extend(block.reshape(own.shape) for block in halo[0])
        theirs.extend(block.reshape(own.shape) for block in halo[1])
        cfg = (rows, tall, len(mine), conv_rows, mix_rows, pairs)
        return pl.pallas_call(
            functools.partial(ready_kernel, cfg),
            out_shape=(
                near_out(wide_rows, 2 * branch),
                near_out(mix_whole, half),
                near_out(2, tall, half),
                near_out(2, tall, half),
            ),
            in_specs=[SMEM] + [VMEM] * (2 + 2 * len(mine) + len(pieces)),
            out_specs=(VMEM,) * 4,
            compiler_params=scoped(4),
            cost_estimate=cost(0, 2**16),
            name="ready",
        )(
            place,
            near(gains),
            near(gains_p),
            *[near(block) for block in (*mine, *theirs)],
            *[near(piece) for piece in pieces],
        )

    def newest(made, pieces, pairs):
        wide, mix, hm, hp = made
        n_in = 3 + len(pieces)
        z, wide, mix = pl.pallas_call(
            functools.partial(
                conv0_near_kernel, (rows, half, branch, slabs), (conv_rows, mix_rows, pairs)
            ),
            out_shape=(
                near_out(2, 2 * rows, branch),
                near_out(wide_rows, 2 * branch),
                near_out(mix_whole, half),
            ),
            in_specs=[SMEM] + [VMEM] * (n_in + 1),
            out_specs=(VMEM,) * 3,
            input_output_aliases={n_in: 1, n_in + 1: 2},
            scratch_shapes=[pltpu.VMEM((2, slabs[0][1], 2 * branch), F32)],
            compiler_params=scoped(12),
            cost_estimate=cost(0, 2**16),
            name="conv0_near",
        )(place, hm, hp, *[near(piece) for piece in pieces], wide, mix)
        return z, mix, wide, hm, hp

    if 2 * lag == rows:
        flat = own.reshape(2 * rows, half)
        gains_p, halo, made, beside, weights1, pairs1 = exchange(
            place, flat, chunks, gains, seq, ready, newest
        )
        last = halo[-1].reshape(own.shape)
    else:
        gains_p = swap_chan(gains)
        halo = [from_behind(own, seq, k * (lag // rows)) for k in range(1, 7)]
        newer = (own, *halo[:-1])
        newer = newer, tuple(swap_chan(block) for block in newer)
        made = newest(ready(gains_p, newer, weights[0], None), [], None)
        last, beside, weights1, pairs1 = halo[-1], (), weights[1], None
    za_mine, mix_mine, wide, hm, hp = made
    last_theirs, za_theirs, mix_theirs = lax.optimization_barrier(
        (swap_chan(last), swap_chan(za_mine), swap_chan(mix_mine))
    )

    z = pl.pallas_call(
        functools.partial(conv0_far_kernel, (rows, half, branch, far_slabs)),
        out_shape=(
            near_out(rows, branch),
            near_out(rows, branch),
            near_out(2, tall, half),
            near_out(2, tall, half),
        ),
        in_specs=[SMEM] + [VMEM] * 7,
        out_specs=(VMEM,) * 4,
        input_output_aliases={6: 2, 7: 3},
        scratch_shapes=[pltpu.VMEM((2, rows, 2 * branch), F32)],
        compiler_params=scoped(8),
        cost_estimate=cost(0, 2**16),
        name="conv0_far",
    )(place, near(gains), near(gains_p), near(last), near(last_theirs), wide, hm, hp)[:2]

    def mix0(z, z_theirs, blocks_used, name):
        n = len(blocks_used)
        states = [near_out(2, rows, half)] if blocks_used[0] == 0 else []
        return pl.pallas_call(
            functools.partial(mix0_kernel, (rows, half, branch, 1, n, len(z))),
            out_shape=(near_out(n, 2, rows, half), near_out(n, 2, rows, half), *states),
            in_specs=[SMEM] + [VMEM] * (4 + 2 * len(z) + 2 * n),
            out_specs=(VMEM,) * (2 + len(states)),
            compiler_params=scoped(12),
            cost_estimate=cost(0, 2**16),
            name=name,
        )(
            place,
            near(gains),
            near(gains_p),
            near(mix_mine),
            near(mix_theirs),
            *[near(t) for t in (*z, *z_theirs)],
            *[near(mine[b]) for b in blocks_used],
            *[near(theirs[b]) for b in blocks_used],
        )

    za_mine, *z = lax.optimization_barrier((za_mine, *z))
    hm1, hp1, state = mix0([za_mine], [za_theirs], used[:2], "mix0_near")
    hm, hp = mix0(z, [swap_chan(t) for t in z], used[2:], "mix0_far")
    hm, hp, hm1, hp1, *weights1 = lax.optimization_barrier((hm, hp, hm1, hp1, *weights1))
    z_mine, mix_last = pl.pallas_call(
        functools.partial(
            conv1_kernel, (rows, half, branch), (conv_rows, mix_rows, pairs1)
        ),
        out_shape=(near_out(2, rows, branch), near_out(mix_whole, half)),
        in_specs=[SMEM] + [VMEM] * (4 + len(weights1)),
        out_specs=(VMEM, VMEM),
        scratch_shapes=[
            pltpu.VMEM((wide_rows, 2 * branch), BF16),
            pltpu.VMEM((2 * rows, 2 * branch), F32),
        ],
        compiler_params=scoped(12),
        name="conv1",
    )(place, hm1, hp1, hm, hp, *[near(w) for w in weights1])
    z_theirs = swap_chan(z_mine)
    return pl.pallas_call(
        functools.partial(mix1_kernel, (branch,)),
        out_shape=(
            jax.ShapeDtypeStruct((rows, half), BF16),
            jax.ShapeDtypeStruct((rows, half), BF16),
        ),
        in_specs=[SMEM] + [VMEM] * 4,
        out_specs=(VMEM, VMEM),
        compiler_params=scoped(4),
        name="mix1",
    )(place, z_mine, near(z_theirs), mix_last, state)


def solution(mesh):
    return jax.shard_map(
        on_device,
        mesh=mesh,
        in_specs=(
            P(("groups", "seq"), "chan"),
            P(("groups", "seq"), "chan"),
            P(None, "chan"),
            P(None, "seq", None, "chan"),
            P(None, "seq", "chan"),
        ),
        out_specs=(P(("groups", "seq"), "chan"), P(("groups", "seq"), "chan")),
        check_vma=False,
    )
```

```python
import functools

import jax
import jax.numpy as jnp
from jax import lax
from jax.experimental import pallas as pl
from jax.experimental.pallas import tpu as pltpu
from jax.sharding import PartitionSpec as P

TAPS = 3
EPS = 1e-05
F32 = jnp.float32
BF16 = jnp.bfloat16
VMEM = pl.BlockSpec(memory_space=pltpu.VMEM)
SMEM = pl.BlockSpec(memory_space=pltpu.SMEM)
ANY = pl.BlockSpec(memory_space=pltpu.HBM)


def scoped(mebibytes):
    return pltpu.CompilerParams(vmem_limit_bytes=mebibytes * 2**20)


def near(block):
    return pltpu.with_memory_space_constraint(block, pltpu.VMEM)


def far(block):
    return pltpu.with_memory_space_constraint(block, pltpu.HBM)


def near_out(*shape):
    return pltpu.VMEM(shape, BF16)


def cost(flops, bytes_moved):
    return pl.CostEstimate(flops=flops, bytes_accessed=bytes_moved, transcendentals=0)


def swap_chan(block):
    return lax.ppermute(block, "chan", [(0, 1), (1, 0)])


def swap_groups(block):
    return lax.ppermute(block, "groups", [(0, 1), (1, 0)])


def swap_pair(block, seq):
    return lax.ppermute(block, "seq", [(s, s ^ 1) for s in range(seq)])


def ring(block, seq, by):
    return lax.ppermute(block, "seq", [(s, (s + by) % seq) for s in range(seq)])


def from_behind(block, seq, by):
    return lax.ppermute(block, "seq", [(s - by, s) for s in range(by, seq)])


def weight_moves(place, refs, conv_rows, mix_rows, pairs, wide, mix):
    if pairs is None:
        return [(refs[0], wide), (refs[1], mix)]
    s, g = place[0], place[1]
    seq, order = pairs
    moves = []
    for index, begin, skip, count, by, dx, dy in order:
        owner = lax.rem(s + (seq - by), seq)
        if dx:
            owner = owner + 1 - 2 * lax.rem(owner, 2)
        half = (1 - g) if dy else g
        unit = owner * 2 + half
        n_conv = min(conv_rows - skip, count)
        if wide is not None:
            to = pl.multiple_of(unit * conv_rows + skip, 16)
            moves.append((refs[index].at[pl.ds(begin, n_conv)], wide.at[pl.ds(to, n_conv)]))
        if count > n_conv and mix is not None:
            to = pl.multiple_of(unit * mix_rows, 16)
            moves.append(
                (refs[index].at[pl.ds(begin + n_conv, mix_rows)], mix.at[pl.ds(to, mix_rows)])
            )
    return moves


def normalise(xm, xp, dxm, dxp, gm, gp, width):
    total = jnp.sum(xm * xm, axis=1, keepdims=True) + jnp.sum(xp * xp, axis=1, keepdims=True)
    cross = jnp.sum(xm * dxm, axis=1, keepdims=True) + jnp.sum(xp * dxp, axis=1, keepdims=True)
    scale = lax.rsqrt(total / width + EPS)
    factor = scale * scale * scale * (cross / width)
    return (
        (gm * xm * scale).astype(BF16),
        (gp * xp * scale).astype(BF16),
        (gm * (dxm * scale - xm * factor)).astype(BF16),
        (gp * (dxp * scale - xp * factor)).astype(BF16),
    )


def gate_into(out, full, dfull, branch):
    tanh_f = jnp.tanh(full[:, :branch])
    sig_g = jax.nn.sigmoid(full[:, branch:])
    out[0][...] = (tanh_f * sig_g).astype(BF16)
    out[1][...] = (
        (1.0 - tanh_f * tanh_f) * sig_g * dfull[:, :branch]
        + tanh_f * sig_g * (1.0 - sig_g) * dfull[:, branch:]
    ).astype(BF16)


def norm_rows(gm, gp, mine, theirs, hm, hp, base):
    rows, half = mine.shape[1:]
    step = 64

    def body(i, carry):
        at = pl.ds(pl.multiple_of(i * step, step), step)
        to = pl.ds(pl.multiple_of(base + i * step, step), step)
        xm = mine[0, at, :].astype(F32)
        dxm = mine[1, at, :].astype(F32)
        xp = theirs[0, at, :].astype(F32)
        dxp = theirs[1, at, :].astype(F32)
        hm[0, to, :], hp[0, to, :], hm[1, to, :], hp[1, to, :] = normalise(
            xm, xp, dxm, dxp, gm, gp, 2 * half
        )
        return carry

    lax.fori_loop(0, rows // step, body, 0)


def ready_kernel(cfg, place, gm_ref, gp_ref, *refs):
    rows, tall, n_blocks, conv_rows, mix_rows, pairs = cfg
    wide, mix, hm, hp = refs[-4:]
    convs = refs[2 * n_blocks : -4]
    for src, dst in weight_moves(place, convs, conv_rows, mix_rows, pairs, wide, mix):
        dst[...] = src[...]
    for b in range(n_blocks):
        norm_rows(
            gm_ref[0:1, :],
            gp_ref[0:1, :],
            refs[b],
            refs[n_blocks + b],
            hm,
            hp,
            tall - (b + 1) * rows,
        )


def conv_slabs(cfg, place, hm, hp, wide, z_refs, acc):
    rows, half, branch, slabs = cfg
    c = place[2]
    at_m = pl.multiple_of(c * half, half)
    at_p = pl.multiple_of((1 - c) * half, half)
    for begin, size, taps in slabs:
        for v in range(2):
            full = None
            for k, row in enumerate(taps):
                for h, at in ((hm, at_m), (hp, at_p)):
                    part = jnp.dot(
                        h[v, row : row + size, :],
                        wide[pl.ds(2 * half * k + at, half), :],
                        preferred_element_type=F32,
                    )
                    full = part if full is None else full + part
            acc[v, 0:size, :] = full
        for r in range(0, size, rows):
            gate_into(
                [z_ref.at[begin + r : begin + r + rows, :] for z_ref in z_refs],
                acc[0, r : r + rows, :],
                acc[1, r : r + rows, :],
                branch,
            )


def conv0_near_kernel(cfg, weight_cfg, place, hm, hp, *refs):
    z_ref, wide, mix, acc = refs[-4:]
    if weight_cfg[2] is not None:
        for src, dst in weight_moves(place, refs[:-6], *weight_cfg, wide, mix):
            dst[...] = src[...]
    conv_slabs(cfg, place, hm, hp, wide, (z_ref.at[0], z_ref.at[1]), acc)


def conv0_far_kernel(cfg, place, gm_ref, gp_ref, mine, theirs, wide, _, __, *refs):
    z_ref, dz_ref, hm, hp, acc = refs
    norm_rows(gm_ref[0:1, :], gp_ref[0:1, :], mine, theirs, hm, hp, 0)
    conv_slabs(cfg, place, hm, hp, wide, (z_ref, dz_ref), acc)


def mix0_kernel(cfg, place, gm_ref, gp_ref, mixm_ref, mixp_ref, *refs):
    rows, half, branch, layer, count, n_z = cfg
    if n_z == 1:
        zm_refs, zp_refs = ([ref.at[0], ref.at[1]] for ref in refs[:2])
    else:
        zm_refs, zp_refs = refs[:2], refs[2:4]
    refs = refs[2 * n_z :]
    mine, theirs = refs[:count], refs[count : 2 * count]
    hm_ref, hp_ref, *state_refs = refs[2 * count :]
    c = place[2]
    at_m = pl.ds(pl.multiple_of(c * branch, branch), branch)
    at_p = pl.ds(pl.multiple_of((1 - c) * branch, branch), branch)
    gm = gm_ref[layer : layer + 1, :]
    gp = gp_ref[layer : layer + 1, :]
    for j in range(count):
        at = slice((count - 1 - j) * rows, (count - j) * rows)
        new = []
        for v in range(2):
            zm = zm_refs[v][at, :]
            zp = zp_refs[v][at, :]
            for x_ref, mix in ((mine[j], mixm_ref), (theirs[j], mixp_ref)):
                y = jnp.dot(zm, mix[at_m, :], preferred_element_type=F32)
                y = y + jnp.dot(zp, mix[at_p, :], preferred_element_type=F32)
                new.append((x_ref[v].astype(F32) + y).astype(BF16))
        if j == 0 and state_refs:
            state_refs[0][0] = new[0]
            state_refs[0][1] = new[2]
        xm, xp, dxm, dxp = (t.astype(F32) for t in new)
        hm_ref[j, 0], hp_ref[j, 0], hm_ref[j, 1], hp_ref[j, 1] = normalise(
            xm, xp, dxm, dxp, gm, gp, 2 * half
        )


def conv1_kernel(cfg, weight_cfg, place, hm_near, hp_near, hm_far, hp_far, *refs):
    rows, half, branch = cfg
    z_ref, mix, wide, acc = refs[-4:]
    for src, dst in weight_moves(place, refs[:-4], *weight_cfg, wide, mix):
        dst[...] = src[...]
    c = place[2]
    at_m = pl.multiple_of(c * half, half)
    at_p = pl.multiple_of((1 - c) * half, half)
    full = None
    for k in range(TAPS):
        for near_ref, far_ref, at in ((hm_near, hm_far, at_m), (hp_near, hp_far, at_p)):
            part = jnp.dot(
                (near_ref[k] if k < 2 else far_ref[0]).reshape(2 * rows, half),
                wide[pl.ds(2 * half * k + at, half), :],
                preferred_element_type=F32,
            )
            full = part if full is None else full + part
    acc[...] = full
    gate_into((z_ref.at[0], z_ref.at[1]), acc[0:rows, :], acc[rows : 2 * rows, :], branch)


def mix1_kernel(cfg, place, zm_ref, zp_ref, mix_ref, state_ref, out_ref, dout_ref):
    (branch,) = cfg
    c = place[2]
    at_m = pl.ds(pl.multiple_of(c * branch, branch), branch)
    at_p = pl.ds(pl.multiple_of((1 - c) * branch, branch), branch)
    for v, out in ((0, out_ref), (1, dout_ref)):
        y = jnp.dot(zm_ref[v], mix_ref[at_m, :], preferred_element_type=F32)
        y = y + jnp.dot(zp_ref[v], mix_ref[at_p, :], preferred_element_type=F32)
        out[...] = (state_ref[v].astype(F32) + y).astype(BF16)


def chunk_kernel(conv, mix, both, *chunks):
    for layer, chunk in enumerate(chunks):
        chunk[0 : conv.shape[1], :] = conv[layer]
        chunk[conv.shape[1] :, :] = mix[layer]
        begin = layer * chunk.shape[0]
        both[begin : begin + chunk.shape[0], :] = chunk[...]


def pack(seq, place, *buffers):
    arrays = []

    def index(array):
        for i, known in enumerate(arrays):
            if known is array:
                return i
        arrays.append(array)
        return len(arrays) - 1

    plan = []
    for buffer in buffers:
        parts = []
        for array, begin, count, *mark in buffer:
            planes, even = (mark + [None, None])[:2] if mark else (None, None)
            parts.append(
                (index(array), begin, count, planes, None if even is None else index(even))
            )
        plan.append(parts)
    width = arrays[0].shape[-1]

    def kernel(place_ref, *refs):
        s = place_ref[0]
        for out, parts in zip(refs[len(arrays) :], plan):
            to = 0
            for i, begin, count, planes, even in parts:
                value = refs[i][begin : begin + count, :]
                if planes is not None:
                    value = jnp.where(s < max(2 * planes, 1), jnp.zeros_like(value), value)
                if even is not None:
                    value = jnp.where(lax.rem(s, 2) == 1, value, refs[even][...])
                out[to : to + count, :] = value
                to += count

    return pl.pallas_call(
        kernel,
        out_shape=tuple(near_out(sum(part[2] for part in buf), width) for buf in buffers),
        in_specs=[SMEM] + [VMEM] * len(arrays),
        out_specs=(VMEM,) * len(buffers),
        compiler_params=scoped(4),
        name="pack",
    )(place, *[near(array) for array in arrays])


def exchange(place, own, chunks, gains, seq, ready, newest):
    both, c0, c1 = chunks
    unit = both.shape[0] // 2
    tall = own.shape[0]
    pieces = ([], [])
    order = ([], [])

    def keep(layer, array, *slots):
        for begin, skip, count, k, dx, dy in slots:
            order[layer].append((len(pieces[layer]), begin, skip, count, 2 * k, dx, dy))
        pieces[layer].append(array)

    def whole(layer, array, *slots):
        keep(layer, array, *[(i * unit, 0, unit, *slot) for i, slot in enumerate(slots)])

    def together(*blocks):
        return lax.optimization_barrier(blocks)

    def x(block):
        return swap_pair(block, seq)

    def y(block):
        return swap_groups(block)

    def z(block, by=1):
        return ring(block, seq, 2 * by)

    whole(0, both, (0, 0, 0))
    keep(1, both, (unit, 0, unit, 0, 0, 0))
    z1a, z1b, x1, y1, own, c1 = together(z(c0), z(c0, 3), x(both), y(both), own, c1)
    whole(0, z1a, (1, 0, 0))
    whole(0, z1b, (3, 0, 0))
    whole(0, x1, (0, 1, 0))
    keep(1, x1, (unit, 0, unit, 0, 1, 0))
    whole(0, y1, (0, 0, 1))
    keep(1, y1, (unit, 0, unit, 0, 0, 1))
    to_z, to_x, to_y = pack(
        seq,
        place,
        [(z1a, 0, unit), (own, 0, tall)],
        [(z1a, 0, unit), (z1b, 0, unit), (y1, unit, unit)],
        [(z1a, 0, unit), (z1b, 0, unit), (x1, 0, unit)],
    )
    z2, x2, y2, own, c1, gains_p, own_p = together(
        z(to_z), x(to_x), y(to_y), own, c1, swap_chan(gains), swap_chan(own)
    )
    keep(0, z2, (0, 0, unit, 2, 0, 0))
    whole(0, x2, (1, 1, 0), (3, 1, 0))
    keep(1, x2, (2 * unit, 0, unit, 0, 1, 1))
    whole(0, y2, (1, 0, 1), (3, 0, 1), (0, 1, 1))
    to_z, to_x, to_y, two = pack(
        seq,
        place,
        [(both, unit, unit), (x2, 2 * unit, unit)],
        [(z2, 0, unit), (z2, unit, tall, 1, own)],
        [(z2, 0, unit), (x2, 0, 2 * unit)],
        [(z2, unit, tall, 1)],
    )
    z3a, z3b, x3, y3 = together(z(to_z), z(c1, 3), x(to_x), y(to_y))
    whole(1, z3a, (1, 0, 0), (1, 1, 1))
    whole(1, z3b, (3, 0, 0))
    keep(0, x3, (0, 0, unit, 2, 1, 0))
    whole(0, y3, (2, 0, 1), (1, 1, 1), (3, 1, 1))
    cut = unit // 2
    to_z, to_x, w_x, w_y, one = pack(
        seq,
        place,
        [(z3a, 0, unit), (x3, unit, tall, 0)],
        [(z3a, 0, unit), (z3b, 0, unit)],
        [(y3, 0, cut)],
        [(x3, cut, unit - cut)],
        [(x3, unit, tall, 0)],
    )
    x4a, y4a = x(w_x), y(w_y)
    halo = (own, one, two), (own_p, swap_chan(one), swap_chan(two))
    first = ready(gains_p, halo, pieces[0], (seq, tuple(order[0])))
    pieces[0].clear()
    order[0].clear()
    keep(0, x4a, (0, 0, cut, 2, 1, 1))
    keep(0, y4a, (0, cut, unit - cut, 2, 1, 1))
    made = newest(first, pieces[0], (seq, tuple(order[0])))
    to_x = together(to_x, x4a, y4a)[0]
    z4, x4, y4, made = together(z(to_z), x(to_x), y(to_x), made)
    keep(1, z4, (0, 0, unit, 2, 0, 0))
    whole(1, x4, (1, 1, 0), (3, 1, 0))
    whole(1, y4, (1, 0, 1), (3, 0, 1))
    to_z, to_x, to_y, three = pack(
        seq,
        place,
        [(z3a, unit, unit)],
        [(z4, 0, unit), (y4, unit, cut)],
        [(z4, 0, unit), (x4, unit + cut, unit - cut)],
        [(z4, unit, tall, 1)],
    )
    x5, y5, z5 = x(to_x), y(to_y), z(to_z)
    whole(1, z5, (2, 1, 1))
    keep(1, x5, (0, 0, unit, 2, 1, 0), (unit, 0, cut, 3, 1, 1))
    keep(1, y5, (0, 0, unit, 2, 0, 1), (unit, cut, unit - cut, 3, 1, 1))
    return gains_p, (one, two, three), made, (x5, y5, z5), pieces[1], (seq, tuple(order[1]))


def on_device(signal, tangent, gains, convolution_kernel, mixing_kernel):
    rows, half = signal.shape
    seq = lax.axis_size("seq")
    layers = gains.shape[0]
    branch = convolution_kernel.shape[3]
    shard = convolution_kernel.shape[1]
    mix_shard = mixing_kernel.shape[1]
    lag = rows * seq // 16
    place = jnp.stack([lax.axis_index("seq"), lax.axis_index("groups"), lax.axis_index("chan")])
    place = place.astype(jnp.int32)
    wide_rows, mix_whole = shard * seq, mix_shard * seq

    own = jnp.stack([signal, tangent], 0)
    if 2 * lag == rows:
        conv_rows, mix_rows = shard // 2, mix_shard // 2
        g = lax.axis_index("groups")
        conv_part = lax.dynamic_slice_in_dim(
            convolution_kernel, g * conv_rows, conv_rows, 1
        ).reshape(layers, conv_rows, 2 * branch)
        mix_part = lax.dynamic_slice_in_dim(mixing_kernel, g * mix_rows, mix_rows, 1)
        unit = conv_rows + mix_rows
        chunks = pl.pallas_call(
            chunk_kernel,
            out_shape=(
                near_out(layers * unit, 2 * branch),
                *[near_out(unit, 2 * branch) for _ in range(layers)],
            ),
            in_specs=[VMEM, VMEM],
            out_specs=(VMEM,) * (1 + layers),
            compiler_params=scoped(2),
            name="chunk",
        )(near(conv_part), near(mix_part))
        step, used = lag, (0, 1, 2)
        blocks = 4
    else:
        conv_rows, mix_rows = shard, mix_shard
        conv_local = convolution_kernel.reshape(layers, shard, 2 * branch)
        weights = [
            [
                lax.all_gather(conv_local[l], "seq", axis=0, tiled=True),
                lax.all_gather(mixing_kernel[l], "seq", axis=0, tiled=True),
            ]
            for l in range(layers)
        ]
        step, used = rows, (0, 2, 4)
        blocks = 7
    tall = blocks * rows
    starts = tuple(tall - rows - m * step for m in range(7))
    if 2 * lag == rows:
        slabs = ((0, 2 * rows, tuple(starts[2 + k] for k in range(TAPS))),)
    else:
        slabs = tuple(
            ((1 - j) * rows, rows, tuple(starts[2 * j + k] for k in range(TAPS))) for j in range(2)
        )
    far_slabs = ((0, rows, tuple(starts[4 + k] for k in range(TAPS))),)

    mine, theirs = [], []

    def ready(gains_p, halo, pieces, pairs):
        mine.extend(block.reshape(own.shape) for block in halo[0])
        theirs.extend(block.reshape(own.shape) for block in halo[1])
        cfg = (rows, tall, len(mine), conv_rows, mix_rows, pairs)
        return pl.pallas_call(
            functools.partial(ready_kernel, cfg),
            out_shape=(
                near_out(wide_rows, 2 * branch),
                near_out(mix_whole, half),
                near_out(2, tall, half),
                near_out(2, tall, half),
            ),
            in_specs=[SMEM] + [VMEM] * (2 + 2 * len(mine) + len(pieces)),
            out_specs=(VMEM,) * 4,
            compiler_params=scoped(4),
            cost_estimate=cost(0, 2**16),
            name="ready",
        )(
            place,
            near(gains),
            near(gains_p),
            *[near(block) for block in (*mine, *theirs)],
            *[near(piece) for piece in pieces],
        )

    def newest(made, pieces, pairs):
        wide, mix, hm, hp = made
        n_in = 3 + len(pieces)
        z, wide, mix = pl.pallas_call(
            functools.partial(
                conv0_near_kernel, (rows, half, branch, slabs), (conv_rows, mix_rows, pairs)
            ),
            out_shape=(
                near_out(2, 2 * rows, branch),
                near_out(wide_rows, 2 * branch),
                near_out(mix_whole, half),
            ),
            in_specs=[SMEM] + [VMEM] * (n_in + 1),
            out_specs=(VMEM,) * 3,
            input_output_aliases={n_in: 1, n_in + 1: 2},
            scratch_shapes=[pltpu.VMEM((2, slabs[0][1], 2 * branch), F32)],
            compiler_params=scoped(12),
            cost_estimate=cost(0, 2**16),
            name="conv0_near",
        )(place, hm, hp, *[near(piece) for piece in pieces], wide, mix)
        return z, mix, wide, hm, hp

    if 2 * lag == rows:
        flat = own.reshape(2 * rows, half)
        gains_p, halo, made, beside, weights1, pairs1 = exchange(
            place, flat, chunks, gains, seq, ready, newest
        )
        last = halo[-1].reshape(own.shape)
    else:
        gains_p = swap_chan(gains)
        halo = [from_behind(own, seq, k * (lag // rows)) for k in range(1, 7)]
        newer = (own, *halo[:-1])
        newer = newer, tuple(swap_chan(block) for block in newer)
        made = newest(ready(gains_p, newer, weights[0], None), [], None)
        last, beside, weights1, pairs1 = halo[-1], (), weights[1], None
    za_mine, mix_mine, wide, hm, hp = made
    last_theirs, za_theirs, mix_theirs = lax.optimization_barrier(
        (swap_chan(last), swap_chan(za_mine), swap_chan(mix_mine))
    )

    z = pl.pallas_call(
        functools.partial(conv0_far_kernel, (rows, half, branch, far_slabs)),
        out_shape=(
            near_out(rows, branch),
            near_out(rows, branch),
            near_out(2, tall, half),
            near_out(2, tall, half),
        ),
        in_specs=[SMEM] + [VMEM] * 7,
        out_specs=(VMEM,) * 4,
        input_output_aliases={6: 2, 7: 3},
        scratch_shapes=[pltpu.VMEM((2, rows, 2 * branch), F32)],
        compiler_params=scoped(8),
        cost_estimate=cost(0, 2**16),
        name="conv0_far",
    )(place, near(gains), near(gains_p), near(last), near(last_theirs), wide, hm, hp)[:2]

    def mix0(z, z_theirs, blocks_used, name):
        n = len(blocks_used)
        states = [near_out(2, rows, half)] if blocks_used[0] == 0 else []
        return pl.pallas_call(
            functools.partial(mix0_kernel, (rows, half, branch, 1, n, len(z))),
            out_shape=(near_out(n, 2, rows, half), near_out(n, 2, rows, half), *states),
            in_specs=[SMEM] + [VMEM] * (4 + 2 * len(z) + 2 * n),
            out_specs=(VMEM,) * (2 + len(states)),
            compiler_params=scoped(12),
            cost_estimate=cost(0, 2**16),
            name=name,
        )(
            place,
            near(gains),
            near(gains_p),
            near(mix_mine),
            near(mix_theirs),
            *[near(t) for t in (*z, *z_theirs)],
            *[near(mine[b]) for b in blocks_used],
            *[near(theirs[b]) for b in blocks_used],
        )

    za_mine, *z = lax.optimization_barrier((za_mine, *z))
    hm1, hp1, state = mix0([za_mine], [za_theirs], used[:2], "mix0_near")
    hm, hp = mix0(z, [swap_chan(t) for t in z], used[2:], "mix0_far")
    hm, hp, hm1, hp1, *weights1 = lax.optimization_barrier((hm, hp, hm1, hp1, *weights1))
    z_mine, mix_last = pl.pallas_call(
        functools.partial(
            conv1_kernel, (rows, half, branch), (conv_rows, mix_rows, pairs1)
        ),
        out_shape=(near_out(2, rows, branch), near_out(mix_whole, half)),
        in_specs=[SMEM] + [VMEM] * (4 + len(weights1)),
        out_specs=(VMEM, VMEM),
        scratch_shapes=[
            pltpu.VMEM((wide_rows, 2 * branch), BF16),
            pltpu.VMEM((2 * rows, 2 * branch), F32),
        ],
        compiler_params=scoped(12),
        name="conv1",
    )(place, hm1, hp1, hm, hp, *[near(w) for w in weights1])
    z_theirs = swap_chan(z_mine)
    return pl.pallas_call(
        functools.partial(mix1_kernel, (branch,)),
        out_shape=(
            jax.ShapeDtypeStruct((rows, half), BF16),
            jax.ShapeDtypeStruct((rows, half), BF16),
        ),
        in_specs=[SMEM] + [VMEM] * 4,
        out_specs=(VMEM, VMEM),
        compiler_params=scoped(4),
        name="mix1",
    )(place, z_mine, near(z_theirs), mix_last, state)


def solution(mesh):
    return jax.shard_map(
        on_device,
        mesh=mesh,
        in_specs=(
            P(("groups", "seq"), "chan"),
            P(("groups", "seq"), "chan"),
            P(None, "chan"),
            P(None, "seq", None, "chan"),
            P(None, "seq", "chan"),
        ),
        out_specs=(P(("groups", "seq"), "chan"), P(("groups", "seq"), "chan")),
        check_vma=False,
    )
```

```python
import functools

import jax
import jax.numpy as jnp
from jax import lax
from jax.experimental import pallas as pl
from jax.experimental.pallas import tpu as pltpu
from jax.sharding import PartitionSpec as P

TAPS = 3
EPS = 1e-05
F32 = jnp.float32
BF16 = jnp.bfloat16
VMEM = pl.BlockSpec(memory_space=pltpu.VMEM)
SMEM = pl.BlockSpec(memory_space=pltpu.SMEM)
ANY = pl.BlockSpec(memory_space=pltpu.HBM)


def scoped(mebibytes):
    return pltpu.CompilerParams(vmem_limit_bytes=mebibytes * 2**20)


def near(block):
    return pltpu.with_memory_space_constraint(block, pltpu.VMEM)


def far(block):
    return pltpu.with_memory_space_constraint(block, pltpu.HBM)


def near_out(*shape):
    return pltpu.VMEM(shape, BF16)


def cost(flops, bytes_moved):
    return pl.CostEstimate(flops=flops, bytes_accessed=bytes_moved, transcendentals=0)


def swap_chan(block):
    return lax.ppermute(block, "chan", [(0, 1), (1, 0)])


def swap_groups(block):
    return lax.ppermute(block, "groups", [(0, 1), (1, 0)])


def swap_pair(block, seq):
    return lax.ppermute(block, "seq", [(s, s ^ 1) for s in range(seq)])


def ring(block, seq, by):
    return lax.ppermute(block, "seq", [(s, (s + by) % seq) for s in range(seq)])


def from_behind(block, seq, by):
    return lax.ppermute(block, "seq", [(s - by, s) for s in range(by, seq)])


def weight_moves(place, refs, conv_rows, mix_rows, pairs, wide, mix):
    if pairs is None:
        return [(refs[0], wide), (refs[1], mix)]
    s, g = place[0], place[1]
    seq, order = pairs
    moves = []
    for index, begin, skip, count, by, dx, dy in order:
        owner = lax.rem(s + (seq - by), seq)
        if dx:
            owner = owner + 1 - 2 * lax.rem(owner, 2)
        half = (1 - g) if dy else g
        unit = owner * 2 + half
        n_conv = min(conv_rows - skip, count)
        if wide is not None:
            to = pl.multiple_of(unit * conv_rows + skip, 16)
            moves.append((refs[index].at[pl.ds(begin, n_conv)], wide.at[pl.ds(to, n_conv)]))
        if count > n_conv and mix is not None:
            to = pl.multiple_of(unit * mix_rows, 16)
            moves.append(
                (refs[index].at[pl.ds(begin + n_conv, mix_rows)], mix.at[pl.ds(to, mix_rows)])
            )
    return moves


def normalise(xm, xp, dxm, dxp, gm, gp, width):
    total = jnp.sum(xm * xm, axis=1, keepdims=True) + jnp.sum(xp * xp, axis=1, keepdims=True)
    cross = jnp.sum(xm * dxm, axis=1, keepdims=True) + jnp.sum(xp * dxp, axis=1, keepdims=True)
    scale = lax.rsqrt(total / width + EPS)
    factor = scale * scale * scale * (cross / width)
    return (
        (gm * xm * scale).astype(BF16),
        (gp * xp * scale).astype(BF16),
        (gm * (dxm * scale - xm * factor)).astype(BF16),
        (gp * (dxp * scale - xp * factor)).astype(BF16),
    )


def gate_into(out, full, dfull, branch):
    tanh_f = jnp.tanh(full[:, :branch])
    sig_g = jax.nn.sigmoid(full[:, branch:])
    out[0][...] = (tanh_f * sig_g).astype(BF16)
    out[1][...] = (
        (1.0 - tanh_f * tanh_f) * sig_g * dfull[:, :branch]
        + tanh_f * sig_g * (1.0 - sig_g) * dfull[:, branch:]
    ).astype(BF16)


def norm_rows(gm, gp, mine, theirs, hm, hp, base):
    rows, half = mine.shape[1:]
    step = min(256, rows)

    def body(i, carry):
        at = pl.ds(pl.multiple_of(i * step, step), step)
        to = pl.ds(pl.multiple_of(base + i * step, step), step)
        xm = mine[0, at, :].astype(F32)
        dxm = mine[1, at, :].astype(F32)
        xp = theirs[0, at, :].astype(F32)
        dxp = theirs[1, at, :].astype(F32)
        hm[0, to, :], hp[0, to, :], hm[1, to, :], hp[1, to, :] = normalise(
            xm, xp, dxm, dxp, gm, gp, 2 * half
        )
        return carry

    lax.fori_loop(0, rows // step, body, 0)


def ready_kernel(cfg, place, gm_ref, gp_ref, *refs):
    rows, tall, n_blocks, conv_rows, mix_rows, pairs = cfg
    wide, mix, hm, hp = refs[-4:]
    convs = refs[2 * n_blocks : -4]
    for src, dst in weight_moves(place, convs, conv_rows, mix_rows, pairs, wide, mix):
        dst[...] = src[...]
    for b in range(n_blocks):
        norm_rows(
            gm_ref[0:1, :],
            gp_ref[0:1, :],
            refs[b],
            refs[n_blocks + b],
            hm,
            hp,
            tall - (b + 1) * rows,
        )


def conv_slabs(cfg, place, hm, hp, wide, z_refs, acc):
    rows, half, branch, slabs = cfg
    c = place[2]
    at_m = pl.multiple_of(c * half, half)
    at_p = pl.multiple_of((1 - c) * half, half)
    for begin, size, taps in slabs:
        for v in range(2):
            full = None
            for k, row in enumerate(taps):
                for h, at in ((hm, at_m), (hp, at_p)):
                    part = jnp.dot(
                        h[v, row : row + size, :],
                        wide[pl.ds(2 * half * k + at, half), :],
                        preferred_element_type=F32,
                    )
                    full = part if full is None else full + part
            acc[v, 0:size, :] = full
        for r in range(0, size, rows):
            gate_into(
                [z_ref.at[begin + r : begin + r + rows, :] for z_ref in z_refs],
                acc[0, r : r + rows, :],
                acc[1, r : r + rows, :],
                branch,
            )


def conv0_near_kernel(cfg, weight_cfg, place, hm, hp, *refs):
    z_ref, wide, mix, acc = refs[-4:]
    if weight_cfg[2] is not None:
        for src, dst in weight_moves(place, refs[:-6], *weight_cfg, wide, mix):
            dst[...] = src[...]
    conv_slabs(cfg, place, hm, hp, wide, (z_ref.at[0], z_ref.at[1]), acc)


def conv0_far_kernel(cfg, place, gm_ref, gp_ref, mine, theirs, wide, _, __, *refs):
    z_ref, dz_ref, hm, hp, acc = refs
    norm_rows(gm_ref[0:1, :], gp_ref[0:1, :], mine, theirs, hm, hp, 0)
    conv_slabs(cfg, place, hm, hp, wide, (z_ref, dz_ref), acc)


def mix0_kernel(cfg, place, gm_ref, gp_ref, mixm_ref, mixp_ref, *refs):
    rows, half, branch, layer, count, n_z = cfg
    if n_z == 1:
        zm_refs, zp_refs = ([ref.at[0], ref.at[1]] for ref in refs[:2])
    else:
        zm_refs, zp_refs = refs[:2], refs[2:4]
    refs = refs[2 * n_z :]
    mine, theirs = refs[:count], refs[count : 2 * count]
    hm_ref, hp_ref, *state_refs = refs[2 * count :]
    c = place[2]
    at_m = pl.ds(pl.multiple_of(c * branch, branch), branch)
    at_p = pl.ds(pl.multiple_of((1 - c) * branch, branch), branch)
    gm = gm_ref[layer : layer + 1, :]
    gp = gp_ref[layer : layer + 1, :]
    for j in range(count):
        at = slice((count - 1 - j) * rows, (count - j) * rows)
        new = []
        for v in range(2):
            zm = zm_refs[v][at, :]
            zp = zp_refs[v][at, :]
            for x_ref, mix in ((mine[j], mixm_ref), (theirs[j], mixp_ref)):
                y = jnp.dot(zm, mix[at_m, :], preferred_element_type=F32)
                y = y + jnp.dot(zp, mix[at_p, :], preferred_element_type=F32)
                new.append((x_ref[v].astype(F32) + y).astype(BF16))
        if j == 0 and state_refs:
            state_refs[0][0] = new[0]
            state_refs[0][1] = new[2]
        xm, xp, dxm, dxp = (t.astype(F32) for t in new)
        hm_ref[j, 0], hp_ref[j, 0], hm_ref[j, 1], hp_ref[j, 1] = normalise(
            xm, xp, dxm, dxp, gm, gp, 2 * half
        )


def conv1_kernel(cfg, weight_cfg, place, hm_near, hp_near, hm_far, hp_far, *refs):
    rows, half, branch = cfg
    z_ref, mix, wide, acc = refs[-4:]
    for src, dst in weight_moves(place, refs[:-4], *weight_cfg, wide, mix):
        dst[...] = src[...]
    c = place[2]
    at_m = pl.multiple_of(c * half, half)
    at_p = pl.multiple_of((1 - c) * half, half)
    full = None
    for k in range(TAPS):
        for near_ref, far_ref, at in ((hm_near, hm_far, at_m), (hp_near, hp_far, at_p)):
            part = jnp.dot(
                (near_ref[k] if k < 2 else far_ref[0]).reshape(2 * rows, half),
                wide[pl.ds(2 * half * k + at, half), :],
                preferred_element_type=F32,
            )
            full = part if full is None else full + part
    acc[...] = full
    gate_into((z_ref.at[0], z_ref.at[1]), acc[0:rows, :], acc[rows : 2 * rows, :], branch)


def mix1_kernel(cfg, place, zm_ref, zp_ref, mix_ref, state_ref, out_ref, dout_ref):
    (branch,) = cfg
    c = place[2]
    at_m = pl.ds(pl.multiple_of(c * branch, branch), branch)
    at_p = pl.ds(pl.multiple_of((1 - c) * branch, branch), branch)
    for v, out in ((0, out_ref), (1, dout_ref)):
        y = jnp.dot(zm_ref[v], mix_ref[at_m, :], preferred_element_type=F32)
        y = y + jnp.dot(zp_ref[v], mix_ref[at_p, :], preferred_element_type=F32)
        out[...] = (state_ref[v].astype(F32) + y).astype(BF16)


def chunk_kernel(conv, mix, both, *chunks):
    for layer, chunk in enumerate(chunks):
        chunk[0 : conv.shape[1], :] = conv[layer]
        chunk[conv.shape[1] :, :] = mix[layer]
        begin = layer * chunk.shape[0]
        both[begin : begin + chunk.shape[0], :] = chunk[...]


def pack(seq, place, *buffers):
    arrays = []

    def index(array):
        for i, known in enumerate(arrays):
            if known is array:
                return i
        arrays.append(array)
        return len(arrays) - 1

    plan = []
    for buffer in buffers:
        parts = []
        for array, begin, count, *mark in buffer:
            planes, even = (mark + [None, None])[:2] if mark else (None, None)
            parts.append(
                (index(array), begin, count, planes, None if even is None else index(even))
            )
        plan.append(parts)
    width = arrays[0].shape[-1]

    def kernel(place_ref, *refs):
        s = place_ref[0]
        for out, parts in zip(refs[len(arrays) :], plan):
            to = 0
            for i, begin, count, planes, even in parts:
                value = refs[i][begin : begin + count, :]
                if planes is not None:
                    value = jnp.where(s < max(2 * planes, 1), jnp.zeros_like(value), value)
                if even is not None:
                    value = jnp.where(lax.rem(s, 2) == 1, value, refs[even][...])
                out[to : to + count, :] = value
                to += count

    return pl.pallas_call(
        kernel,
        out_shape=tuple(near_out(sum(part[2] for part in buf), width) for buf in buffers),
        in_specs=[SMEM] + [VMEM] * len(arrays),
        out_specs=(VMEM,) * len(buffers),
        compiler_params=scoped(4),
        name="pack",
    )(place, *[near(array) for array in arrays])


def exchange(place, own, chunks, gains, seq, ready, newest):
    both, c0, c1 = chunks
    unit = both.shape[0] // 2
    tall = own.shape[0]
    pieces = ([], [])
    order = ([], [])

    def keep(layer, array, *slots):
        for begin, skip, count, k, dx, dy in slots:
            order[layer].append((len(pieces[layer]), begin, skip, count, 2 * k, dx, dy))
        pieces[layer].append(array)

    def whole(layer, array, *slots):
        keep(layer, array, *[(i * unit, 0, unit, *slot) for i, slot in enumerate(slots)])

    def together(*blocks):
        return lax.optimization_barrier(blocks)

    def x(block):
        return swap_pair(block, seq)

    def y(block):
        return swap_groups(block)

    def z(block, by=1):
        return ring(block, seq, 2 * by)

    whole(0, both, (0, 0, 0))
    keep(1, both, (unit, 0, unit, 0, 0, 0))
    z1a, z1b, x1, y1, own, c1 = together(z(c0), z(c0, 3), x(both), y(both), own, c1)
    whole(0, z1a, (1, 0, 0))
    whole(0, z1b, (3, 0, 0))
    whole(0, x1, (0, 1, 0))
    keep(1, x1, (unit, 0, unit, 0, 1, 0))
    whole(0, y1, (0, 0, 1))
    keep(1, y1, (unit, 0, unit, 0, 0, 1))
    to_z, to_x, to_y = pack(
        seq,
        place,
        [(z1a, 0, unit), (own, 0, tall)],
        [(z1a, 0, unit), (z1b, 0, unit), (y1, unit, unit)],
        [(z1a, 0, unit), (z1b, 0, unit), (x1, 0, unit)],
    )
    z2, x2, y2, own, c1, gains_p, own_p = together(
        z(to_z), x(to_x), y(to_y), own, c1, swap_chan(gains), swap_chan(own)
    )
    keep(0, z2, (0, 0, unit, 2, 0, 0))
    whole(0, x2, (1, 1, 0), (3, 1, 0))
    keep(1, x2, (2 * unit, 0, unit, 0, 1, 1))
    whole(0, y2, (1, 0, 1), (3, 0, 1), (0, 1, 1))
    to_z, to_x, to_y, two = pack(
        seq,
        place,
        [(both, unit, unit), (x2, 2 * unit, unit)],
        [(z2, 0, unit), (z2, unit, tall, 1, own)],
        [(z2, 0, unit), (x2, 0, 2 * unit)],
        [(z2, unit, tall, 1)],
    )
    z3a, z3b, x3, y3 = together(z(to_z), z(c1, 3), x(to_x), y(to_y))
    whole(1, z3a, (1, 0, 0), (1, 1, 1))
    whole(1, z3b, (3, 0, 0))
    keep(0, x3, (0, 0, unit, 2, 1, 0))
    whole(0, y3, (2, 0, 1), (1, 1, 1), (3, 1, 1))
    cut = unit // 2
    to_z, to_x, w_x, w_y, one = pack(
        seq,
        place,
        [(z3a, 0, unit), (x3, unit, tall, 0)],
        [(z3a, 0, unit), (z3b, 0, unit)],
        [(y3, 0, cut)],
        [(x3, cut, unit - cut)],
        [(x3, unit, tall, 0)],
    )
    x4a, y4a = x(w_x), y(w_y)
    halo = (own, one, two), (own_p, swap_chan(one), swap_chan(two))
    first = ready(gains_p, halo, pieces[0], (seq, tuple(order[0])))
    pieces[0].clear()
    order[0].clear()
    keep(0, x4a, (0, 0, cut, 2, 1, 1))
    keep(0, y4a, (0, cut, unit - cut, 2, 1, 1))
    made = newest(first, pieces[0], (seq, tuple(order[0])))
    to_x = together(to_x, x4a, y4a)[0]
    z4, x4, y4, made = together(z(to_z), x(to_x), y(to_x), made)
    keep(1, z4, (0, 0, unit, 2, 0, 0))
    whole(1, x4, (1, 1, 0), (3, 1, 0))
    whole(1, y4, (1, 0, 1), (3, 0, 1))
    to_z, to_x, to_y, three = pack(
        seq,
        place,
        [(z3a, unit, unit)],
        [(z4, 0, unit), (y4, unit, cut)],
        [(z4, 0, unit), (x4, unit + cut, unit - cut)],
        [(z4, unit, tall, 1)],
    )
    x5, y5, z5 = x(to_x), y(to_y), z(to_z)
    whole(1, z5, (2, 1, 1))
    keep(1, x5, (0, 0, unit, 2, 1, 0), (unit, 0, cut, 3, 1, 1))
    keep(1, y5, (0, 0, unit, 2, 0, 1), (unit, cut, unit - cut, 3, 1, 1))
    return gains_p, (one, two, three), made, (x5, y5, z5), pieces[1], (seq, tuple(order[1]))


def on_device(signal, tangent, gains, convolution_kernel, mixing_kernel):
    rows, half = signal.shape
    seq = lax.axis_size("seq")
    layers = gains.shape[0]
    branch = convolution_kernel.shape[3]
    shard = convolution_kernel.shape[1]
    mix_shard = mixing_kernel.shape[1]
    lag = rows * seq // 16
    place = jnp.stack([lax.axis_index("seq"), lax.axis_index("groups"), lax.axis_index("chan")])
    place = place.astype(jnp.int32)
    wide_rows, mix_whole = shard * seq, mix_shard * seq

    own = jnp.stack([signal, tangent], 0)
    if 2 * lag == rows:
        conv_rows, mix_rows = shard // 2, mix_shard // 2
        g = lax.axis_index("groups")
        conv_part = lax.dynamic_slice_in_dim(
            convolution_kernel, g * conv_rows, conv_rows, 1
        ).reshape(layers, conv_rows, 2 * branch)
        mix_part = lax.dynamic_slice_in_dim(mixing_kernel, g * mix_rows, mix_rows, 1)
        unit = conv_rows + mix_rows
        chunks = pl.pallas_call(
            chunk_kernel,
            out_shape=(
                near_out(layers * unit, 2 * branch),
                *[near_out(unit, 2 * branch) for _ in range(layers)],
            ),
            in_specs=[VMEM, VMEM],
            out_specs=(VMEM,) * (1 + layers),
            compiler_params=scoped(2),
            name="chunk",
        )(near(conv_part), near(mix_part))
        step, used = lag, (0, 1, 2)
        blocks = 4
    else:
        conv_rows, mix_rows = shard, mix_shard
        conv_local = convolution_kernel.reshape(layers, shard, 2 * branch)
        weights = [
            [
                lax.all_gather(conv_local[l], "seq", axis=0, tiled=True),
                lax.all_gather(mixing_kernel[l], "seq", axis=0, tiled=True),
            ]
            for l in range(layers)
        ]
        step, used = rows, (0, 2, 4)
        blocks = 7
    tall = blocks * rows
    starts = tuple(tall - rows - m * step for m in range(7))
    if 2 * lag == rows:
        slabs = ((0, 2 * rows, tuple(starts[2 + k] for k in range(TAPS))),)
    else:
        slabs = tuple(
            ((1 - j) * rows, rows, tuple(starts[2 * j + k] for k in range(TAPS))) for j in range(2)
        )
    far_slabs = ((0, rows, tuple(starts[4 + k] for k in range(TAPS))),)

    mine, theirs = [], []

    def ready(gains_p, halo, pieces, pairs):
        mine.extend(block.reshape(own.shape) for block in halo[0])
        theirs.extend(block.reshape(own.shape) for block in halo[1])
        cfg = (rows, tall, len(mine), conv_rows, mix_rows, pairs)
        return pl.pallas_call(
            functools.partial(ready_kernel, cfg),
            out_shape=(
                near_out(wide_rows, 2 * branch),
                near_out(mix_whole, half),
                near_out(2, tall, half),
                near_out(2, tall, half),
            ),
            in_specs=[SMEM] + [VMEM] * (2 + 2 * len(mine) + len(pieces)),
            out_specs=(VMEM,) * 4,
            compiler_params=scoped(10),
            cost_estimate=cost(0, 2**16),
            name="ready",
        )(
            place,
            near(gains),
            near(gains_p),
            *[near(block) for block in (*mine, *theirs)],
            *[near(piece) for piece in pieces],
        )

    def newest(made, pieces, pairs):
        wide, mix, hm, hp = made
        n_in = 3 + len(pieces)
        z, wide, mix = pl.pallas_call(
            functools.partial(
                conv0_near_kernel, (rows, half, branch, slabs), (conv_rows, mix_rows, pairs)
            ),
            out_shape=(
                near_out(2, 2 * rows, branch),
                near_out(wide_rows, 2 * branch),
                near_out(mix_whole, half),
            ),
            in_specs=[SMEM] + [VMEM] * (n_in + 1),
            out_specs=(VMEM,) * 3,
            input_output_aliases={n_in: 1, n_in + 1: 2},
            scratch_shapes=[pltpu.VMEM((2, slabs[0][1], 2 * branch), F32)],
            compiler_params=scoped(12),
            cost_estimate=cost(0, 2**16),
            name="conv0_near",
        )(place, hm, hp, *[near(piece) for piece in pieces], wide, mix)
        return z, mix, wide, hm, hp

    if 2 * lag == rows:
        flat = own.reshape(2 * rows, half)
        gains_p, halo, made, beside, weights1, pairs1 = exchange(
            place, flat, chunks, gains, seq, ready, newest
        )
        last = halo[-1].reshape(own.shape)
    else:
        gains_p = swap_chan(gains)
        halo = [from_behind(own, seq, k * (lag // rows)) for k in range(1, 7)]
        newer = (own, *halo[:-1])
        newer = newer, tuple(swap_chan(block) for block in newer)
        made = newest(ready(gains_p, newer, weights[0], None), [], None)
        last, beside, weights1, pairs1 = halo[-1], (), weights[1], None
    za_mine, mix_mine, wide, hm, hp = made
    last_theirs, za_theirs, mix_theirs = lax.optimization_barrier(
        (swap_chan(last), swap_chan(za_mine), swap_chan(mix_mine))
    )

    z = pl.pallas_call(
        functools.partial(conv0_far_kernel, (rows, half, branch, far_slabs)),
        out_shape=(
            near_out(rows, branch),
            near_out(rows, branch),
            near_out(2, tall, half),
            near_out(2, tall, half),
        ),
        in_specs=[SMEM] + [VMEM] * 7,
        out_specs=(VMEM,) * 4,
        input_output_aliases={6: 2, 7: 3},
        scratch_shapes=[pltpu.VMEM((2, rows, 2 * branch), F32)],
        compiler_params=scoped(12),
        cost_estimate=cost(0, 2**16),
        name="conv0_far",
    )(place, near(gains), near(gains_p), near(last), near(last_theirs), wide, hm, hp)[:2]

    def mix0(z, z_theirs, blocks_used, name):
        n = len(blocks_used)
        states = [near_out(2, rows, half)] if blocks_used[0] == 0 else []
        return pl.pallas_call(
            functools.partial(mix0_kernel, (rows, half, branch, 1, n, len(z))),
            out_shape=(near_out(n, 2, rows, half), near_out(n, 2, rows, half), *states),
            in_specs=[SMEM] + [VMEM] * (4 + 2 * len(z) + 2 * n),
            out_specs=(VMEM,) * (2 + len(states)),
            compiler_params=scoped(12),
            cost_estimate=cost(0, 2**16),
            name=name,
        )(
            place,
            near(gains),
            near(gains_p),
            near(mix_mine),
            near(mix_theirs),
            *[near(t) for t in (*z, *z_theirs)],
            *[near(mine[b]) for b in blocks_used],
            *[near(theirs[b]) for b in blocks_used],
        )

    za_mine, *z = lax.optimization_barrier((za_mine, *z))
    hm1, hp1, state = mix0([za_mine], [za_theirs], used[:2], "mix0_near")
    hm, hp = mix0(z, [swap_chan(t) for t in z], used[2:], "mix0_far")
    hm, hp, hm1, hp1, *weights1 = lax.optimization_barrier((hm, hp, hm1, hp1, *weights1))
    z_mine, mix_last = pl.pallas_call(
        functools.partial(
            conv1_kernel, (rows, half, branch), (conv_rows, mix_rows, pairs1)
        ),
        out_shape=(near_out(2, rows, branch), near_out(mix_whole, half)),
        in_specs=[SMEM] + [VMEM] * (4 + len(weights1)),
        out_specs=(VMEM, VMEM),
        scratch_shapes=[
            pltpu.VMEM((wide_rows, 2 * branch), BF16),
            pltpu.VMEM((2 * rows, 2 * branch), F32),
        ],
        compiler_params=scoped(12),
        name="conv1",
    )(place, hm1, hp1, hm, hp, *[near(w) for w in weights1])
    z_theirs = swap_chan(z_mine)
    return pl.pallas_call(
        functools.partial(mix1_kernel, (branch,)),
        out_shape=(
            jax.ShapeDtypeStruct((rows, half), BF16),
            jax.ShapeDtypeStruct((rows, half), BF16),
        ),
        in_specs=[SMEM] + [VMEM] * 4,
        out_specs=(VMEM, VMEM),
        compiler_params=scoped(4),
        name="mix1",
    )(place, z_mine, near(z_theirs), mix_last, state)


def solution(mesh):
    return jax.shard_map(
        on_device,
        mesh=mesh,
        in_specs=(
            P(("groups", "seq"), "chan"),
            P(("groups", "seq"), "chan"),
            P(None, "chan"),
            P(None, "seq", None, "chan"),
            P(None, "seq", "chan"),
        ),
        out_specs=(P(("groups", "seq"), "chan"), P(("groups", "seq"), "chan")),
        check_vma=False,
    )
```

```python
import functools

import jax
import jax.numpy as jnp
from jax import lax
from jax.experimental import pallas as pl
from jax.experimental.pallas import tpu as pltpu
from jax.sharding import PartitionSpec as P

TAPS = 3
EPS = 1e-05
F32 = jnp.float32
BF16 = jnp.bfloat16
VMEM = pl.BlockSpec(memory_space=pltpu.VMEM)
SMEM = pl.BlockSpec(memory_space=pltpu.SMEM)
ANY = pl.BlockSpec(memory_space=pltpu.HBM)


def scoped(mebibytes):
    return pltpu.CompilerParams(vmem_limit_bytes=mebibytes * 2**20)


def near(block):
    return pltpu.with_memory_space_constraint(block, pltpu.VMEM)


def far(block):
    return pltpu.with_memory_space_constraint(block, pltpu.HBM)


def near_out(*shape):
    return pltpu.VMEM(shape, BF16)


def cost(flops, bytes_moved):
    return pl.CostEstimate(flops=flops, bytes_accessed=bytes_moved, transcendentals=0)


def swap_chan(block):
    return lax.ppermute(block, "chan", [(0, 1), (1, 0)])


def swap_groups(block):
    return lax.ppermute(block, "groups", [(0, 1), (1, 0)])


def swap_pair(block, seq):
    return lax.ppermute(block, "seq", [(s, s ^ 1) for s in range(seq)])


def ring(block, seq, by):
    return lax.ppermute(block, "seq", [(s, (s + by) % seq) for s in range(seq)])


def from_behind(block, seq, by):
    return lax.ppermute(block, "seq", [(s - by, s) for s in range(by, seq)])


def weight_moves(place, refs, conv_rows, mix_rows, pairs, wide, mix):
    if pairs is None:
        return [(refs[0], wide), (refs[1], mix)]
    s, g = place[0], place[1]
    seq, order = pairs
    moves = []
    for index, begin, skip, count, by, dx, dy in order:
        owner = lax.rem(s + (seq - by), seq)
        if dx:
            owner = owner + 1 - 2 * lax.rem(owner, 2)
        half = (1 - g) if dy else g
        unit = owner * 2 + half
        n_conv = min(conv_rows - skip, count)
        if wide is not None:
            to = pl.multiple_of(unit * conv_rows + skip, 16)
            moves.append((refs[index].at[pl.ds(begin, n_conv)], wide.at[pl.ds(to, n_conv)]))
        if count > n_conv and mix is not None:
            to = pl.multiple_of(unit * mix_rows, 16)
            moves.append(
                (refs[index].at[pl.ds(begin + n_conv, mix_rows)], mix.at[pl.ds(to, mix_rows)])
            )
    return moves


def normalise(xm, xp, dxm, dxp, gm, gp, width):
    total = jnp.sum(xm * xm, axis=1, keepdims=True) + jnp.sum(xp * xp, axis=1, keepdims=True)
    cross = jnp.sum(xm * dxm, axis=1, keepdims=True) + jnp.sum(xp * dxp, axis=1, keepdims=True)
    scale = lax.rsqrt(total / width + EPS)
    factor = scale * scale * scale * (cross / width)
    return (
        (gm * xm * scale).astype(BF16),
        (gp * xp * scale).astype(BF16),
        (gm * (dxm * scale - xm * factor)).astype(BF16),
        (gp * (dxp * scale - xp * factor)).astype(BF16),
    )


def gate_into(out, full, dfull, branch):
    tanh_f = jnp.tanh(full[:, :branch])
    sig_g = jax.nn.sigmoid(full[:, branch:])
    out[0][...] = (tanh_f * sig_g).astype(BF16)
    out[1][...] = (
        (1.0 - tanh_f * tanh_f) * sig_g * dfull[:, :branch]
        + tanh_f * sig_g * (1.0 - sig_g) * dfull[:, branch:]
    ).astype(BF16)


def norm_rows(gm, gp, mine, theirs, hm, hp, base):
    rows, half = mine.shape[1:]
    step = 64

    def body(i, carry):
        at = pl.ds(pl.multiple_of(i * step, step), step)
        to = pl.ds(pl.multiple_of(base + i * step, step), step)
        xm = mine[0, at, :].astype(F32)
        dxm = mine[1, at, :].astype(F32)
        xp = theirs[0, at, :].astype(F32)
        dxp = theirs[1, at, :].astype(F32)
        hm[0, to, :], hp[0, to, :], hm[1, to, :], hp[1, to, :] = normalise(
            xm, xp, dxm, dxp, gm, gp, 2 * half
        )
        return carry

    lax.fori_loop(0, rows // step, body, 0)


def ready_kernel(cfg, place, gm_ref, gp_ref, *refs):
    rows, tall, n_blocks, conv_rows, mix_rows, pairs = cfg
    wide, mix, hm, hp = refs[-4:]
    convs = refs[2 * n_blocks : -4]
    for src, dst in weight_moves(place, convs, conv_rows, mix_rows, pairs, wide, mix):
        dst[...] = src[...]
    for b in range(n_blocks):
        norm_rows(
            gm_ref[0:1, :],
            gp_ref[0:1, :],
            refs[b],
            refs[n_blocks + b],
            hm,
            hp,
            tall - (b + 1) * rows,
        )


def conv_slabs(cfg, place, hm, hp, wide, z_refs, acc):
    rows, half, branch, slabs = cfg
    c = place[2]
    at_m = pl.multiple_of(c * half, half)
    at_p = pl.multiple_of((1 - c) * half, half)
    for begin, size, taps in slabs:
        for v in range(2):
            full = None
            for k, row in enumerate(taps):
                for h, at in ((hm, at_m), (hp, at_p)):
                    part = jnp.dot(
                        h[v, row : row + size, :],
                        wide[pl.ds(2 * half * k + at, half), :],
                        preferred_element_type=F32,
                    )
                    full = part if full is None else full + part
            acc[v, 0:size, :] = full
        for r in range(0, size, rows):
            gate_into(
                [z_ref.at[begin + r : begin + r + rows, :] for z_ref in z_refs],
                acc[0, r : r + rows, :],
                acc[1, r : r + rows, :],
                branch,
            )


def conv0_near_kernel(cfg, weight_cfg, place, hm, hp, *refs):
    z_ref, wide, mix, acc = refs[-4:]
    if weight_cfg[2] is not None:
        for src, dst in weight_moves(place, refs[:-6], *weight_cfg, wide, mix):
            dst[...] = src[...]
    conv_slabs(cfg, place, hm, hp, wide, (z_ref.at[0], z_ref.at[1]), acc)


def conv0_far_kernel(cfg, place, gm_ref, gp_ref, mine, theirs, wide, _, __, *refs):
    z_ref, dz_ref, hm, hp, acc = refs
    norm_rows(gm_ref[0:1, :], gp_ref[0:1, :], mine, theirs, hm, hp, 0)
    conv_slabs(cfg, place, hm, hp, wide, (z_ref, dz_ref), acc)


def mix0_kernel(cfg, place, gm_ref, gp_ref, mixm_ref, mixp_ref, *refs):
    rows, half, branch, layer, count, n_z = cfg
    if n_z == 1:
        zm_refs, zp_refs = ([ref.at[0], ref.at[1]] for ref in refs[:2])
    else:
        zm_refs, zp_refs = refs[:2], refs[2:4]
    refs = refs[2 * n_z :]
    mine, theirs = refs[:count], refs[count : 2 * count]
    hm_ref, hp_ref, *state_refs = refs[2 * count :]
    c = place[2]
    at_m = pl.ds(pl.multiple_of(c * branch, branch), branch)
    at_p = pl.ds(pl.multiple_of((1 - c) * branch, branch), branch)
    gm = gm_ref[layer : layer + 1, :]
    gp = gp_ref[layer : layer + 1, :]
    for j in range(count):
        at = slice((count - 1 - j) * rows, (count - j) * rows)
        new = []
        for v in range(2):
            zm = zm_refs[v][at, :]
            zp = zp_refs[v][at, :]
            for x_ref, mix in ((mine[j], mixm_ref), (theirs[j], mixp_ref)):
                y = jnp.dot(zm, mix[at_m, :], preferred_element_type=F32)
                y = y + jnp.dot(zp, mix[at_p, :], preferred_element_type=F32)
                new.append((x_ref[v].astype(F32) + y).astype(BF16))
        if j == 0 and state_refs:
            state_refs[0][0] = new[0]
            state_refs[0][1] = new[2]
        xm, xp, dxm, dxp = (t.astype(F32) for t in new)
        hm_ref[j, 0], hp_ref[j, 0], hm_ref[j, 1], hp_ref[j, 1] = normalise(
            xm, xp, dxm, dxp, gm, gp, 2 * half
        )


def conv1_kernel(cfg, weight_cfg, place, hm_near, hp_near, hm_far, hp_far, *refs):
    rows, half, branch = cfg
    z_ref, mix, wide, acc = refs[-4:]
    for src, dst in weight_moves(place, refs[:-4], *weight_cfg, wide, mix):
        dst[...] = src[...]
    c = place[2]
    at_m = pl.multiple_of(c * half, half)
    at_p = pl.multiple_of((1 - c) * half, half)
    full = None
    for k in range(TAPS):
        for near_ref, far_ref, at in ((hm_near, hm_far, at_m), (hp_near, hp_far, at_p)):
            part = jnp.dot(
                (near_ref[k] if k < 2 else far_ref[0]).reshape(2 * rows, half),
                wide[pl.ds(2 * half * k + at, half), :],
                preferred_element_type=F32,
            )
            full = part if full is None else full + part
    acc[...] = full
    gate_into((z_ref.at[0], z_ref.at[1]), acc[0:rows, :], acc[rows : 2 * rows, :], branch)


def mix1_kernel(cfg, place, zm_ref, zp_ref, mix_ref, state_ref, out_ref, dout_ref):
    (branch,) = cfg
    c = place[2]
    at_m = pl.ds(pl.multiple_of(c * branch, branch), branch)
    at_p = pl.ds(pl.multiple_of((1 - c) * branch, branch), branch)
    for v, out in ((0, out_ref), (1, dout_ref)):
        y = jnp.dot(zm_ref[v], mix_ref[at_m, :], preferred_element_type=F32)
        y = y + jnp.dot(zp_ref[v], mix_ref[at_p, :], preferred_element_type=F32)
        out[...] = (state_ref[v].astype(F32) + y).astype(BF16)


def chunk_kernel(conv, mix, both, *chunks):
    for layer, chunk in enumerate(chunks):
        chunk[0 : conv.shape[1], :] = conv[layer]
        chunk[conv.shape[1] :, :] = mix[layer]
        begin = layer * chunk.shape[0]
        both[begin : begin + chunk.shape[0], :] = chunk[...]


def pack(seq, place, *buffers):
    arrays = []

    def index(array):
        for i, known in enumerate(arrays):
            if known is array:
                return i
        arrays.append(array)
        return len(arrays) - 1

    plan = []
    for buffer in buffers:
        parts = []
        for array, begin, count, *mark in buffer:
            planes, even = (mark + [None, None])[:2] if mark else (None, None)
            parts.append(
                (index(array), begin, count, planes, None if even is None else index(even))
            )
        plan.append(parts)
    width = arrays[0].shape[-1]

    def kernel(place_ref, *refs):
        s = place_ref[0]
        for out, parts in zip(refs[len(arrays) :], plan):
            to = 0
            for i, begin, count, planes, even in parts:
                value = refs[i][begin : begin + count, :]
                if planes is not None:
                    value = jnp.where(s < max(2 * planes, 1), jnp.zeros_like(value), value)
                if even is not None:
                    value = jnp.where(lax.rem(s, 2) == 1, value, refs[even][...])
                out[to : to + count, :] = value
                to += count

    return pl.pallas_call(
        kernel,
        out_shape=tuple(near_out(sum(part[2] for part in buf), width) for buf in buffers),
        in_specs=[SMEM] + [VMEM] * len(arrays),
        out_specs=(VMEM,) * len(buffers),
        compiler_params=scoped(4),
        name="pack",
    )(place, *[near(array) for array in arrays])


def exchange(place, own, chunks, gains, seq, ready, newest):
    both, c0, c1 = chunks
    unit = both.shape[0] // 2
    tall = own.shape[0]
    pieces = ([], [])
    order = ([], [])

    def keep(layer, array, *slots):
        for begin, skip, count, k, dx, dy in slots:
            order[layer].append((len(pieces[layer]), begin, skip, count, 2 * k, dx, dy))
        pieces[layer].append(array)

    def whole(layer, array, *slots):
        keep(layer, array, *[(i * unit, 0, unit, *slot) for i, slot in enumerate(slots)])

    def together(*blocks):
        return lax.optimization_barrier(blocks)

    def x(block):
        return swap_pair(block, seq)

    def y(block):
        return swap_groups(block)

    def z(block, by=1):
        return ring(block, seq, 2 * by)

    whole(0, both, (0, 0, 0))
    keep(1, both, (unit, 0, unit, 0, 0, 0))
    z1a, z1b, x1, y1, own, c1, gains_p = together(
        z(c0), z(c0, 3), x(both), y(both), own, c1, swap_chan(gains)
    )
    whole(0, z1a, (1, 0, 0))
    whole(0, z1b, (3, 0, 0))
    whole(0, x1, (0, 1, 0))
    keep(1, x1, (unit, 0, unit, 0, 1, 0))
    whole(0, y1, (0, 0, 1))
    keep(1, y1, (unit, 0, unit, 0, 0, 1))
    to_z, to_x, to_y = pack(
        seq,
        place,
        [(z1a, 0, unit), (own, 0, tall)],
        [(z1a, 0, unit), (z1b, 0, unit), (y1, unit, unit)],
        [(z1a, 0, unit), (z1b, 0, unit), (x1, 0, unit)],
    )
    z2, x2, y2, own, c1, own_p = together(z(to_z), x(to_x), y(to_y), own, c1, swap_chan(own))
    keep(0, z2, (0, 0, unit, 2, 0, 0))
    whole(0, x2, (1, 1, 0), (3, 1, 0))
    keep(1, x2, (2 * unit, 0, unit, 0, 1, 1))
    whole(0, y2, (1, 0, 1), (3, 0, 1), (0, 1, 1))
    to_z, to_x, to_y, two = pack(
        seq,
        place,
        [(both, unit, unit), (x2, 2 * unit, unit)],
        [(z2, 0, unit), (z2, unit, tall, 1, own)],
        [(z2, 0, unit), (x2, 0, 2 * unit)],
        [(z2, unit, tall, 1)],
    )
    z3a, z3b, x3, y3 = together(z(to_z), z(c1, 3), x(to_x), y(to_y))
    whole(1, z3a, (1, 0, 0), (1, 1, 1))
    whole(1, z3b, (3, 0, 0))
    keep(0, x3, (0, 0, unit, 2, 1, 0))
    whole(0, y3, (2, 0, 1), (1, 1, 1), (3, 1, 1))
    cut = unit // 2
    to_z, to_x, w_x, w_y, one = pack(
        seq,
        place,
        [(z3a, 0, unit), (x3, unit, tall, 0)],
        [(z3a, 0, unit), (z3b, 0, unit)],
        [(y3, 0, cut)],
        [(x3, cut, unit - cut)],
        [(x3, unit, tall, 0)],
    )
    x4a, y4a = x(w_x), y(w_y)
    halo = (own, one, two), (own_p, swap_chan(one), swap_chan(two))
    first = ready(gains_p, halo, pieces[0], (seq, tuple(order[0])))
    pieces[0].clear()
    order[0].clear()
    keep(0, x4a, (0, 0, cut, 2, 1, 1))
    keep(0, y4a, (0, cut, unit - cut, 2, 1, 1))
    made = newest(first, pieces[0], (seq, tuple(order[0])))
    to_x = together(to_x, x4a, y4a)[0]
    z4, x4, y4, made = together(z(to_z), x(to_x), y(to_x), made)
    keep(1, z4, (0, 0, unit, 2, 0, 0))
    whole(1, x4, (1, 1, 0), (3, 1, 0))
    whole(1, y4, (1, 0, 1), (3, 0, 1))
    to_z, to_x, to_y, three = pack(
        seq,
        place,
        [(z3a, unit, unit)],
        [(z4, 0, unit), (y4, unit, cut)],
        [(z4, 0, unit), (x4, unit + cut, unit - cut)],
        [(z4, unit, tall, 1)],
    )
    x5, y5, z5 = x(to_x), y(to_y), z(to_z)
    whole(1, z5, (2, 1, 1))
    keep(1, x5, (0, 0, unit, 2, 1, 0), (unit, 0, cut, 3, 1, 1))
    keep(1, y5, (0, 0, unit, 2, 0, 1), (unit, cut, unit - cut, 3, 1, 1))
    return gains_p, (one, two, three), made, (x5, y5, z5), pieces[1], (seq, tuple(order[1]))


def on_device(signal, tangent, gains, convolution_kernel, mixing_kernel):
    rows, half = signal.shape
    seq = lax.axis_size("seq")
    layers = gains.shape[0]
    branch = convolution_kernel.shape[3]
    shard = convolution_kernel.shape[1]
    mix_shard = mixing_kernel.shape[1]
    lag = rows * seq // 16
    place = jnp.stack([lax.axis_index("seq"), lax.axis_index("groups"), lax.axis_index("chan")])
    place = place.astype(jnp.int32)
    wide_rows, mix_whole = shard * seq, mix_shard * seq

    own = jnp.stack([signal, tangent], 0)
    if 2 * lag == rows:
        conv_rows, mix_rows = shard // 2, mix_shard // 2
        g = lax.axis_index("groups")
        conv_part = lax.dynamic_slice_in_dim(
            convolution_kernel, g * conv_rows, conv_rows, 1
        ).reshape(layers, conv_rows, 2 * branch)
        mix_part = lax.dynamic_slice_in_dim(mixing_kernel, g * mix_rows, mix_rows, 1)
        unit = conv_rows + mix_rows
        chunks = pl.pallas_call(
            chunk_kernel,
            out_shape=(
                near_out(layers * unit, 2 * branch),
                *[near_out(unit, 2 * branch) for _ in range(layers)],
            ),
            in_specs=[VMEM, VMEM],
            out_specs=(VMEM,) * (1 + layers),
            compiler_params=scoped(2),
            name="chunk",
        )(near(conv_part), near(mix_part))
        step, used = lag, (0, 1, 2)
        blocks = 4
    else:
        conv_rows, mix_rows = shard, mix_shard
        conv_local = convolution_kernel.reshape(layers, shard, 2 * branch)
        weights = [
            [
                lax.all_gather(conv_local[l], "seq", axis=0, tiled=True),
                lax.all_gather(mixing_kernel[l], "seq", axis=0, tiled=True),
            ]
            for l in range(layers)
        ]
        step, used = rows, (0, 2, 4)
        blocks = 7
    tall = blocks * rows
    starts = tuple(tall - rows - m * step for m in range(7))
    if 2 * lag == rows:
        slabs = ((0, 2 * rows, tuple(starts[2 + k] for k in range(TAPS))),)
    else:
        slabs = tuple(
            ((1 - j) * rows, rows, tuple(starts[2 * j + k] for k in range(TAPS))) for j in range(2)
        )
    far_slabs = ((0, rows, tuple(starts[4 + k] for k in range(TAPS))),)

    mine, theirs = [], []

    def ready(gains_p, halo, pieces, pairs):
        mine.extend(block.reshape(own.shape) for block in halo[0])
        theirs.extend(block.reshape(own.shape) for block in halo[1])
        cfg = (rows, tall, len(mine), conv_rows, mix_rows, pairs)
        return pl.pallas_call(
            functools.partial(ready_kernel, cfg),
            out_shape=(
                near_out(wide_rows, 2 * branch),
                near_out(mix_whole, half),
                near_out(2, tall, half),
                near_out(2, tall, half),
            ),
            in_specs=[SMEM] + [VMEM] * (2 + 2 * len(mine) + len(pieces)),
            out_specs=(VMEM,) * 4,
            compiler_params=scoped(4),
            cost_estimate=cost(0, 2**16),
            name="ready",
        )(
            place,
            near(gains),
            near(gains_p),
            *[near(block) for block in (*mine, *theirs)],
            *[near(piece) for piece in pieces],
        )

    def newest(made, pieces, pairs):
        wide, mix, hm, hp = made
        n_in = 3 + len(pieces)
        z, wide, mix = pl.pallas_call(
            functools.partial(
                conv0_near_kernel, (rows, half, branch, slabs), (conv_rows, mix_rows, pairs)
            ),
            out_shape=(
                near_out(2, 2 * rows, branch),
                near_out(wide_rows, 2 * branch),
                near_out(mix_whole, half),
            ),
            in_specs=[SMEM] + [VMEM] * (n_in + 1),
            out_specs=(VMEM,) * 3,
            input_output_aliases={n_in: 1, n_in + 1: 2},
            scratch_shapes=[pltpu.VMEM((2, slabs[0][1], 2 * branch), F32)],
            compiler_params=scoped(12),
            cost_estimate=cost(0, 2**16),
            name="conv0_near",
        )(place, hm, hp, *[near(piece) for piece in pieces], wide, mix)
        return z, mix, wide, hm, hp

    if 2 * lag == rows:
        flat = own.reshape(2 * rows, half)
        gains_p, halo, made, beside, weights1, pairs1 = exchange(
            place, flat, chunks, gains, seq, ready, newest
        )
        last = halo[-1].reshape(own.shape)
    else:
        gains_p = swap_chan(gains)
        halo = [from_behind(own, seq, k * (lag // rows)) for k in range(1, 7)]
        newer = (own, *halo[:-1])
        newer = newer, tuple(swap_chan(block) for block in newer)
        made = newest(ready(gains_p, newer, weights[0], None), [], None)
        last, beside, weights1, pairs1 = halo[-1], (), weights[1], None
    za_mine, mix_mine, wide, hm, hp = made
    last_theirs, za_theirs, mix_theirs = lax.optimization_barrier(
        (swap_chan(last), swap_chan(za_mine), swap_chan(mix_mine))
    )

    z = pl.pallas_call(
        functools.partial(conv0_far_kernel, (rows, half, branch, far_slabs)),
        out_shape=(
            near_out(rows, branch),
            near_out(rows, branch),
            near_out(2, tall, half),
            near_out(2, tall, half),
        ),
        in_specs=[SMEM] + [VMEM] * 7,
        out_specs=(VMEM,) * 4,
        input_output_aliases={6: 2, 7: 3},
        scratch_shapes=[pltpu.VMEM((2, rows, 2 * branch), F32)],
        compiler_params=scoped(8),
        cost_estimate=cost(0, 2**16),
        name="conv0_far",
    )(place, near(gains), near(gains_p), near(last), near(last_theirs), wide, hm, hp)[:2]

    def mix0(z, z_theirs, blocks_used, name):
        n = len(blocks_used)
        states = [near_out(2, rows, half)] if blocks_used[0] == 0 else []
        return pl.pallas_call(
            functools.partial(mix0_kernel, (rows, half, branch, 1, n, len(z))),
            out_shape=(near_out(n, 2, rows, half), near_out(n, 2, rows, half), *states),
            in_specs=[SMEM] + [VMEM] * (4 + 2 * len(z) + 2 * n),
            out_specs=(VMEM,) * (2 + len(states)),
            compiler_params=scoped(12),
            cost_estimate=cost(0, 2**16),
            name=name,
        )(
            place,
            near(gains),
            near(gains_p),
            near(mix_mine),
            near(mix_theirs),
            *[near(t) for t in (*z, *z_theirs)],
            *[near(mine[b]) for b in blocks_used],
            *[near(theirs[b]) for b in blocks_used],
        )

    za_mine, *z = lax.optimization_barrier((za_mine, *z))
    hm1, hp1, state = mix0([za_mine], [za_theirs], used[:2], "mix0_near")
    hm, hp = mix0(z, [swap_chan(t) for t in z], used[2:], "mix0_far")
    hm, hp, hm1, hp1, *weights1 = lax.optimization_barrier((hm, hp, hm1, hp1, *weights1))
    z_mine, mix_last = pl.pallas_call(
        functools.partial(
            conv1_kernel, (rows, half, branch), (conv_rows, mix_rows, pairs1)
        ),
        out_shape=(near_out(2, rows, branch), near_out(mix_whole, half)),
        in_specs=[SMEM] + [VMEM] * (4 + len(weights1)),
        out_specs=(VMEM, VMEM),
        scratch_shapes=[
            pltpu.VMEM((wide_rows, 2 * branch), BF16),
            pltpu.VMEM((2 * rows, 2 * branch), F32),
        ],
        compiler_params=scoped(12),
        name="conv1",
    )(place, hm1, hp1, hm, hp, *[near(w) for w in weights1])
    z_theirs = swap_chan(z_mine)
    return pl.pallas_call(
        functools.partial(mix1_kernel, (branch,)),
        out_shape=(
            jax.ShapeDtypeStruct((rows, half), BF16),
            jax.ShapeDtypeStruct((rows, half), BF16),
        ),
        in_specs=[SMEM] + [VMEM] * 4,
        out_specs=(VMEM, VMEM),
        compiler_params=scoped(4),
        name="mix1",
    )(place, z_mine, near(z_theirs), mix_last, state)


def solution(mesh):
    return jax.shard_map(
        on_device,
        mesh=mesh,
        in_specs=(
            P(("groups", "seq"), "chan"),
            P(("groups", "seq"), "chan"),
            P(None, "chan"),
            P(None, "seq", None, "chan"),
            P(None, "seq", "chan"),
        ),
        out_specs=(P(("groups", "seq"), "chan"), P(("groups", "seq"), "chan")),
        check_vma=False,
    )
```
